32 devices in a mesh: view: 8 (over z, y), mp: 4 (over x, core).
Axes of the slice: x: 2, y: 2, z: 4, core: 2. Of those that a mesh axis runs over, the one named last changes fastest.
Arguments:
- tokens: bfloat16 [32, 384, 1024], P('view', None, 'mp'), may hold values from -6 to 6
- pairs: int32 [64, 2], P('view'), may hold values from 0 to 31, as said below
- w_embed: bfloat16 [1024, 768], replicated, may hold values from -0.1875 to 0.1875
- w_query: bfloat16 [2, 768, 768], replicated, may hold values from -8 to 8
- w_keyval: bfloat16 [2, 768, 1536], replicated, may hold values from -0.21875 to 0.21875
- w_out: bfloat16 [2, 768, 768], replicated, may hold values from -0.21875 to 0.21875
- w_head: bfloat16 [2, 4, 768], replicated, may hold values from -0.21875 to 0.21875
- gains: float32 [2, 3, 768], replicated, may hold values from 0.1 to 1.9
Outputs:
- view_sums: float32 [32, 4, 384], P('view')
The draws below stay inside these ranges and needn't reach their ends.
Inputs may be any that keep to these rules, and one draw needn't show every extreme that they name: Owner of a view: view // 4. Among the 16 sides of the pairs of one index of view, at most 2 name views of one owner, and in every such block some owner is named exactly 2 times. The two views of a pair differ.
All inputs are finite; a program needn't handle non-finite values.
Results may differ from the reference program's by a relative error of at most 0.012.
Values may be sent and summed in bfloat16 or wider, within the bound.
No kernel may reach another device: no remote copies, remote signals or barrier semaphores. Data moves between devices by JAX's collectives and lax.ppermute only.
A program may use at most 128 MiB of HBM per device.

```python
import jax
import jax.numpy as jnp
from jax import lax

E = 1024
D = 768
HEADS = 12
TOKV = 384
VIEW_DEV = 4
PAIR_DEV = 2
CAP = 2
VIEWS = 32
PAIRS = 64
N_VIEW = 8
N_MP = 4


def draw_pairs(key, part):
    block_pairs = PAIR_DEV * N_MP
    block_sides = 2 * block_pairs
    listed = N_VIEW * CAP

    def one_block(block_key):
        keys = jax.random.split(block_key, 6)
        owner_of = jnp.arange(listed, dtype=jnp.int32) // CAP
        chosen = jax.random.randint(keys[0], (), 0, N_VIEW)
        ranks = jax.random.permutation(keys[1], listed).astype(jnp.int32)
        scores = jnp.where(owner_of == chosen, -1 - jnp.arange(listed, dtype=jnp.int32), ranks)
        order = jnp.argsort(scores, stable=True)
        picked = jnp.take(owner_of, order)[:block_sides]
        picked = jax.random.permutation(keys[2], picked)
        owners = picked.reshape(block_pairs, 2)
        first = jax.random.randint(keys[3], (block_pairs,), 0, VIEW_DEV)
        offset = jax.random.randint(keys[4], (block_pairs,), 1, VIEW_DEV)
        loose = jax.random.randint(keys[5], (block_pairs,), 0, VIEW_DEV)
        second = jnp.where(owners[:, 0] == owners[:, 1], (first + offset) % VIEW_DEV, loose)
        return jnp.stack([owners[:, 0] * VIEW_DEV + first, owners[:, 1] * VIEW_DEV + second], axis=1)
    blocks = jax.vmap(one_block)(jax.random.split(key, N_VIEW))
    return blocks.reshape(PAIRS, 2).astype(jnp.int32)


def draw_w_query(key, part):
    base = jax.random.normal(key, (2, D, D), jnp.float32) * D ** (-0.5)
    return jnp.clip(base, -8.0, 8.0).astype(jnp.bfloat16)


def block_levels(key, extent, pieces, least, top_value):
    gain, own = 1.0, jax.random.fold_in(key, 6)
    for dim, parts in pieces:
        steps = jnp.exp(jax.random.uniform(jax.random.fold_in(own, dim), (parts,), jnp.float32, least / len(pieces), top_value / len(pieces)))
        gain = gain * jnp.repeat(steps, extent[dim] // parts).reshape([-1 if axis == dim else 1 for axis in range(len(extent))])
    return gain


def gaussian(stream_key, shape, scale, limit, pieces=(), held_as=jnp.bfloat16):
    result = scale * jax.random.normal(stream_key, shape, jnp.float32)
    if pieces:
        result = result * block_levels(stream_key, shape, pieces, -0.22, 0.18)
    return jnp.clip(result, -limit, limit).astype(held_as)


def setup_inputs(seed: int = 0) -> dict:
    streams_of = jax.random.split(jax.random.key(seed), 9)
    return {
        "tokens": gaussian(streams_of[0], (VIEWS, TOKV, E), 1.0, 6.0, ((0, 8), (2, 4))),
        "pairs": draw_pairs(jax.random.fold_in(streams_of[8], 71), 0),
        "w_embed": gaussian(streams_of[2], (E, D), E ** -0.5, 0.1875),
        "w_query": draw_w_query(jax.random.fold_in(streams_of[8], 71), 0),
        "w_keyval": gaussian(streams_of[4], (2, D, 2 * D), D ** -0.5, 0.21875),
        "w_out": gaussian(streams_of[5], (2, D, D), D ** -0.5, 0.21875),
        "w_head": gaussian(streams_of[6], (2, 4, D), D ** -0.5, 0.21875),
        "gains": jnp.clip(1.0 + 0.18 * jax.random.normal(streams_of[7], (2, 3, D), jnp.float32), 0.1, 1.9),
    }


def layer_norm(values):
    mean = lax.optimization_barrier(jnp.mean(values, axis=-1, keepdims=True))
    centred = values - mean
    var = lax.optimization_barrier(jnp.mean(centred * centred, axis=-1, keepdims=True))
    return centred * lax.rsqrt(var + 1e-06)

def decode_pair(emb, w_query, w_keyval, w_out, w_head, gains):
    width = emb.shape[-1]
    head_size = width // HEADS
    records = []
    for side in range(2):
        other = 1 - side
        query_in = (layer_norm(emb[side].astype(jnp.float32)) * gains[side, 0]).astype(jnp.bfloat16)
        memory_in = (layer_norm(emb[other].astype(jnp.float32)) * gains[side, 1]).astype(jnp.bfloat16)
        query = jnp.dot(query_in, w_query[side], preferred_element_type=jnp.float32).astype(jnp.bfloat16)
        keyval = jnp.dot(memory_in, w_keyval[side], preferred_element_type=jnp.float32).astype(jnp.bfloat16)
        count = query.shape[0]
        query_h = query.reshape(count, HEADS, head_size).astype(jnp.float32)
        key_h = keyval[:, :width].reshape(count, HEADS, head_size).astype(jnp.float32)
        value_h = keyval[:, width:].reshape(count, HEADS, head_size).astype(jnp.float32)
        scores = jnp.einsum('qhd,khd->hqk', query_h, key_h) * (1.0 / head_size ** 0.5)
        weights = jax.nn.softmax(scores, axis=-1)
        probs = weights.astype(jnp.bfloat16).astype(jnp.float32)
        context = jnp.einsum('hqk,khd->qhd', probs, value_h).astype(jnp.bfloat16).reshape(count, width)
        updated = emb[side].astype(jnp.float32) + jnp.dot(context, w_out[side], preferred_element_type=jnp.float32)
        final = (layer_norm(updated) * gains[side, 2]).astype(jnp.bfloat16)
        head = jnp.dot(w_head[side], final.T, preferred_element_type=jnp.float32)
        conf = 1.0 + jnp.exp(head[3])
        records.append(jnp.concatenate([conf[None, :] * head[:3], conf[None, :]], axis=0))
    return jnp.stack(records, axis=0)

def reference(tokens, pairs, w_embed, w_query, w_keyval, w_out, w_head, gains):
    start = jnp.zeros((VIEWS, 4, TOKV), jnp.float32)

    def one_pair(total, pair):
        chosen = jnp.take(tokens, pair.astype(jnp.int32), axis=0)
        emb = jnp.dot(chosen.reshape(2 * TOKV, E), w_embed, preferred_element_type=jnp.float32)
        emb = emb.astype(jnp.bfloat16).reshape(2, TOKV, D)
        record = decode_pair(emb, w_query, w_keyval, w_out, w_head, gains)
        total = total.at[pair[0]].add(record[0])
        total = total.at[pair[1]].add(record[1])
        return (total, None)
    total, unused = lax.scan(one_pair, start, pairs)
    return total
```

```python
import functools

import jax
import jax.numpy as jnp
from jax import lax
from jax.experimental import pallas as pl
from jax.experimental.pallas import tpu as pltpu
from jax.sharding import PartitionSpec as P

HEADS = 12
EPS = 1e-06
ANY = pl.BlockSpec(memory_space=pl.ANY)
SMEM = pl.BlockSpec(memory_space=pltpu.SMEM)
VMEM = pl.BlockSpec(memory_space=pltpu.VMEM)


def xor_pairs(count, step):
    return [(i, i ^ step) for i in range(count)]


def embed_kernel(count, parts, cap, me_ref, asked_ref, w_ref, *refs):
    pieces, outs = refs[:parts], refs[parts : parts + count]
    x_ref, w_vmem, emb_ref, in_sem, w_sem, out_sem = refs[parts + count :]
    views, rows, feat = pieces[0].shape
    width = w_ref.shape[1]
    row, column = me_ref[0], me_ref[1]
    w_copy = pltpu.make_async_copy(w_ref, w_vmem, w_sem)
    w_copy.start()
    copies = []
    for j in range(parts):
        start = pl.multiple_of((column ^ j) * feat, feat)
        copies.append(
            pltpu.make_async_copy(pieces[j], x_ref.at[:, :, pl.ds(start, feat)], in_sem.at[j])
        )
        copies[-1].start()
    w_copy.wait()
    for copy in copies:
        copy.wait()
    emb = jnp.dot(
        x_ref[...].reshape(views * rows, parts * feat), w_vmem[...], preferred_element_type=jnp.float32
    )
    emb_ref[...] = emb.astype(jnp.bfloat16).reshape(views, rows, width)
    copies = []
    for k in range(count):
        for c in range(cap):
            view = asked_ref[row ^ k, c]
            copies.append(
                pltpu.make_async_copy(emb_ref.at[view], outs[k].at[c], out_sem.at[k * cap + c])
            )
            copies[-1].start()
    for copy in copies:
        copy.wait()


def route_kernel(count, parts, cap, me_ref, side_ref, *refs):
    fetched, outs = refs[:count], refs[count : count + parts]
    stage_ref, in_sem, out_sem = refs[count + parts :]
    row, column = me_ref[0], me_ref[1]

    def slots(act):
        for k in range(count):
            for c in range(cap):
                side = side_ref[(row ^ k) * cap + c]

                @pl.when(side >= 0)
                def _():
                    act(
                        pltpu.make_async_copy(
                            fetched[k].at[c], stage_ref.at[side], in_sem.at[k * cap + c]
                        )
                    )

    slots(lambda copy: copy.start())
    slots(lambda copy: copy.wait())
    copies = []
    for j in range(parts):
        copies.append(
            pltpu.make_async_copy(
                stage_ref.at[pl.ds(2 * (column ^ j), 2)], outs[j], out_sem.at[j]
            )
        )
        copies[-1].start()
    for copy in copies:
        copy.wait()


def normed(values):
    mean = jnp.mean(values, axis=-1, keepdims=True)
    centred = values - mean
    var = jnp.mean(centred * centred, axis=-1, keepdims=True)
    return centred * lax.rsqrt(var + EPS)


def decode_kernel(parts, me_ref, gains_ref, whead_ref, wq_ref, wkv_ref, wo_ref, *refs):
    pieces, out_ref = refs[:parts], refs[parts]
    emb_ref, wq, wkv, wo, qin_ref, min_ref, q_ref, kv_ref, ctx_ref, sem, w_sem = refs[parts + 1 :]
    rows = pieces[0].shape[1]
    tokv, width = emb_ref.shape[1:]
    column = me_ref[1]
    copies = []
    for j in range(parts):
        start = pl.multiple_of((column ^ j) * rows, rows)
        copies.append(
            pltpu.make_async_copy(pieces[j], emb_ref.at[:, pl.ds(start, rows), :], sem.at[j])
        )
        copies[-1].start()
    wq_copy = pltpu.make_async_copy(wq_ref, wq, w_sem.at[0])
    wkv_copy = pltpu.make_async_copy(wkv_ref, wkv, w_sem.at[1])
    wo_copy = pltpu.make_async_copy(wo_ref, wo, w_sem.at[2])
    wq_copy.start()
    wkv_copy.start()
    wo_copy.start()
    for copy in copies:
        copy.wait()
    for side in range(2):
        xhat = normed(emb_ref[side].astype(jnp.float32))
        qin_ref[side] = (xhat * gains_ref[side, 0:1, :]).astype(jnp.bfloat16)
        min_ref[1 - side] = (xhat * gains_ref[1 - side, 1:2, :]).astype(jnp.bfloat16)
    wq_copy.wait()
    for side in range(2):
        q_ref[side] = jnp.dot(
            qin_ref[side], wq[side], preferred_element_type=jnp.float32
        ).astype(jnp.bfloat16)
    wkv_copy.wait()
    for side in range(2):
        kv_ref[side] = jnp.dot(
            min_ref[side], wkv[side], preferred_element_type=jnp.float32
        ).astype(jnp.bfloat16)

    head_size = width // HEADS
    lanes = 2 * head_size
    low = lax.broadcasted_iota(jnp.int32, (tokv, lanes), 1) < head_size

    def split(values):
        zero = jnp.zeros_like(values)
        return jnp.concatenate([jnp.where(low, values, zero), jnp.where(low, zero, values)], axis=0)

    def soft(scores):
        top = jnp.max(scores, axis=-1, keepdims=True)
        e = jnp.exp((scores - top) * (1.0 / head_size**0.5))
        return (e * (1.0 / jnp.sum(e, axis=-1, keepdims=True))).astype(jnp.bfloat16)

    def two_heads(i, carry):
        start = pl.multiple_of(i * lanes, lanes)
        for side in range(2):
            query = q_ref[side, :, pl.ds(start, lanes)]
            keys = split(kv_ref[side, :, pl.ds(start, lanes)])
            values = split(kv_ref[side, :, pl.ds(width + start, lanes)])
            scores = lax.dot_general(
                query, keys, (((1,), (1,)), ((), ())), preferred_element_type=jnp.float32
            )
            probs = jnp.concatenate([soft(scores[:, :tokv]), soft(scores[:, tokv:])], axis=1)
            ctx_ref[side, :, pl.ds(start, lanes)] = jnp.dot(
                probs, values, preferred_element_type=jnp.float32
            ).astype(jnp.bfloat16)
        return carry

    lax.fori_loop(0, HEADS // 2, two_heads, 0)
    wo_copy.wait()
    for side in range(2):
        updated = emb_ref[side].astype(jnp.float32) + jnp.dot(
            ctx_ref[side], wo[side], preferred_element_type=jnp.float32
        )
        final = (normed(updated) * gains_ref[side, 2:3, :]).astype(jnp.bfloat16)
        head = lax.dot_general(
            whead_ref[side], final, (((1,), (1,)), ((), ())), preferred_element_type=jnp.float32
        )
        conf = 1.0 + jnp.exp(head[3:4, :])
        out_ref[side, 0:3, :] = head[0:3, :] * conf
        out_ref[side, 3:4, :] = conf


def embed(count, parts, cap, me, asked, w_embed, pieces):
    views, rows, feat = pieces[0].shape
    full, width = w_embed.shape
    return pl.pallas_call(
        functools.partial(embed_kernel, count, parts, cap),
        out_shape=[jax.ShapeDtypeStruct((cap, rows, width), jnp.bfloat16)] * count,
        in_specs=[SMEM, SMEM, ANY] + [ANY] * parts,
        out_specs=[ANY] * count,
        scratch_shapes=[
            pltpu.VMEM((views, rows, full), jnp.bfloat16),
            pltpu.VMEM((full, width), jnp.bfloat16),
            pltpu.VMEM((views, rows, width), jnp.bfloat16),
            pltpu.SemaphoreType.DMA((parts,)),
            pltpu.SemaphoreType.DMA,
            pltpu.SemaphoreType.DMA((count * cap,)),
        ],
        name="embed",
    )(me, asked, w_embed, *pieces)


def route(count, parts, cap, me, sides, fetched):
    unused, rows, width = fetched[0].shape
    return pl.pallas_call(
        functools.partial(route_kernel, count, parts, cap),
        out_shape=[jax.ShapeDtypeStruct((2, rows, width), jnp.bfloat16)] * parts,
        in_specs=[SMEM, SMEM] + [ANY] * count,
        out_specs=[ANY] * parts,
        scratch_shapes=[
            pltpu.VMEM((2 * parts, rows, width), jnp.bfloat16),
            pltpu.SemaphoreType.DMA((count * cap,)),
            pltpu.SemaphoreType.DMA((parts,)),
        ],
        name="route",
    )(me, sides, *fetched)


def decode(parts, me, gains, w_head, w_query, w_keyval, w_out, pieces):
    unused, rows, width = pieces[0].shape
    tokv = parts * rows
    return pl.pallas_call(
        functools.partial(decode_kernel, parts),
        out_shape=jax.ShapeDtypeStruct((2, 4, tokv), jnp.float32),
        in_specs=[SMEM, VMEM, VMEM, ANY, ANY, ANY] + [ANY] * parts,
        out_specs=VMEM,
        scratch_shapes=[
            pltpu.VMEM((2, tokv, width), jnp.bfloat16),
            pltpu.VMEM(w_query.shape, jnp.bfloat16),
            pltpu.VMEM(w_keyval.shape, jnp.bfloat16),
            pltpu.VMEM(w_out.shape, jnp.bfloat16),
            pltpu.VMEM((2, tokv, width), jnp.bfloat16),
            pltpu.VMEM((2, tokv, width), jnp.bfloat16),
            pltpu.VMEM((2, tokv, width), jnp.bfloat16),
            pltpu.VMEM((2, tokv, 2 * width), jnp.bfloat16),
            pltpu.VMEM((2, tokv, width), jnp.bfloat16),
            pltpu.SemaphoreType.DMA((parts,)),
            pltpu.SemaphoreType.DMA((3,)),
        ],
        compiler_params=pltpu.CompilerParams(vmem_limit_bytes=44 * 1024 * 1024),
        name="decode",
    )(me, gains, w_head, w_query, w_keyval, w_out, *pieces)


def on_device(tokens, pairs, w_embed, w_query, w_keyval, w_out, w_head, gains):
    count = lax.axis_size("view")
    parts = lax.axis_size("mp")
    row = lax.axis_index("view")
    column = lax.axis_index("mp")
    me = jnp.stack([row, column]).astype(jnp.int32)
    view_dev, tokv, feat = tokens.shape
    rows = tokv // parts
    block_pairs = pairs.shape[0]
    pair_dev = block_pairs // parts
    side_count = 2 * block_pairs
    cap = max(2, (side_count + count - 1) // count)
    slot_total = count * cap

    pieces = []
    for j in range(parts):
        piece = lax.dynamic_slice_in_dim(tokens, (column ^ j) * rows, rows, axis=1)
        pieces.append(lax.ppermute(piece, "mp", xor_pairs(parts, j)) if j else piece)

    side_views = pairs.reshape(side_count)
    owners = side_views // view_dev
    local_ids = side_views % view_dev
    positions = jnp.arange(side_count, dtype=jnp.int32)
    same_owner = owners[:, None] == owners[None, :]
    slot_rank = jnp.sum(
        jnp.logical_and(same_owner, positions[None, :] < positions[:, None]), axis=1
    )
    slot_index = owners * cap + slot_rank
    slot_match = jnp.arange(slot_total, dtype=jnp.int32)[:, None] == slot_index[None, :]
    wanted = jnp.sum(jnp.where(slot_match, local_ids[None, :], 0), axis=1)
    used = jnp.any(slot_match, axis=1)
    slot_side = jnp.where(used, jnp.sum(jnp.where(slot_match, positions[None, :], 0), axis=1), -1)
    wanted = jnp.where(used, wanted, -1).reshape(count, cap)
    asked = lax.all_to_all(wanted, "view", split_axis=0, concat_axis=0, tiled=True)

    payload = embed(count, parts, cap, me, jnp.maximum(asked, 0), w_embed, pieces)
    fetched = [
        lax.ppermute(payload[k], "view", xor_pairs(count, k)) if k else payload[k]
        for k in range(count)
    ]
    results = []
    for c in range(pair_dev):
        slot_pair = slot_side // 2
        mine = jnp.logical_and(slot_side >= 0, slot_pair % pair_dev == c)
        place = jnp.where(mine, 2 * (slot_pair // pair_dev) + slot_side % 2, -1).astype(jnp.int32)
        parcels = route(count, parts, cap, me, place, fetched)
        arrived = [
            lax.ppermute(parcels[j], "mp", xor_pairs(parts, j)) if j else parcels[j]
            for j in range(parts)
        ]
        results.append(decode(parts, me, gains, w_head, w_query, w_keyval, w_out, arrived))
    results = jnp.stack(results)

    every = lax.all_gather(results, "mp", axis=0, tiled=True).reshape(side_count, 4 * tokv)
    slotted = jnp.dot(slot_match.astype(jnp.float32), every, precision=lax.Precision.HIGHEST)
    slotted = slotted.reshape(count, cap, 4, tokv)
    returned = lax.all_to_all(slotted, "view", split_axis=0, concat_axis=0, tiled=True)
    picker = (asked[:, :, None] == jnp.arange(view_dev, dtype=jnp.int32)[None, None, :]).astype(
        jnp.float32
    )
    summed = jnp.einsum(
        "rcv,rcx->vx",
        picker,
        returned.reshape(count, cap, 4 * tokv),
        precision=lax.Precision.HIGHEST,
    )
    return summed.reshape(view_dev, 4, tokv)


def solution(mesh):
    return jax.shard_map(
        on_device,
        mesh=mesh,
        in_specs=(P("view", None, "mp"), P("view", None), P(), P(), P(), P(), P(), P()),
        out_specs=P("view", None, None),
        check_vma=False,
    )
```

```python
import functools

import jax
import jax.numpy as jnp
from jax import lax
from jax.experimental import pallas as pl
from jax.experimental.pallas import tpu as pltpu
from jax.sharding import PartitionSpec as P

HEADS = 12
EPS = 1e-06
HBM = pl.BlockSpec(memory_space=pltpu.HBM)
SMEM = pl.BlockSpec(memory_space=pltpu.SMEM)
VMEM = pl.BlockSpec(memory_space=pltpu.VMEM)


def xor_pairs(count, step):
    return [(i, i ^ step) for i in range(count)]


def embed_kernel(parts, cuts, me_ref, w_ref, *refs):
    pieces, outs = refs[:parts], refs[parts : parts + len(cuts)]
    x_ref, w_vmem, emb_ref, in_sem, w_sem, out_sem = refs[parts + len(cuts) :]
    views, rows, feat = pieces[0].shape
    width = w_ref.shape[1]
    column = me_ref[1]
    w_copy = pltpu.make_async_copy(w_ref, w_vmem, w_sem)
    w_copy.start()
    copies = []
    for j in range(parts):
        start = pl.multiple_of((column ^ j) * feat, feat)
        copies.append(
            pltpu.make_async_copy(pieces[j], x_ref.at[:, :, pl.ds(start, feat)], in_sem.at[j])
        )
        copies[-1].start()
    w_copy.wait()
    for copy in copies:
        copy.wait()
    copies = []
    for q, (first, size) in enumerate(cuts):
        emb = jnp.dot(
            x_ref[:, first : first + size, :].reshape(views * size, parts * feat),
            w_vmem[...],
            preferred_element_type=jnp.float32,
        )
        emb_ref[:, first : first + size, :] = emb.astype(jnp.bfloat16).reshape(views, size, width)
        copies.append(
            pltpu.make_async_copy(
                emb_ref.at[:, pl.ds(first, size), :], outs[q], out_sem.at[q]
            )
        )
        copies[-1].start()
    for copy in copies:
        copy.wait()


def pick_kernel(sources, count, cap, offset, me_ref, asked_ref, *refs):
    parts, outs = refs[:sources], refs[sources : sources + count]
    stage_ref, in_sem, out_sem = refs[sources + count :]
    row = me_ref[0]
    copies, first = [], 0
    for i in range(sources):
        size = parts[i].shape[1]
        copies.append(
            pltpu.make_async_copy(parts[i], stage_ref.at[:, pl.ds(first, size), :], in_sem.at[i])
        )
        copies[-1].start()
        first += size
    for copy in copies:
        copy.wait()
    copies = []
    for k in range(count):
        for c in range(cap):
            view = jnp.maximum(asked_ref[(row ^ k) * (2 * cap) + offset + c], 0)
            copies.append(
                pltpu.make_async_copy(stage_ref.at[view], outs[k].at[c], out_sem.at[k * cap + c])
            )
            copies[-1].start()
    for copy in copies:
        copy.wait()


def route_kernel(half, parts, cap, first, groups, me_ref, side_ref, *refs):
    near, far = refs[:half], refs[half : 2 * half]
    outs = refs[2 * half : 2 * half + parts * groups]
    stage_ref, in_sem, out_sem = refs[2 * half + parts * groups :]
    size = stage_ref.shape[1]
    share = stage_ref.shape[0] // (parts * groups)
    row, column = me_ref[0], me_ref[1]

    def slots(act):
        for k in range(2 * half):
            for c in range(cap):
                side = side_ref[(row ^ k) * cap + c]
                source = near[k].at[c, pl.ds(first, size)] if k < half else far[k - half].at[c]

                @pl.when(side >= 0)
                def _():
                    act(pltpu.make_async_copy(source, stage_ref.at[side], in_sem.at[k * cap + c]))

    slots(lambda copy: copy.start())
    slots(lambda copy: copy.wait())
    copies = []
    for g in range(groups):
        for j in range(parts):
            start = ((column ^ j) * groups + g) * share
            copies.append(
                pltpu.make_async_copy(
                    stage_ref.at[pl.ds(start, share)],
                    outs[g * parts + j],
                    out_sem.at[g * parts + j],
                )
            )
            copies[-1].start()
    for copy in copies:
        copy.wait()


def normed(values):
    mean = jnp.mean(values, axis=-1, keepdims=True)
    centred = values - mean
    var = jnp.mean(centred * centred, axis=-1, keepdims=True)
    return centred * lax.rsqrt(var + EPS)


def decode_kernel(parts, cuts, pair, me_ref, gains_ref, whead_ref, wq, wkv, wo, *refs):
    pieces, out_ref = refs[: parts * len(cuts)], refs[parts * len(cuts)]
    emb_ref, qin_ref, min_ref, q_ref, kv_ref, ctx_ref, sem = refs[parts * len(cuts) + 1 :]
    tokv, width = emb_ref.shape[1:]
    rows = tokv // parts
    column = me_ref[1]
    copies = []
    for q, (first, size) in enumerate(cuts):
        for j in range(parts):
            i = q * parts + j
            at = 2 * pair if pieces[i].shape[0] > 2 else 0
            start = pl.multiple_of((column ^ j) * rows + first, size)
            copies.append(
                pltpu.make_async_copy(
                    pieces[i].at[at : at + 2], emb_ref.at[:, pl.ds(start, size), :], sem.at[i]
                )
            )
            copies[-1].start()
    for copy in copies:
        copy.wait()
    for side in range(2):
        xhat = normed(emb_ref[side].astype(jnp.float32))
        qin_ref[side] = (xhat * gains_ref[side, 0:1, :]).astype(jnp.bfloat16)
        min_ref[1 - side] = (xhat * gains_ref[1 - side, 1:2, :]).astype(jnp.bfloat16)
    for side in range(2):
        q_ref[side] = jnp.dot(
            qin_ref[side], wq[side], preferred_element_type=jnp.float32
        ).astype(jnp.bfloat16)
    for side in range(2):
        kv_ref[side] = jnp.dot(
            min_ref[side], wkv[side], preferred_element_type=jnp.float32
        ).astype(jnp.bfloat16)

    head_size = width // HEADS
    lanes = 2 * head_size
    low = lax.broadcasted_iota(jnp.int32, (tokv, lanes), 1) < head_size

    def split(values):
        zero = jnp.zeros_like(values)
        return jnp.concatenate([jnp.where(low, values, zero), jnp.where(low, zero, values)], axis=0)

    def soft(scores):
        top = jnp.max(scores, axis=-1, keepdims=True)
        e = jnp.exp((scores - top) * (1.0 / head_size**0.5))
        return (e * (1.0 / jnp.sum(e, axis=-1, keepdims=True))).astype(jnp.bfloat16)

    def two_heads(i, carry):
        start = pl.multiple_of(i * lanes, lanes)
        for side in range(2):
            query = q_ref[side, :, pl.ds(start, lanes)]
            keys = split(kv_ref[side, :, pl.ds(start, lanes)])
            values = split(kv_ref[side, :, pl.ds(width + start, lanes)])
            scores = lax.dot_general(
                query, keys, (((1,), (1,)), ((), ())), preferred_element_type=jnp.float32
            )
            probs = jnp.concatenate([soft(scores[:, :tokv]), soft(scores[:, tokv:])], axis=1)
            ctx_ref[side, :, pl.ds(start, lanes)] = jnp.dot(
                probs, values, preferred_element_type=jnp.float32
            ).astype(jnp.bfloat16)
        return carry

    for i in range(HEADS // 2):
        two_heads(i, 0)
    for side in range(2):
        updated = emb_ref[side].astype(jnp.float32) + jnp.dot(
            ctx_ref[side], wo[side], preferred_element_type=jnp.float32
        )
        final = (normed(updated) * gains_ref[side, 2:3, :]).astype(jnp.bfloat16)
        head = lax.dot_general(
            whead_ref[side], final, (((1,), (1,)), ((), ())), preferred_element_type=jnp.float32
        )
        conf = 1.0 + jnp.exp(head[3:4, :])
        out_ref[side, 0:3, :] = head[0:3, :] * conf
        out_ref[side, 3:4, :] = conf


def embed(parts, cuts, me, w_embed, pieces):
    views, rows, feat = pieces[0].shape
    full, width = w_embed.shape
    return pl.pallas_call(
        functools.partial(embed_kernel, parts, cuts),
        out_shape=[jax.ShapeDtypeStruct((views, size, width), jnp.bfloat16) for _, size in cuts],
        in_specs=[SMEM] + [HBM] * (parts + 1),
        out_specs=[HBM] * len(cuts),
        scratch_shapes=[
            pltpu.VMEM((views, rows, full), jnp.bfloat16),
            pltpu.VMEM((full, width), jnp.bfloat16),
            pltpu.VMEM((views, rows, width), jnp.bfloat16),
            pltpu.SemaphoreType.DMA((parts,)),
            pltpu.SemaphoreType.DMA,
            pltpu.SemaphoreType.DMA((len(cuts),)),
        ],
        compiler_params=pltpu.CompilerParams(vmem_limit_bytes=16 * 1024 * 1024),
        cost_estimate=pl.CostEstimate(
            flops=2 * views * rows * full * width,
            bytes_accessed=2 * (full * width + 2 * views * rows * full),
            transcendentals=0,
        ),
        name="embed",
    )(me, w_embed, *pieces)


def pick(count, cap, offset, me, asked, sources):
    views, unused, width = sources[0].shape
    rows = sum(source.shape[1] for source in sources)
    return pl.pallas_call(
        functools.partial(pick_kernel, len(sources), count, cap, offset),
        out_shape=[jax.ShapeDtypeStruct((cap, rows, width), jnp.bfloat16)] * count,
        in_specs=[SMEM, SMEM] + [HBM] * len(sources),
        out_specs=[HBM] * count,
        scratch_shapes=[
            pltpu.VMEM((views, rows, width), jnp.bfloat16),
            pltpu.SemaphoreType.DMA((len(sources),)),
            pltpu.SemaphoreType.DMA((count * cap,)),
        ],
        compiler_params=pltpu.CompilerParams(vmem_limit_bytes=16 * 1024 * 1024),
        cost_estimate=pl.CostEstimate(
            flops=0, bytes_accessed=4 * count * cap * rows * width, transcendentals=0
        ),
        name="pick",
    )(me, asked, *sources)


def route(parts, cap, first, size, groups, sides, me, slot_side, near, far):
    half, width = len(near), near[0].shape[2]
    share = sides // (parts * groups)
    return pl.pallas_call(
        functools.partial(route_kernel, half, parts, cap, first, groups),
        out_shape=[jax.ShapeDtypeStruct((share, size, width), jnp.bfloat16)] * (parts * groups),
        in_specs=[SMEM, SMEM] + [HBM] * (2 * half),
        out_specs=[HBM] * (parts * groups),
        scratch_shapes=[
            pltpu.VMEM((sides, size, width), jnp.bfloat16),
            pltpu.SemaphoreType.DMA((2 * half * cap,)),
            pltpu.SemaphoreType.DMA((parts * groups,)),
        ],
        compiler_params=pltpu.CompilerParams(vmem_limit_bytes=16 * 1024 * 1024),
        cost_estimate=pl.CostEstimate(
            flops=0, bytes_accessed=4 * sides * size * width, transcendentals=0
        ),
        name="route",
    )(me, slot_side, *near, *far)


def decode(parts, cuts, pair, me, gains, w_head, w_query, w_keyval, w_out, pieces):
    width = pieces[0].shape[2]
    tokv = parts * sum(size for _, size in cuts)
    flops = 2 * 2 * tokv * width * (5 * width + 2 * tokv)
    return pl.pallas_call(
        functools.partial(decode_kernel, parts, cuts, pair),
        out_shape=jax.ShapeDtypeStruct((2, 4, tokv), jnp.float32),
        in_specs=[SMEM, VMEM, VMEM, VMEM, VMEM, VMEM] + [HBM] * (parts * len(cuts)),
        out_specs=VMEM,
        scratch_shapes=[
            pltpu.VMEM((2, tokv, width), jnp.bfloat16),
            pltpu.VMEM((2, tokv, width), jnp.bfloat16),
            pltpu.VMEM((2, tokv, width), jnp.bfloat16),
            pltpu.VMEM((2, tokv, width), jnp.bfloat16),
            pltpu.VMEM((2, tokv, 2 * width), jnp.bfloat16),
            pltpu.VMEM((2, tokv, width), jnp.bfloat16),
            pltpu.SemaphoreType.DMA((parts * len(cuts),)),
        ],
        compiler_params=pltpu.CompilerParams(vmem_limit_bytes=36 * 1024 * 1024),
        cost_estimate=pl.CostEstimate(
            flops=flops, bytes_accessed=20 * width * width, transcendentals=2 * HEADS * tokv * tokv
        ),
        name="decode",
    )(me, gains, w_head, w_query, w_keyval, w_out, *pieces)


def on_device(tokens, pairs, w_embed, w_query, w_keyval, w_out, w_head, gains):
    count = lax.axis_size("view")
    parts = lax.axis_size("mp")
    row = lax.axis_index("view")
    column = lax.axis_index("mp")
    me = jnp.stack([row, column]).astype(jnp.int32)
    view_dev, tokv, feat = tokens.shape
    rows = tokv // parts
    block_pairs = pairs.shape[0]
    pair_dev = block_pairs // parts
    side_count = 2 * block_pairs
    cap = max(2, (side_count + count - 1) // count)
    slot_total = count * cap
    half = count // 2
    cuts = ((0, rows // 2), (rows // 2, rows // 2)) if rows % 32 == 0 else ((0, rows),)
    last = len(cuts) - 1

    pieces = []
    for j in range(parts):
        piece = lax.dynamic_slice_in_dim(tokens, (column ^ j) * rows, rows, axis=1)
        pieces.append(lax.ppermute(piece, "mp", xor_pairs(parts, j)) if j else piece)

    side_views = pairs.reshape(side_count)
    owners = side_views // view_dev
    local_ids = side_views % view_dev
    positions = jnp.arange(side_count, dtype=jnp.int32)
    same_owner = owners[:, None] == owners[None, :]
    slot_rank = jnp.sum(
        jnp.logical_and(same_owner, positions[None, :] < positions[:, None]), axis=1
    )
    slot_index = owners * cap + slot_rank
    slot_match = jnp.arange(slot_total, dtype=jnp.int32)[:, None] == slot_index[None, :]
    wanted = jnp.sum(jnp.where(slot_match, local_ids[None, :], 0), axis=1)
    used = jnp.any(slot_match, axis=1)
    slot_side = jnp.where(used, jnp.sum(jnp.where(slot_match, positions[None, :], 0), axis=1), -1)
    slot_side = slot_side.astype(jnp.int32)
    wanted = jnp.where(used, wanted, -1).reshape(count, cap)
    wanted = jnp.concatenate([wanted, jnp.roll(wanted, half, axis=0)], axis=1)
    asked = lax.all_to_all(wanted, "view", split_axis=0, concat_axis=0, tiled=True)
    asked_flat = asked.reshape(count * 2 * cap)

    embedded = embed(parts, cuts, me, w_embed, pieces)
    mirrored = [lax.ppermute(part, "view", xor_pairs(count, half)) for part in embedded]
    near = pick(half, cap, 0, me, asked_flat, embedded)
    near = [
        lax.ppermute(near[k], "view", xor_pairs(count, k)) if k else near[k] for k in range(half)
    ]
    early, results = [], []
    for q, (first, size) in enumerate(cuts):
        far = pick(half, cap, cap, me, asked_flat, [mirrored[q]])
        far = [
            lax.ppermute(far[k], "view", xor_pairs(count, k)) if k else far[k] for k in range(half)
        ]
        groups = pair_dev if q == last else 1
        parcels = route(
            parts, cap, first, size, groups, side_count, me, slot_side, near, far
        )
        if q < last:
            early += [
                lax.ppermute(parcels[j], "mp", xor_pairs(parts, j)) if j else parcels[j]
                for j in range(parts)
            ]
    for c in range(pair_dev):
        own = parcels[c * parts : (c + 1) * parts]
        if c:
            own, arrived = lax.optimization_barrier((own, arrived))
        arrived = [
            lax.ppermute(own[j], "mp", xor_pairs(parts, j)) if j else own[j] for j in range(parts)
        ]
        results.append(
            decode(parts, cuts, c, me, gains, w_head, w_query, w_keyval, w_out, early + arrived)
        )
    results = jnp.stack(results)

    every = lax.all_gather(results, "mp", axis=0, tiled=True).reshape(side_count, 4 * tokv)
    slotted = jnp.dot(slot_match.astype(jnp.float32), every, precision=lax.Precision.HIGHEST)
    slotted = slotted.reshape(count, cap, 4, tokv)
    returned = lax.all_to_all(slotted, "view", split_axis=0, concat_axis=0, tiled=True)
    picker = (asked[:, :cap, None] == jnp.arange(view_dev, dtype=jnp.int32)[None, None, :]).astype(
        jnp.float32
    )
    summed = jnp.einsum(
        "rcv,rcx->vx",
        picker,
        returned.reshape(count, cap, 4 * tokv),
        precision=lax.Precision.HIGHEST,
    )
    return summed.reshape(view_dev, 4, tokv)


def solution(mesh):
    return jax.shard_map(
        on_device,
        mesh=mesh,
        in_specs=(P("view", None, "mp"), P("view", None), P(), P(), P(), P(), P(), P()),
        out_specs=P("view", None, None),
        check_vma=False,
    )
```

```python
import functools

import jax
import jax.numpy as jnp
from jax import lax
from jax.experimental import pallas as pl
from jax.experimental.pallas import tpu as pltpu
from jax.sharding import PartitionSpec as P

HEADS = 12
EPS = 1e-06
HBM = pl.BlockSpec(memory_space=pltpu.HBM)
SMEM = pl.BlockSpec(memory_space=pltpu.SMEM)
VMEM = pl.BlockSpec(memory_space=pltpu.VMEM)


def xor_pairs(count, step):
    return [(i, i ^ step) for i in range(count)]


def embed_kernel(parts, cuts, me_ref, w_ref, *refs):
    pieces, outs = refs[:parts], refs[parts : parts + len(cuts)]
    x_ref, w_vmem, emb_ref, in_sem, w_sem, out_sem = refs[parts + len(cuts) :]
    views, rows, feat = pieces[0].shape
    width = w_ref.shape[1]
    column = me_ref[1]
    w_copy = pltpu.make_async_copy(w_ref, w_vmem, w_sem)
    w_copy.start()
    copies = []
    for j in range(parts):
        start = pl.multiple_of((column ^ j) * feat, feat)
        copies.append(
            pltpu.make_async_copy(pieces[j], x_ref.at[:, :, pl.ds(start, feat)], in_sem.at[j])
        )
        copies[-1].start()
    w_copy.wait()
    for copy in copies:
        copy.wait()
    copies = []
    for q, (first, size) in enumerate(cuts):
        emb = jnp.dot(
            x_ref[:, first : first + size, :].reshape(views * size, parts * feat),
            w_vmem[...],
            preferred_element_type=jnp.float32,
        )
        emb_ref[:, first : first + size, :] = emb.astype(jnp.bfloat16).reshape(views, size, width)
        copies.append(
            pltpu.make_async_copy(
                emb_ref.at[:, pl.ds(first, size), :], outs[q], out_sem.at[q]
            )
        )
        copies[-1].start()
    for copy in copies:
        copy.wait()


def pick_kernel(lanes, reach, slots, cap, me_ref, line_ref, want_ref, *refs):
    count = 1 + 2 * reach
    own, below, above = refs[0], refs[1 : 1 + reach], refs[1 + reach : count]
    outs = refs[count : count + lanes]
    stage_ref, in_sem, out_sem = refs[count + lanes :]
    place, lane = me_ref[0] // lanes, me_ref[0] % lanes
    rows = line_ref.shape[0] * lanes

    def sources(act):
        for n, i in enumerate(slots):
            at = line_ref[i]
            if i == 0:
                act(pltpu.make_async_copy(own, stage_ref.at[n], in_sem.at[n]))
            for p in range(1, i + 1):
                for want, source in ((place - p, below[p - 1]), (place + p, above[p - 1])):

                    @pl.when(at == want)
                    def _():
                        act(pltpu.make_async_copy(source, stage_ref.at[n], in_sem.at[n]))

    sources(lambda copy: copy.start())
    sources(lambda copy: copy.wait())
    copies = []
    for j in range(lanes):
        for n, i in enumerate(slots):
            for c in range(cap):
                view = want_ref[(j * rows + line_ref[i] * lanes + lane) * cap + c]
                copies.append(
                    pltpu.make_async_copy(
                        stage_ref.at[n, jnp.maximum(view, 0)], outs[j].at[n, c], out_sem.at[len(copies)]
                    )
                )
                copies[-1].start()
    for copy in copies:
        copy.wait()


def route_kernel(lanes, parts, cap, cuts, groups, me_ref, line_ref, side_ref, *refs):
    count = len(cuts) * len(groups) * lanes
    fetched, outs = refs[:count], refs[count : count + parts]
    stage_ref, in_sem, out_sem = refs[count + parts :]
    lane, column = me_ref[0] % lanes, me_ref[1]

    def slots(act):
        number = 0
        for q, (first, size) in enumerate(cuts):
            for g, group in enumerate(groups):
                for j in range(lanes):
                    source = fetched[(q * len(groups) + g) * lanes + j]
                    for n, i in enumerate(group):
                        for c in range(cap):
                            side = side_ref[(line_ref[i] * lanes + (lane ^ j)) * cap + c]

                            @pl.when(side >= 0)
                            def _():
                                act(
                                    pltpu.make_async_copy(
                                        source.at[n, c],
                                        stage_ref.at[side, pl.ds(first, size), :],
                                        in_sem.at[number],
                                    )
                                )

                            number += 1

    slots(lambda copy: copy.start())
    slots(lambda copy: copy.wait())
    copies = []
    for j in range(parts):
        copies.append(
            pltpu.make_async_copy(
                stage_ref.at[pl.ds(2 * (column ^ j), 2)], outs[j], out_sem.at[j]
            )
        )
        copies[-1].start()
    for copy in copies:
        copy.wait()


def normed(values):
    mean = jnp.mean(values, axis=-1, keepdims=True)
    centred = values - mean
    var = jnp.mean(centred * centred, axis=-1, keepdims=True)
    return centred * lax.rsqrt(var + EPS)


def decode_kernel(parts, cuts, me_ref, gains_ref, whead_ref, wkv, wq_ref, wo_ref, *refs):
    pieces, out_ref = refs[: parts * len(cuts)], refs[parts * len(cuts)]
    scratch = refs[parts * len(cuts) + 1 :]
    emb_ref, qin_ref, min_ref, q_ref, kv_ref, ctx_ref, wq, wo, sem, w_sem = scratch
    tokv, width = emb_ref.shape[1:]
    rows = tokv // parts
    column = me_ref[1]
    copies = []
    for q, (first, size) in enumerate(cuts):
        for j in range(parts):
            i = q * parts + j
            start = pl.multiple_of((column ^ j) * rows + first, size)
            copies.append(
                pltpu.make_async_copy(pieces[i], emb_ref.at[:, pl.ds(start, size), :], sem.at[i])
            )
            copies[-1].start()
    wq_copy = pltpu.make_async_copy(wq_ref, wq, w_sem.at[0])
    wo_copy = pltpu.make_async_copy(wo_ref, wo, w_sem.at[1])
    wq_copy.start()
    for copy in copies:
        copy.wait()
    wo_copy.start()
    for side in range(2):
        xhat = normed(emb_ref[side].astype(jnp.float32))
        qin_ref[side] = (xhat * gains_ref[side, 0:1, :]).astype(jnp.bfloat16)
        min_ref[1 - side] = (xhat * gains_ref[1 - side, 1:2, :]).astype(jnp.bfloat16)
    wq_copy.wait()
    for side in range(2):
        q_ref[side] = jnp.dot(
            qin_ref[side], wq[side], preferred_element_type=jnp.float32
        ).astype(jnp.bfloat16)
    for side in range(2):
        kv_ref[side] = jnp.dot(
            min_ref[side], wkv[side], preferred_element_type=jnp.float32
        ).astype(jnp.bfloat16)

    head_size = width // HEADS
    lanes = 2 * head_size
    low = lax.broadcasted_iota(jnp.int32, (tokv, lanes), 1) < head_size

    def split(values):
        zero = jnp.zeros_like(values)
        return jnp.concatenate([jnp.where(low, values, zero), jnp.where(low, zero, values)], axis=0)

    def soft(scores):
        top = jnp.max(scores, axis=-1, keepdims=True)
        e = jnp.exp((scores - top) * (1.0 / head_size**0.5))
        return (e * (1.0 / jnp.sum(e, axis=-1, keepdims=True))).astype(jnp.bfloat16)

    def two_heads(i, carry):
        start = pl.multiple_of(i * lanes, lanes)
        for side in range(2):
            query = q_ref[side, :, pl.ds(start, lanes)]
            keys = split(kv_ref[side, :, pl.ds(start, lanes)])
            values = split(kv_ref[side, :, pl.ds(width + start, lanes)])
            scores = lax.dot_general(
                query, keys, (((1,), (1,)), ((), ())), preferred_element_type=jnp.float32
            )
            probs = jnp.concatenate([soft(scores[:, :tokv]), soft(scores[:, tokv:])], axis=1)
            ctx_ref[side, :, pl.ds(start, lanes)] = jnp.dot(
                probs, values, preferred_element_type=jnp.float32
            ).astype(jnp.bfloat16)
        return carry

    for i in range(HEADS // 2):
        two_heads(i, 0)
    wo_copy.wait()
    for side in range(2):
        updated = emb_ref[side].astype(jnp.float32) + jnp.dot(
            ctx_ref[side], wo[side], preferred_element_type=jnp.float32
        )
        final = (normed(updated) * gains_ref[side, 2:3, :]).astype(jnp.bfloat16)
        head = lax.dot_general(
            whead_ref[side], final, (((1,), (1,)), ((), ())), preferred_element_type=jnp.float32
        )
        conf = 1.0 + jnp.exp(head[3:4, :])
        out_ref[side, 0:3, :] = head[0:3, :] * conf
        out_ref[side, 3:4, :] = conf


def embed(parts, cuts, me, w_embed, pieces):
    views, rows, feat = pieces[0].shape
    full, width = w_embed.shape
    return pl.pallas_call(
        functools.partial(embed_kernel, parts, cuts),
        out_shape=[jax.ShapeDtypeStruct((views, size, width), jnp.bfloat16) for _, size in cuts],
        in_specs=[SMEM] + [HBM] * (parts + 1),
        out_specs=[HBM] * len(cuts),
        scratch_shapes=[
            pltpu.VMEM((views, rows, full), jnp.bfloat16),
            pltpu.VMEM((full, width), jnp.bfloat16),
            pltpu.VMEM((views, rows, width), jnp.bfloat16),
            pltpu.SemaphoreType.DMA((parts,)),
            pltpu.SemaphoreType.DMA,
            pltpu.SemaphoreType.DMA((len(cuts),)),
        ],
        compiler_params=pltpu.CompilerParams(vmem_limit_bytes=16 * 1024 * 1024),
        cost_estimate=pl.CostEstimate(
            flops=2 * views * rows * full * width,
            bytes_accessed=2 * (full * width + 2 * views * rows * full),
            transcendentals=0,
        ),
        name="embed",
    )(me, w_embed, *pieces)


def pick(lanes, slots, cap, me, line, wants, own, below, above):
    views, size, width = own.shape
    reach = len(below)
    return pl.pallas_call(
        functools.partial(pick_kernel, lanes, reach, slots, cap),
        out_shape=[jax.ShapeDtypeStruct((len(slots), cap, size, width), jnp.bfloat16)] * lanes,
        in_specs=[SMEM, SMEM, SMEM] + [HBM] * (1 + 2 * reach),
        out_specs=[HBM] * lanes,
        scratch_shapes=[
            pltpu.VMEM((len(slots), views, size, width), jnp.bfloat16),
            pltpu.SemaphoreType.DMA((len(slots),)),
            pltpu.SemaphoreType.DMA((lanes * len(slots) * cap,)),
        ],
        compiler_params=pltpu.CompilerParams(vmem_limit_bytes=16 * 1024 * 1024),
        cost_estimate=pl.CostEstimate(
            flops=0,
            bytes_accessed=4 * lanes * len(slots) * cap * size * width,
            transcendentals=0,
        ),
        name="pick",
    )(me, line, wants, own, *below, *above)


def route(lanes, parts, cap, cuts, groups, me, line, sides, fetched):
    width = fetched[0].shape[-1]
    size = sum(size for _, size in cuts)
    base = cuts[0][0]
    cuts = tuple((first - base, each) for first, each in cuts)
    copies = len(cuts) * sum(len(group) for group in groups) * lanes * cap
    return pl.pallas_call(
        functools.partial(route_kernel, lanes, parts, cap, cuts, groups),
        out_shape=[jax.ShapeDtypeStruct((2, size, width), jnp.bfloat16)] * parts,
        in_specs=[SMEM, SMEM, SMEM] + [HBM] * len(fetched),
        out_specs=[HBM] * parts,
        scratch_shapes=[
            pltpu.VMEM((2 * parts, size, width), jnp.bfloat16),
            pltpu.SemaphoreType.DMA((copies,)),
            pltpu.SemaphoreType.DMA((parts,)),
        ],
        compiler_params=pltpu.CompilerParams(vmem_limit_bytes=16 * 1024 * 1024),
        cost_estimate=pl.CostEstimate(
            flops=0, bytes_accessed=8 * parts * size * width, transcendentals=0
        ),
        name="route",
    )(me, line, sides, *fetched)


def decode(parts, cuts, me, gains, w_head, w_query, w_keyval, w_out, pieces):
    width = pieces[0].shape[2]
    tokv = parts * sum(size for _, size in cuts)
    flops = 2 * 2 * tokv * width * (5 * width + 2 * tokv)
    return pl.pallas_call(
        functools.partial(decode_kernel, parts, cuts),
        out_shape=jax.ShapeDtypeStruct((2, 4, tokv), jnp.float32),
        in_specs=[SMEM, VMEM, VMEM, VMEM, HBM, HBM] + [HBM] * (parts * len(cuts)),
        out_specs=VMEM,
        scratch_shapes=[
            pltpu.VMEM((2, tokv, width), jnp.bfloat16),
            pltpu.VMEM((2, tokv, width), jnp.bfloat16),
            pltpu.VMEM((2, tokv, width), jnp.bfloat16),
            pltpu.VMEM((2, tokv, width), jnp.bfloat16),
            pltpu.VMEM((2, tokv, 2 * width), jnp.bfloat16),
            pltpu.VMEM((2, tokv, width), jnp.bfloat16),
            pltpu.VMEM(w_query.shape, jnp.bfloat16),
            pltpu.VMEM(w_out.shape, jnp.bfloat16),
            pltpu.SemaphoreType.DMA((parts * len(cuts),)),
            pltpu.SemaphoreType.DMA((2,)),
        ],
        compiler_params=pltpu.CompilerParams(vmem_limit_bytes=56 * 1024 * 1024),
        cost_estimate=pl.CostEstimate(
            flops=flops, bytes_accessed=20 * width * width, transcendentals=2 * HEADS * tokv * tokv
        ),
        name="decode",
    )(me, gains, w_head, w_keyval, w_query, w_out, *pieces)


def on_device(tokens, pairs, w_embed, w_query, w_keyval, w_out, w_head, gains):
    count = lax.axis_size("view")
    parts = lax.axis_size("mp")
    row = lax.axis_index("view")
    column = lax.axis_index("mp")
    me = jnp.stack([row, column]).astype(jnp.int32)
    view_dev, tokv, feat = tokens.shape
    rows = tokv // parts
    block_pairs = pairs.shape[0]
    pair_dev = block_pairs // parts
    side_count = 2 * block_pairs
    cap = max(2, (side_count + count - 1) // count)
    slot_total = count * cap
    lanes = 1 << ((count.bit_length() - 1) // 2)
    length = count // lanes
    cuts = ((0, rows // 2), (rows // 2, rows // 2)) if rows % 32 == 0 else ((0, rows),)

    pieces = []
    for j in range(parts):
        piece = lax.dynamic_slice_in_dim(tokens, (column ^ j) * rows, rows, axis=1)
        pieces.append(lax.ppermute(piece, "mp", xor_pairs(parts, j)) if j else piece)

    side_views = pairs.reshape(side_count)
    owners = side_views // view_dev
    local_ids = side_views % view_dev
    positions = jnp.arange(side_count, dtype=jnp.int32)
    same_owner = owners[:, None] == owners[None, :]
    slot_rank = jnp.sum(
        jnp.logical_and(same_owner, positions[None, :] < positions[:, None]), axis=1
    )
    slot_index = owners * cap + slot_rank
    slot_match = jnp.arange(slot_total, dtype=jnp.int32)[:, None] == slot_index[None, :]
    wanted = jnp.sum(jnp.where(slot_match, local_ids[None, :], 0), axis=1)
    used = jnp.any(slot_match, axis=1)
    slot_side = jnp.where(used, jnp.sum(jnp.where(slot_match, positions[None, :], 0), axis=1), -1)
    slot_side = slot_side.astype(jnp.int32)
    wanted = jnp.where(used, wanted, -1).astype(jnp.int32)
    wants = jnp.concatenate(
        [lax.ppermute(wanted, "view", xor_pairs(count, j)) if j else wanted for j in range(lanes)]
    )
    nearest = [sorted(range(length), key=lambda at: (abs(at - z), at)) for z in range(length)]
    line = jnp.asarray(nearest, jnp.int32)[row // lanes]

    embedded = embed(parts, cuts, me, w_embed, pieces)
    below, above = [[] for _ in cuts], [[] for _ in cuts]
    for p in range(1, length):
        up = [
            (z * lanes + y, (z + 1) * lanes + y) for z in range(p - 1, length - 1) for y in range(lanes)
        ]
        down = [
            (z * lanes + y, (z - 1) * lanes + y) for z in range(1, length - p + 1) for y in range(lanes)
        ]
        for q in range(len(cuts)):
            below[q].append(lax.ppermute((below[q] or [embedded[q]])[-1], "view", up))
            above[q].append(lax.ppermute((above[q] or [embedded[q]])[-1], "view", down))
    groups = (tuple(range(length - 1)), (length - 1,))
    fetched = []
    for q in range(len(cuts)):
        for group in groups:
            reach = group[-1]
            picked = pick(
                lanes, group, cap, me, line, wants, embedded[q], below[q][:reach], above[q][:reach]
            )
            fetched.append(
                [
                    lax.ppermute(picked[j], "view", xor_pairs(count, j)) if j else picked[j]
                    for j in range(lanes)
                ]
            )
    slot_pair = slot_side // 2
    results, arrived = [], None
    for c in range(pair_dev):
        mine = jnp.logical_and(slot_side >= 0, slot_pair % pair_dev == c)
        place = jnp.where(mine, 2 * (slot_pair // pair_dev) + slot_side % 2, -1).astype(jnp.int32)
        steps = [(cut,) for cut in cuts] if c == 0 else [cuts]
        parcels = []
        for q, step in enumerate(steps):
            wave = fetched[2 * q : 2 * q + 2] if c == 0 else fetched
            parcels += route(
                lanes, parts, cap, step, groups, me, line, place, [each for g in wave for each in g]
            )
        if c:
            parcels, arrived = lax.optimization_barrier((parcels, arrived))
        arrived = [
            lax.ppermute(parcel, "mp", xor_pairs(parts, i % parts)) if i % parts else parcel
            for i, parcel in enumerate(parcels)
        ]
        results.append(
            decode(
                parts,
                cuts if c == 0 else ((0, rows),),
                me,
                gains,
                w_head,
                w_query,
                w_keyval,
                w_out,
                arrived,
            )
        )
    results = jnp.stack(results)

    every = lax.all_gather(results, "mp", axis=0, tiled=True).reshape(side_count, 4 * tokv)
    slotted = jnp.dot(slot_match.astype(jnp.float32), every, precision=lax.Precision.HIGHEST)
    tags = jnp.broadcast_to(wanted.astype(jnp.float32)[:, None], (slot_total, 128))
    slotted = jnp.concatenate([slotted, tags], axis=1).reshape(count, cap, 4 * tokv + 128)
    returned = lax.all_to_all(slotted, "view", split_axis=0, concat_axis=0, tiled=True)
    picker = returned[:, :, 4 * tokv :][:, :, :1] == jnp.arange(view_dev, dtype=jnp.float32)
    summed = jnp.einsum(
        "rcv,rcx->vx",
        picker.astype(jnp.float32),
        returned[:, :, : 4 * tokv],
        precision=lax.Precision.HIGHEST,
    )
    return summed.reshape(view_dev, 4, tokv)


def solution(mesh):
    return jax.shard_map(
        on_device,
        mesh=mesh,
        in_specs=(P("view", None, "mp"), P("view", None), P(), P(), P(), P(), P(), P()),
        out_specs=P("view", None, None),
        check_vma=False,
    )
```

```python
import functools

import jax
import jax.numpy as jnp
from jax import lax
from jax.experimental import pallas as pl
from jax.experimental.pallas import tpu as pltpu
from jax.sharding import PartitionSpec as P

HEADS = 12
EPS = 1e-06
HBM = pl.BlockSpec(memory_space=pltpu.HBM)
SMEM = pl.BlockSpec(memory_space=pltpu.SMEM)
VMEM = pl.BlockSpec(memory_space=pltpu.VMEM)


def xor_pairs(count, step):
    return [(i, i ^ step) for i in range(count)]


def load_kernel(*refs):
    count = len(refs) // 2
    copies = [pltpu.make_async_copy(refs[i], refs[count + i], refs[-1].at[i]) for i in range(count)]
    for copy in copies:
        copy.start()
    for copy in copies:
        copy.wait()


def embed_kernel(parts, cuts, me_ref, w_vmem, *refs):
    pieces, outs, whole = refs[:parts], refs[parts : parts + len(cuts)], refs[parts + len(cuts)]
    x_ref, emb_ref, in_sem, out_sem = refs[parts + len(cuts) + 1 :]
    views, rows, feat = pieces[0].shape
    width = w_vmem.shape[1]
    column = me_ref[1]
    copies = []
    for j in range(parts):
        start = pl.multiple_of((column ^ j) * feat, feat)
        copies.append(
            pltpu.make_async_copy(pieces[j], x_ref.at[:, :, pl.ds(start, feat)], in_sem.at[j])
        )
        copies[-1].start()
    for copy in copies:
        copy.wait()
    copies = []
    for q, (first, size) in enumerate(cuts):
        emb = jnp.dot(
            x_ref[:, first : first + size, :].reshape(views * size, parts * feat),
            w_vmem[...],
            preferred_element_type=jnp.float32,
        )
        emb_ref[:, first : first + size, :] = emb.astype(jnp.bfloat16).reshape(views, size, width)
        copies.append(
            pltpu.make_async_copy(
                emb_ref.at[:, pl.ds(first, size), :], outs[q], out_sem.at[q]
            )
        )
        copies[-1].start()
    copies.append(pltpu.make_async_copy(emb_ref, whole, out_sem.at[len(cuts)]))
    copies[-1].start()
    for copy in copies:
        copy.wait()


def pick_kernel(lanes, reach, slots, cap, me_ref, line_ref, want_ref, *refs):
    count = 1 + 2 * reach
    own, below, above = refs[0], refs[1 : 1 + reach], refs[1 + reach : count]
    outs = refs[count : count + lanes]
    stage_ref, in_sem, out_sem = refs[count + lanes :]
    place, lane = me_ref[0] // lanes, me_ref[0] % lanes
    rows = line_ref.shape[0] * lanes

    def sources(act):
        for n, i in enumerate(slots):
            at = line_ref[i]
            if i == 0:
                act(pltpu.make_async_copy(own, stage_ref.at[n], in_sem.at[n]))
            for p in range(1, i + 1):
                for want, source in ((place - p, below[p - 1]), (place + p, above[p - 1])):

                    @pl.when(at == want)
                    def _():
                        act(pltpu.make_async_copy(source, stage_ref.at[n], in_sem.at[n]))

    sources(lambda copy: copy.start())
    sources(lambda copy: copy.wait())
    copies = []
    for j in range(lanes):
        for n, i in enumerate(slots):
            for c in range(cap):
                view = want_ref[(j * rows + line_ref[i] * lanes + lane) * cap + c]
                copies.append(
                    pltpu.make_async_copy(
                        stage_ref.at[n, jnp.maximum(view, 0)], outs[j].at[n, c], out_sem.at[len(copies)]
                    )
                )
                copies[-1].start()
    for copy in copies:
        copy.wait()


def route_kernel(lanes, parts, cap, base, cuts, groups, me_ref, line_ref, side_ref, *refs):
    count = len(cuts) * len(groups) * lanes
    fetched, outs = refs[:count], refs[count : count + parts]
    stage_ref, in_sem, out_sem = refs[count + parts :]
    lane, column = me_ref[0] % lanes, me_ref[1]

    def slots(act):
        number = 0
        for q, (first, size) in enumerate(cuts):
            for g, group in enumerate(groups):
                for j in range(lanes):
                    source = fetched[(q * len(groups) + g) * lanes + j]
                    for n, i in enumerate(group):
                        for c in range(cap):
                            side = side_ref[(line_ref[i] * lanes + (lane ^ j)) * cap + c]
                            part = source.at[n, c]
                            if source.shape[2] > size:
                                part = source.at[n, c, pl.ds(base + first, size)]

                            @pl.when(side >= 0)
                            def _():
                                act(
                                    pltpu.make_async_copy(
                                        part,
                                        stage_ref.at[side, pl.ds(first, size), :],
                                        in_sem.at[number],
                                    )
                                )

                            number += 1

    slots(lambda copy: copy.start())
    slots(lambda copy: copy.wait())
    copies = []
    for j in range(parts):
        copies.append(
            pltpu.make_async_copy(
                stage_ref.at[pl.ds(2 * (column ^ j), 2)], outs[j], out_sem.at[j]
            )
        )
        copies[-1].start()
    for copy in copies:
        copy.wait()


def normed(values):
    mean = jnp.mean(values, axis=-1, keepdims=True)
    centred = values - mean
    var = jnp.mean(centred * centred, axis=-1, keepdims=True)
    return centred * lax.rsqrt(var + EPS)


def decode_kernel(parts, cuts, me_ref, gains_ref, whead_ref, wkv, wq, wo, *refs):
    pieces, out_ref = refs[: parts * len(cuts)], refs[parts * len(cuts)]
    scratch = refs[parts * len(cuts) + 1 :]
    emb_ref, qin_ref, min_ref, q_ref, kv_ref, ctx_ref, sem = scratch
    tokv, width = emb_ref.shape[1:]
    rows = tokv // parts
    column = me_ref[1]
    copies = []
    for q, (first, size) in enumerate(cuts):
        for j in range(parts):
            i = q * parts + j
            start = pl.multiple_of((column ^ j) * rows + first, size)
            copies.append(
                pltpu.make_async_copy(pieces[i], emb_ref.at[:, pl.ds(start, size), :], sem.at[i])
            )
            copies[-1].start()
    for copy in copies:
        copy.wait()
    for side in range(2):
        xhat = normed(emb_ref[side].astype(jnp.float32))
        qin_ref[side] = (xhat * gains_ref[side, 0:1, :]).astype(jnp.bfloat16)
        min_ref[1 - side] = (xhat * gains_ref[1 - side, 1:2, :]).astype(jnp.bfloat16)
    for side in range(2):
        q_ref[side] = jnp.dot(
            qin_ref[side], wq[side], preferred_element_type=jnp.float32
        ).astype(jnp.bfloat16)
    for side in range(2):
        kv_ref[side] = jnp.dot(
            min_ref[side], wkv[side], preferred_element_type=jnp.float32
        ).astype(jnp.bfloat16)

    head_size = width // HEADS
    lanes = 2 * head_size
    low = lax.broadcasted_iota(jnp.int32, (tokv, lanes), 1) < head_size

    def split(values):
        zero = jnp.zeros_like(values)
        return jnp.concatenate([jnp.where(low, values, zero), jnp.where(low, zero, values)], axis=0)

    def soft(scores):
        top = jnp.max(scores, axis=-1, keepdims=True)
        e = jnp.exp((scores - top) * (1.0 / head_size**0.5))
        return (e * (1.0 / jnp.sum(e, axis=-1, keepdims=True))).astype(jnp.bfloat16)

    def two_heads(i, carry):
        start = pl.multiple_of(i * lanes, lanes)
        for side in range(2):
            query = q_ref[side, :, pl.ds(start, lanes)]
            keys = split(kv_ref[side, :, pl.ds(start, lanes)])
            values = split(kv_ref[side, :, pl.ds(width + start, lanes)])
            scores = lax.dot_general(
                query, keys, (((1,), (1,)), ((), ())), preferred_element_type=jnp.float32
            )
            probs = jnp.concatenate([soft(scores[:, :tokv]), soft(scores[:, tokv:])], axis=1)
            ctx_ref[side, :, pl.ds(start, lanes)] = jnp.dot(
                probs, values, preferred_element_type=jnp.float32
            ).astype(jnp.bfloat16)
        return carry

    for i in range(HEADS // 2):
        two_heads(i, 0)
    for side in range(2):
        updated = emb_ref[side].astype(jnp.float32) + jnp.dot(
            ctx_ref[side], wo[side], preferred_element_type=jnp.float32
        )
        final = (normed(updated) * gains_ref[side, 2:3, :]).astype(jnp.bfloat16)
        head = lax.dot_general(
            whead_ref[side], final, (((1,), (1,)), ((), ())), preferred_element_type=jnp.float32
        )
        conf = 1.0 + jnp.exp(head[3:4, :])
        out_ref[side, 0:3, :] = head[0:3, :] * conf
        out_ref[side, 3:4, :] = conf


def load(*weights):
    return pl.pallas_call(
        load_kernel,
        out_shape=[jax.ShapeDtypeStruct(w.shape, w.dtype) for w in weights],
        in_specs=[HBM] * len(weights),
        out_specs=[VMEM] * len(weights),
        scratch_shapes=[pltpu.SemaphoreType.DMA((len(weights),))],
        compiler_params=pltpu.CompilerParams(vmem_limit_bytes=50 * 1024 * 1024),
        name="load",
    )(*weights)


def embed(parts, cuts, me, w_embed, pieces):
    views, rows, feat = pieces[0].shape
    full, width = w_embed.shape
    return pl.pallas_call(
        functools.partial(embed_kernel, parts, cuts),
        out_shape=[
            jax.ShapeDtypeStruct((views, size, width), jnp.bfloat16)
            for size in [size for _, size in cuts] + [rows]
        ],
        in_specs=[SMEM, VMEM] + [HBM] * parts,
        out_specs=[HBM] * (len(cuts) + 1),
        scratch_shapes=[
            pltpu.VMEM((views, rows, full), jnp.bfloat16),
            pltpu.VMEM((views, rows, width), jnp.bfloat16),
            pltpu.SemaphoreType.DMA((parts,)),
            pltpu.SemaphoreType.DMA((len(cuts) + 1,)),
        ],
        compiler_params=pltpu.CompilerParams(vmem_limit_bytes=16 * 1024 * 1024),
        cost_estimate=pl.CostEstimate(
            flops=2 * views * rows * full * width,
            bytes_accessed=2 * (full * width + 2 * views * rows * full),
            transcendentals=0,
        ),
        name="embed",
    )(me, w_embed, *pieces)


def pick(lanes, slots, cap, me, line, wants, own, below, above):
    views, size, width = own.shape
    reach = len(below)
    return pl.pallas_call(
        functools.partial(pick_kernel, lanes, reach, slots, cap),
        out_shape=[jax.ShapeDtypeStruct((len(slots), cap, size, width), jnp.bfloat16)] * lanes,
        in_specs=[SMEM, SMEM, SMEM] + [HBM] * (1 + 2 * reach),
        out_specs=[HBM] * lanes,
        scratch_shapes=[
            pltpu.VMEM((len(slots), views, size, width), jnp.bfloat16),
            pltpu.SemaphoreType.DMA((len(slots),)),
            pltpu.SemaphoreType.DMA((lanes * len(slots) * cap,)),
        ],
        compiler_params=pltpu.CompilerParams(vmem_limit_bytes=16 * 1024 * 1024),
        cost_estimate=pl.CostEstimate(
            flops=0,
            bytes_accessed=4 * lanes * len(slots) * cap * size * width,
            transcendentals=0,
        ),
        name="pick",
    )(me, line, wants, own, *below, *above)


def route(lanes, parts, cap, cuts, groups, me, line, sides, fetched):
    width = fetched[0].shape[-1]
    size = sum(size for _, size in cuts)
    base = cuts[0][0]
    cuts = tuple((first - base, each) for first, each in cuts)
    copies = len(cuts) * sum(len(group) for group in groups) * lanes * cap
    return pl.pallas_call(
        functools.partial(route_kernel, lanes, parts, cap, base, cuts, groups),
        out_shape=[jax.ShapeDtypeStruct((2, size, width), jnp.bfloat16)] * parts,
        in_specs=[SMEM, SMEM, SMEM] + [HBM] * len(fetched),
        out_specs=[HBM] * parts,
        scratch_shapes=[
            pltpu.VMEM((2 * parts, size, width), jnp.bfloat16),
            pltpu.SemaphoreType.DMA((copies,)),
            pltpu.SemaphoreType.DMA((parts,)),
        ],
        compiler_params=pltpu.CompilerParams(vmem_limit_bytes=16 * 1024 * 1024),
        cost_estimate=pl.CostEstimate(
            flops=0, bytes_accessed=8 * parts * size * width, transcendentals=0
        ),
        name="route",
    )(me, line, sides, *fetched)


def decode(parts, cuts, me, gains, w_head, w_query, w_keyval, w_out, pieces):
    width = pieces[0].shape[2]
    tokv = parts * sum(size for _, size in cuts)
    flops = 2 * 2 * tokv * width * (5 * width + 2 * tokv)
    return pl.pallas_call(
        functools.partial(decode_kernel, parts, cuts),
        out_shape=jax.ShapeDtypeStruct((2, 4, tokv), jnp.float32),
        in_specs=[SMEM, VMEM, VMEM, VMEM, VMEM, VMEM] + [HBM] * (parts * len(cuts)),
        out_specs=VMEM,
        scratch_shapes=[
            pltpu.VMEM((2, tokv, width), jnp.bfloat16),
            pltpu.VMEM((2, tokv, width), jnp.bfloat16),
            pltpu.VMEM((2, tokv, width), jnp.bfloat16),
            pltpu.VMEM((2, tokv, width), jnp.bfloat16),
            pltpu.VMEM((2, tokv, 2 * width), jnp.bfloat16),
            pltpu.VMEM((2, tokv, width), jnp.bfloat16),
            pltpu.SemaphoreType.DMA((parts * len(cuts),)),
        ],
        compiler_params=pltpu.CompilerParams(vmem_limit_bytes=40 * 1024 * 1024),
        cost_estimate=pl.CostEstimate(
            flops=flops, bytes_accessed=20 * width * width, transcendentals=2 * HEADS * tokv * tokv
        ),
        name="decode",
    )(me, gains, w_head, w_keyval, w_query, w_out, *pieces)


def on_device(tokens, pairs, w_embed, w_query, w_keyval, w_out, w_head, gains):
    count = lax.axis_size("view")
    parts = lax.axis_size("mp")
    row = lax.axis_index("view")
    column = lax.axis_index("mp")
    me = jnp.stack([row, column]).astype(jnp.int32)
    view_dev, tokv, feat = tokens.shape
    rows = tokv // parts
    block_pairs = pairs.shape[0]
    pair_dev = block_pairs // parts
    side_count = 2 * block_pairs
    cap = max(2, (side_count + count - 1) // count)
    slot_total = count * cap
    lanes = 1 << ((count.bit_length() - 1) // 2)
    length = count // lanes
    cuts = ((0, rows // 2), (rows // 2, rows // 2)) if rows % 32 == 0 else ((0, rows),)

    pieces = []
    for j in range(parts):
        piece = lax.dynamic_slice_in_dim(tokens, (column ^ j) * rows, rows, axis=1)
        pieces.append(lax.ppermute(piece, "mp", xor_pairs(parts, j)) if j else piece)

    pairs, pieces[1] = lax.optimization_barrier((pairs, pieces[1]))
    side_views = pairs.reshape(side_count)
    owners = side_views // view_dev
    local_ids = side_views % view_dev
    positions = jnp.arange(side_count, dtype=jnp.int32)
    same_owner = owners[:, None] == owners[None, :]
    slot_rank = jnp.sum(
        jnp.logical_and(same_owner, positions[None, :] < positions[:, None]), axis=1
    )
    slot_index = owners * cap + slot_rank
    slot_match = jnp.arange(slot_total, dtype=jnp.int32)[:, None] == slot_index[None, :]
    wanted = jnp.sum(jnp.where(slot_match, local_ids[None, :], 0), axis=1)
    used = jnp.any(slot_match, axis=1)
    slot_side = jnp.where(used, jnp.sum(jnp.where(slot_match, positions[None, :], 0), axis=1), -1)
    slot_side = slot_side.astype(jnp.int32)
    wanted = jnp.where(used, wanted, -1).astype(jnp.int32)
    wants = jnp.concatenate(
        [lax.ppermute(wanted, "view", xor_pairs(count, j)) if j else wanted for j in range(lanes)]
    )
    nearest = [sorted(range(length), key=lambda at: (abs(at - z), at)) for z in range(length)]
    line = jnp.asarray(nearest, jnp.int32)[row // lanes]

    weights = load(w_embed, w_query, w_keyval, w_out)
    pieces, weights = lax.optimization_barrier((pieces, weights))
    w_embed, w_query, w_keyval, w_out = weights
    *embedded, whole = embed(parts, cuts, me, w_embed, pieces)
    embedded, wants = lax.optimization_barrier((embedded, wants))
    groups = ((0,), tuple(range(1, length - 1)), (length - 1,))

    def swap(picked):
        return [
            lax.ppermute(picked[j], "view", xor_pairs(count, j)) if j else picked[j]
            for j in range(lanes)
        ]

    shared = pick(lanes, groups[0], cap, me, line, wants, whole, [], [])
    below, above = [[] for _ in cuts], [[] for _ in cuts]
    for p in range(1, length):
        up = [
            (z * lanes + y, (z + 1) * lanes + y) for z in range(p - 1, length - 1) for y in range(lanes)
        ]
        down = [
            (z * lanes + y, (z - 1) * lanes + y) for z in range(1, length - p + 1) for y in range(lanes)
        ]
        for q in range(len(cuts)):
            below[q].append(lax.ppermute((below[q] or [embedded[q]])[-1], "view", up))
            above[q].append(lax.ppermute((above[q] or [embedded[q]])[-1], "view", down))
        if p == 1:
            below[0], above[0], shared = lax.optimization_barrier((below[0], above[0], shared))
            shared = swap(shared)
        if p == 2:
            below[0], above[0], shared = lax.optimization_barrier((below[0], above[0], shared))
    fetched, picked_last = [], None
    for q in range(len(cuts)):
        picked = [
            pick(
                lanes,
                group,
                cap,
                me,
                line,
                wants,
                embedded[q],
                below[q][: group[-1]],
                above[q][: group[-1]],
            )
            for group in groups[1:]
        ]
        if picked_last is not None:
            picked[0], picked_last = lax.optimization_barrier((picked[0], picked_last))
        picked_last = picked[-1]
        fetched.append(shared + [each for group in picked for each in swap(group)])
    slot_pair = slot_side // 2
    results, arrived = [], None
    for c in range(pair_dev):
        mine = jnp.logical_and(slot_side >= 0, slot_pair % pair_dev == c)
        place = jnp.where(mine, 2 * (slot_pair // pair_dev) + slot_side % 2, -1).astype(jnp.int32)
        steps = [(cut,) for cut in cuts] if c == 0 else [cuts]
        parcels = []
        for q, step in enumerate(steps):
            wave = fetched[q : q + 1] if c == 0 else fetched
            parcels += route(
                lanes, parts, cap, step, groups, me, line, place, [each for g in wave for each in g]
            )
        if c:
            parcels, arrived = lax.optimization_barrier((parcels, arrived))
        arrived = [
            lax.ppermute(parcel, "mp", xor_pairs(parts, i % parts)) if i % parts else parcel
            for i, parcel in enumerate(parcels)
        ]
        results.append(
            decode(
                parts,
                cuts if c == 0 else ((0, rows),),
                me,
                gains,
                w_head,
                w_query,
                w_keyval,
                w_out,
                arrived,
            )
        )
    results = jnp.stack(results)

    every = lax.all_gather(results, "mp", axis=0, tiled=True).reshape(side_count, 4 * tokv)
    slotted = jnp.dot(slot_match.astype(jnp.float32), every, precision=lax.Precision.HIGHEST)
    tags = jnp.broadcast_to(wanted.astype(jnp.float32)[:, None], (slot_total, 128))
    slotted = jnp.concatenate([slotted, tags], axis=1).reshape(count, cap, 4 * tokv + 128)
    returned = lax.all_to_all(slotted, "view", split_axis=0, concat_axis=0, tiled=True)
    picker = returned[:, :, 4 * tokv :][:, :, :1] == jnp.arange(view_dev, dtype=jnp.float32)
    summed = jnp.einsum(
        "rcv,rcx->vx",
        picker.astype(jnp.float32),
        returned[:, :, : 4 * tokv],
        precision=lax.Precision.HIGHEST,
    )
    return summed.reshape(view_dev, 4, tokv)


def solution(mesh):
    return jax.shard_map(
        on_device,
        mesh=mesh,
        in_specs=(P("view", None, "mp"), P("view", None), P(), P(), P(), P(), P(), P()),
        out_specs=P("view", None, None),
        check_vma=False,
    )
```

```python
import functools

import jax
import jax.numpy as jnp
from jax import lax
from jax.experimental import pallas as pl
from jax.experimental.pallas import tpu as pltpu
from jax.sharding import PartitionSpec as P

HEADS = 12
EPS = 1e-06
LOG2_E = 1.4426950408889634
HBM = pl.BlockSpec(memory_space=pltpu.HBM)
SMEM = pl.BlockSpec(memory_space=pltpu.SMEM)
VMEM = pl.BlockSpec(memory_space=pltpu.VMEM)


def xor_pairs(count, step):
    return [(i, i ^ step) for i in range(count)]


def load_kernel(*refs):
    count = len(refs) // 2
    copies = [pltpu.make_async_copy(refs[i], refs[count + i], refs[-1].at[i]) for i in range(count)]
    for copy in copies:
        copy.start()
    for copy in copies:
        copy.wait()


def embed_kernel(parts, cuts, me_ref, w_vmem, *refs):
    pieces, outs, whole = refs[:parts], refs[parts : parts + len(cuts)], refs[parts + len(cuts)]
    x_ref, emb_ref, in_sem, out_sem = refs[parts + len(cuts) + 1 :]
    views, _, feat = pieces[0].shape
    width = w_vmem.shape[1]
    column = me_ref[1]
    copies = []
    for j in range(parts):
        start = pl.multiple_of((column ^ j) * feat, feat)
        copies.append(
            pltpu.make_async_copy(pieces[j], x_ref.at[:, :, pl.ds(start, feat)], in_sem.at[j])
        )
        copies[-1].start()
    for copy in copies:
        copy.wait()
    copies = []
    for q, (first, size) in enumerate(cuts):
        emb = jnp.dot(
            x_ref[:, first : first + size, :].reshape(views * size, parts * feat),
            w_vmem[...],
            preferred_element_type=jnp.float32,
        )
        emb_ref[:, first : first + size, :] = emb.astype(jnp.bfloat16).reshape(views, size, width)
        copies.append(
            pltpu.make_async_copy(
                emb_ref.at[:, pl.ds(first, size), :], outs[q], out_sem.at[q]
            )
        )
        copies[-1].start()
    copies.append(pltpu.make_async_copy(emb_ref, whole, out_sem.at[len(cuts)]))
    copies[-1].start()
    for copy in copies:
        copy.wait()


def pick_kernel(lanes, reach, slots, cap, me_ref, line_ref, want_ref, *refs):
    count = 1 + 2 * reach
    own, below, above = refs[0], refs[1 : 1 + reach], refs[1 + reach : count]
    outs = refs[count : count + lanes]
    stage_ref, in_sem, out_sem = refs[count + lanes :]
    place, lane = me_ref[0] // lanes, me_ref[0] % lanes
    rows = line_ref.shape[0] * lanes

    def sources(act):
        for n, i in enumerate(slots):
            at = line_ref[i]
            if i == 0:
                act(pltpu.make_async_copy(own, stage_ref.at[n], in_sem.at[n]))
            for p in range(1, i + 1):
                for want, source in ((place - p, below[p - 1]), (place + p, above[p - 1])):

                    @pl.when(at == want)
                    def _():
                        act(pltpu.make_async_copy(source, stage_ref.at[n], in_sem.at[n]))

    sources(lambda copy: copy.start())
    sources(lambda copy: copy.wait())
    copies = []
    for j in range(lanes):
        for n, i in enumerate(slots):
            for c in range(cap):
                view = want_ref[(j * rows + line_ref[i] * lanes + lane) * cap + c]
                copies.append(
                    pltpu.make_async_copy(
                        stage_ref.at[n, jnp.maximum(view, 0)], outs[j].at[n, c], out_sem.at[len(copies)]
                    )
                )
                copies[-1].start()
    for copy in copies:
        copy.wait()


def route_kernel(lanes, parts, cap, base, cuts, groups, me_ref, line_ref, side_ref, *refs):
    count = len(cuts) * len(groups) * lanes
    fetched, outs = refs[:count], refs[count : count + parts]
    stage_ref, in_sem, out_sem = refs[count + parts :]
    lane, column = me_ref[0] % lanes, me_ref[1]

    def slots(act):
        number = 0
        for q, (first, size) in enumerate(cuts):
            for g, group in enumerate(groups):
                for j in range(lanes):
                    source = fetched[(q * len(groups) + g) * lanes + j]
                    for n, i in enumerate(group):
                        for c in range(cap):
                            side = side_ref[(line_ref[i] * lanes + (lane ^ j)) * cap + c]
                            part = source.at[n, c]
                            if source.shape[2] > size:
                                part = source.at[n, c, pl.ds(base + first, size)]

                            @pl.when(side >= 0)
                            def _():
                                act(
                                    pltpu.make_async_copy(
                                        part,
                                        stage_ref.at[side, pl.ds(first, size), :],
                                        in_sem.at[number],
                                    )
                                )

                            number += 1

    slots(lambda copy: copy.start())
    slots(lambda copy: copy.wait())
    copies = []
    for j in range(parts):
        copies.append(
            pltpu.make_async_copy(
                stage_ref.at[pl.ds(2 * (column ^ j), 2)], outs[j], out_sem.at[j]
            )
        )
        copies[-1].start()
    for copy in copies:
        copy.wait()


def normed(values):
    mean = jnp.mean(values, axis=-1, keepdims=True)
    centred = values - mean
    var = jnp.mean(centred * centred, axis=-1, keepdims=True)
    return centred * lax.rsqrt(var + EPS)


def decode_kernel(parts, cuts, me_ref, gains_ref, whead_ref, wkv, wq, wo, *refs):
    pieces, out_ref = refs[: parts * len(cuts)], refs[parts * len(cuts)]
    scratch = refs[parts * len(cuts) + 1 :]
    emb_ref, qin_ref, min_ref, q_ref, kv_ref, ctx_ref, sem = scratch
    tokv, width = emb_ref.shape[1:]
    rows = tokv // parts
    column = me_ref[1]
    copies = []
    for q, (first, size) in enumerate(cuts):
        for j in range(parts):
            i = q * parts + j
            start = pl.multiple_of((column ^ j) * rows + first, size)
            copies.append(
                pltpu.make_async_copy(pieces[i], emb_ref.at[:, pl.ds(start, size), :], sem.at[i])
            )
            copies[-1].start()
    for copy in copies:
        copy.wait()
    for side in range(2):
        xhat = normed(emb_ref[side].astype(jnp.float32))
        qin_ref[side] = (xhat * gains_ref[side, 0:1, :]).astype(jnp.bfloat16)
        min_ref[1 - side] = (xhat * gains_ref[1 - side, 1:2, :]).astype(jnp.bfloat16)
    for side in range(2):
        q_ref[side] = jnp.dot(
            qin_ref[side], wq[side], preferred_element_type=jnp.float32
        ).astype(jnp.bfloat16)
    for side in range(2):
        kv_ref[side] = jnp.dot(
            min_ref[side], wkv[side], preferred_element_type=jnp.float32
        ).astype(jnp.bfloat16)

    head_size = width // HEADS
    lanes = 2 * head_size
    low = lax.broadcasted_iota(jnp.int32, (tokv, lanes), 1) < head_size

    def split(values):
        zero = jnp.zeros_like(values)
        return jnp.concatenate([jnp.where(low, values, zero), jnp.where(low, zero, values)], axis=0)

    def soft(scores):
        top = jnp.max(scores, axis=-1, keepdims=True)
        e = jnp.exp2((scores - top) * (LOG2_E / head_size**0.5))
        return (e * (1.0 / jnp.sum(e, axis=-1, keepdims=True))).astype(jnp.bfloat16)

    def two_heads(i, carry):
        start = pl.multiple_of(i * lanes, lanes)
        for side in range(2):
            query = q_ref[side, :, pl.ds(start, lanes)]
            keys = split(kv_ref[side, :, pl.ds(start, lanes)])
            values = split(kv_ref[side, :, pl.ds(width + start, lanes)])
            scores = lax.dot_general(
                query, keys, (((1,), (1,)), ((), ())), preferred_element_type=jnp.float32
            )
            probs = jnp.concatenate([soft(scores[:, :tokv]), soft(scores[:, tokv:])], axis=1)
            ctx_ref[side, :, pl.ds(start, lanes)] = jnp.dot(
                probs, values, preferred_element_type=jnp.float32
            ).astype(jnp.bfloat16)
        return carry

    for i in range(HEADS // 2):
        two_heads(i, 0)
    for side in range(2):
        updated = emb_ref[side].astype(jnp.float32) + jnp.dot(
            ctx_ref[side], wo[side], preferred_element_type=jnp.float32
        )
        final = (normed(updated) * gains_ref[side, 2:3, :]).astype(jnp.bfloat16)
        head = lax.dot_general(
            whead_ref[side], final, (((1,), (1,)), ((), ())), preferred_element_type=jnp.float32
        )
        conf = 1.0 + jnp.exp(head[3:4, :])
        out_ref[side, 0:3, :] = head[0:3, :] * conf
        out_ref[side, 3:4, :] = conf


def load(*weights):
    return pl.pallas_call(
        load_kernel,
        out_shape=[jax.ShapeDtypeStruct(w.shape, w.dtype) for w in weights],
        in_specs=[HBM] * len(weights),
        out_specs=[VMEM] * len(weights),
        scratch_shapes=[pltpu.SemaphoreType.DMA((len(weights),))],
        compiler_params=pltpu.CompilerParams(vmem_limit_bytes=50 * 1024 * 1024),
        name="load",
    )(*weights)


def embed(parts, cuts, me, w_embed, pieces):
    views, rows, _ = pieces[0].shape
    full, width = w_embed.shape
    return pl.pallas_call(
        functools.partial(embed_kernel, parts, cuts),
        out_shape=[
            jax.ShapeDtypeStruct((views, size, width), jnp.bfloat16)
            for size in [size for _, size in cuts] + [rows]
        ],
        in_specs=[SMEM, VMEM] + [HBM] * parts,
        out_specs=[HBM] * (len(cuts) + 1),
        scratch_shapes=[
            pltpu.VMEM((views, rows, full), jnp.bfloat16),
            pltpu.VMEM((views, rows, width), jnp.bfloat16),
            pltpu.SemaphoreType.DMA((parts,)),
            pltpu.SemaphoreType.DMA((len(cuts) + 1,)),
        ],
        compiler_params=pltpu.CompilerParams(vmem_limit_bytes=16 * 1024 * 1024),
        cost_estimate=pl.CostEstimate(
            flops=2 * views * rows * full * width,
            bytes_accessed=2 * (full * width + 2 * views * rows * full),
            transcendentals=0,
        ),
        name="embed",
    )(me, w_embed, *pieces)


def pick(lanes, slots, cap, me, line, wants, own, below, above):
    views, size, width = own.shape
    reach = len(below)
    return pl.pallas_call(
        functools.partial(pick_kernel, lanes, reach, slots, cap),
        out_shape=[jax.ShapeDtypeStruct((len(slots), cap, size, width), jnp.bfloat16)] * lanes,
        in_specs=[SMEM, SMEM, SMEM] + [HBM] * (1 + 2 * reach),
        out_specs=[HBM] * lanes,
        scratch_shapes=[
            pltpu.VMEM((len(slots), views, size, width), jnp.bfloat16),
            pltpu.SemaphoreType.DMA((len(slots),)),
            pltpu.SemaphoreType.DMA((lanes * len(slots) * cap,)),
        ],
        compiler_params=pltpu.CompilerParams(vmem_limit_bytes=16 * 1024 * 1024),
        cost_estimate=pl.CostEstimate(
            flops=0,
            bytes_accessed=4 * lanes * len(slots) * cap * size * width,
            transcendentals=0,
        ),
        name="pick",
    )(me, line, wants, own, *below, *above)


def route(lanes, parts, cap, cuts, groups, me, line, sides, fetched):
    width = fetched[0].shape[-1]
    size = sum(size for _, size in cuts)
    base = cuts[0][0]
    cuts = tuple((first - base, each) for first, each in cuts)
    copies = len(cuts) * sum(len(group) for group in groups) * lanes * cap
    return pl.pallas_call(
        functools.partial(route_kernel, lanes, parts, cap, base, cuts, groups),
        out_shape=[jax.ShapeDtypeStruct((2, size, width), jnp.bfloat16)] * parts,
        in_specs=[SMEM, SMEM, SMEM] + [HBM] * len(fetched),
        out_specs=[HBM] * parts,
        scratch_shapes=[
            pltpu.VMEM((2 * parts, size, width), jnp.bfloat16),
            pltpu.SemaphoreType.DMA((copies,)),
            pltpu.SemaphoreType.DMA((parts,)),
        ],
        compiler_params=pltpu.CompilerParams(vmem_limit_bytes=16 * 1024 * 1024),
        cost_estimate=pl.CostEstimate(
            flops=0, bytes_accessed=8 * parts * size * width, transcendentals=0
        ),
        name="route",
    )(me, line, sides, *fetched)


def decode(parts, cuts, me, gains, w_head, w_query, w_keyval, w_out, pieces):
    width = pieces[0].shape[2]
    tokv = parts * sum(size for _, size in cuts)
    flops = 2 * 2 * tokv * width * (5 * width + 2 * tokv)
    return pl.pallas_call(
        functools.partial(decode_kernel, parts, cuts),
        out_shape=jax.ShapeDtypeStruct((2, 4, tokv), jnp.float32),
        in_specs=[SMEM, VMEM, VMEM, VMEM, VMEM, VMEM] + [HBM] * (parts * len(cuts)),
        out_specs=VMEM,
        scratch_shapes=[
            pltpu.VMEM((2, tokv, width), jnp.bfloat16),
            pltpu.VMEM((2, tokv, width), jnp.bfloat16),
            pltpu.VMEM((2, tokv, width), jnp.bfloat16),
            pltpu.VMEM((2, tokv, width), jnp.bfloat16),
            pltpu.VMEM((2, tokv, 2 * width), jnp.bfloat16),
            pltpu.VMEM((2, tokv, width), jnp.bfloat16),
            pltpu.SemaphoreType.DMA((parts * len(cuts),)),
        ],
        compiler_params=pltpu.CompilerParams(vmem_limit_bytes=40 * 1024 * 1024),
        cost_estimate=pl.CostEstimate(
            flops=flops, bytes_accessed=20 * width * width, transcendentals=2 * HEADS * tokv * tokv
        ),
        name="decode",
    )(me, gains, w_head, w_keyval, w_query, w_out, *pieces)


def on_device(tokens, pairs, w_embed, w_query, w_keyval, w_out, w_head, gains):
    count = lax.axis_size("view")
    parts = lax.axis_size("mp")
    row = lax.axis_index("view")
    column = lax.axis_index("mp")
    me = jnp.stack([row, column]).astype(jnp.int32)
    view_dev, tokv, _ = tokens.shape
    rows = tokv // parts
    block_pairs = pairs.shape[0]
    pair_dev = block_pairs // parts
    side_count = 2 * block_pairs
    cap = max(2, (side_count + count - 1) // count)
    slot_total = count * cap
    lanes = 1 << ((count.bit_length() - 1) // 2)
    length = count // lanes
    cuts = ((0, rows // 2), (rows // 2, rows // 2)) if rows % 32 == 0 else ((0, rows),)

    pieces = []
    for j in range(parts):
        piece = lax.dynamic_slice_in_dim(tokens, (column ^ j) * rows, rows, axis=1)
        pieces.append(lax.ppermute(piece, "mp", xor_pairs(parts, j)) if j else piece)

    pairs, pieces[1] = lax.optimization_barrier((pairs, pieces[1]))
    side_views = pairs.reshape(side_count)
    owners = side_views // view_dev
    local_ids = side_views % view_dev
    positions = jnp.arange(side_count, dtype=jnp.int32)
    same_owner = owners[:, None] == owners[None, :]
    slot_rank = jnp.sum(
        jnp.logical_and(same_owner, positions[None, :] < positions[:, None]), axis=1
    )
    slot_index = owners * cap + slot_rank
    slot_match = jnp.arange(slot_total, dtype=jnp.int32)[:, None] == slot_index[None, :]
    wanted = jnp.sum(jnp.where(slot_match, local_ids[None, :], 0), axis=1)
    used = jnp.any(slot_match, axis=1)
    slot_side = jnp.where(used, jnp.sum(jnp.where(slot_match, positions[None, :], 0), axis=1), -1)
    slot_side = slot_side.astype(jnp.int32)
    wanted = jnp.where(used, wanted, -1).astype(jnp.int32)
    wants = jnp.concatenate(
        [lax.ppermute(wanted, "view", xor_pairs(count, j)) if j else wanted for j in range(lanes)]
    )
    nearest = [sorted(range(length), key=lambda at: (abs(at - z), at)) for z in range(length)]
    line = jnp.asarray(nearest, jnp.int32)[row // lanes]

    weights = load(w_embed, w_query, w_keyval, w_out)
    pieces, weights = lax.optimization_barrier((pieces, weights))
    w_embed, w_query, w_keyval, w_out = weights
    *embedded, whole = embed(parts, cuts, me, w_embed, pieces)
    embedded, wants = lax.optimization_barrier((embedded, wants))
    groups = ((0,), tuple(range(1, length - 1)), (length - 1,))

    def swap(picked):
        return [
            lax.ppermute(picked[j], "view", xor_pairs(count, j)) if j else picked[j]
            for j in range(lanes)
        ]

    shared = pick(lanes, groups[0], cap, me, line, wants, whole, [], [])
    below, above = [[] for _ in cuts], [[] for _ in cuts]
    for p in range(1, length):
        up = [
            (z * lanes + y, (z + 1) * lanes + y) for z in range(p - 1, length - 1) for y in range(lanes)
        ]
        down = [
            (z * lanes + y, (z - 1) * lanes + y) for z in range(1, length - p + 1) for y in range(lanes)
        ]
        for q in range(len(cuts)):
            below[q].append(lax.ppermute((below[q] or [embedded[q]])[-1], "view", up))
            above[q].append(lax.ppermute((above[q] or [embedded[q]])[-1], "view", down))
        if p == 1:
            below[0], above[0], shared = lax.optimization_barrier((below[0], above[0], shared))
            shared = swap(shared)
        if p == 2:
            below[0], above[0], shared = lax.optimization_barrier((below[0], above[0], shared))
    fetched = []
    for q in range(len(cuts)):
        picked = [
            pick(
                lanes,
                group,
                cap,
                me,
                line,
                wants,
                embedded[q],
                below[q][: group[-1]],
                above[q][: group[-1]],
            )
            for group in groups[1:]
        ]
        fetched.append(list(shared))
        for group in picked:
            fetched[-1] += swap(group)
    slot_pair = slot_side // 2
    results, arrived = [], None
    for c in range(pair_dev):
        mine = jnp.logical_and(slot_side >= 0, slot_pair % pair_dev == c)
        place = jnp.where(mine, 2 * (slot_pair // pair_dev) + slot_side % 2, -1).astype(jnp.int32)
        steps = [(cut,) for cut in cuts] if c == 0 else [cuts]
        parcels = []
        for q, step in enumerate(steps):
            wave = fetched[q : q + 1] if c == 0 else fetched
            parcels += route(
                lanes, parts, cap, step, groups, me, line, place, [each for g in wave for each in g]
            )
        if c:
            parcels, arrived = lax.optimization_barrier((parcels, arrived))
        arrived = [
            lax.ppermute(parcel, "mp", xor_pairs(parts, i % parts)) if i % parts else parcel
            for i, parcel in enumerate(parcels)
        ]
        results.append(
            decode(
                parts,
                cuts if c == 0 else ((0, rows),),
                me,
                gains,
                w_head,
                w_query,
                w_keyval,
                w_out,
                arrived,
            )
        )
    results = jnp.stack(results)

    every = lax.all_gather(results, "mp", axis=0, tiled=True).reshape(side_count, 4 * tokv)
    slotted = jnp.dot(slot_match.astype(jnp.float32), every, precision=lax.Precision.HIGHEST)
    tags = jnp.broadcast_to(wanted.astype(jnp.float32)[:, None], (slot_total, 128))
    slotted = jnp.concatenate([slotted, tags], axis=1).reshape(count, cap, 4 * tokv + 128)
    returned = lax.all_to_all(slotted, "view", split_axis=0, concat_axis=0, tiled=True)
    picker = returned[:, :, 4 * tokv :][:, :, :1] == jnp.arange(view_dev, dtype=jnp.float32)
    summed = jnp.einsum(
        "rcv,rcx->vx",
        picker.astype(jnp.float32),
        returned[:, :, : 4 * tokv],
        precision=lax.Precision.HIGHEST,
    )
    return summed.reshape(view_dev, 4, tokv)


def solution(mesh):
    return jax.shard_map(
        on_device,
        mesh=mesh,
        in_specs=(P("view", None, "mp"), P("view", None), P(), P(), P(), P(), P(), P()),
        out_specs=P("view", None, None),
        check_vma=False,
    )
```

```python
import functools

import jax
import jax.numpy as jnp
from jax import lax
from jax.experimental import pallas as pl
from jax.experimental.pallas import tpu as pltpu
from jax.sharding import PartitionSpec as P

HEADS = 12
EPS = 1e-06
LOG2_E = 1.4426950408889634
HBM = pl.BlockSpec(memory_space=pltpu.HBM)
SMEM = pl.BlockSpec(memory_space=pltpu.SMEM)
VMEM = pl.BlockSpec(memory_space=pltpu.VMEM)


def xor_pairs(count, step):
    return [(i, i ^ step) for i in range(count)]


def load_kernel(*refs):
    count = len(refs) // 2
    copies = [pltpu.make_async_copy(refs[i], refs[count + i], refs[-1].at[i]) for i in range(count)]
    for copy in copies:
        copy.start()
    for copy in copies:
        copy.wait()


def embed_kernel(parts, cuts, me_ref, w_vmem, *refs):
    pieces, outs, whole = refs[:parts], refs[parts : parts + len(cuts)], refs[parts + len(cuts)]
    x_ref, emb_ref, in_sem, out_sem = refs[parts + len(cuts) + 1 :]
    views, _, feat = pieces[0].shape
    width = w_vmem.shape[1]
    column = me_ref[1]
    copies = []
    for j in range(parts):
        start = pl.multiple_of((column ^ j) * feat, feat)
        copies.append(
            pltpu.make_async_copy(pieces[j], x_ref.at[:, :, pl.ds(start, feat)], in_sem.at[j])
        )
        copies[-1].start()
    for copy in copies:
        copy.wait()
    copies = []
    for q, (first, size) in enumerate(cuts):
        emb = jnp.dot(
            x_ref[:, first : first + size, :].reshape(views * size, parts * feat),
            w_vmem[...],
            preferred_element_type=jnp.float32,
        )
        emb_ref[:, first : first + size, :] = emb.astype(jnp.bfloat16).reshape(views, size, width)
        copies.append(
            pltpu.make_async_copy(
                emb_ref.at[:, pl.ds(first, size), :], outs[q], out_sem.at[q]
            )
        )
        copies[-1].start()
    copies.append(pltpu.make_async_copy(emb_ref, whole, out_sem.at[len(cuts)]))
    copies[-1].start()
    for copy in copies:
        copy.wait()


def pick_kernel(lanes, reach, slots, cap, me_ref, line_ref, want_ref, *refs):
    count = 1 + 2 * reach
    own, below, above = refs[0], refs[1 : 1 + reach], refs[1 + reach : count]
    outs = refs[count : count + lanes]
    stage_ref, in_sem, out_sem = refs[count + lanes :]
    place, lane = me_ref[0] // lanes, me_ref[0] % lanes
    rows = line_ref.shape[0] * lanes

    def sources(act):
        for n, i in enumerate(slots):
            at = line_ref[i]
            if i == 0:
                act(pltpu.make_async_copy(own, stage_ref.at[n], in_sem.at[n]))
            for p in range(1, i + 1):
                for want, source in ((place - p, below[p - 1]), (place + p, above[p - 1])):

                    @pl.when(at == want)
                    def _():
                        act(pltpu.make_async_copy(source, stage_ref.at[n], in_sem.at[n]))

    sources(lambda copy: copy.start())
    sources(lambda copy: copy.wait())
    copies = []
    for j in range(lanes):
        for n, i in enumerate(slots):
            for c in range(cap):
                view = want_ref[(j * rows + line_ref[i] * lanes + lane) * cap + c]
                copies.append(
                    pltpu.make_async_copy(
                        stage_ref.at[n, jnp.maximum(view, 0)], outs[j].at[n, c], out_sem.at[len(copies)]
                    )
                )
                copies[-1].start()
    for copy in copies:
        copy.wait()


def route_kernel(lanes, parts, cap, base, cuts, groups, me_ref, line_ref, side_ref, *refs):
    count = len(cuts) * len(groups) * lanes
    fetched, outs = refs[:count], refs[count : count + parts]
    stage_ref, in_sem, out_sem = refs[count + parts :]
    lane, column = me_ref[0] % lanes, me_ref[1]

    def slots(act):
        number = 0
        for q, (first, size) in enumerate(cuts):
            for g, group in enumerate(groups):
                for j in range(lanes):
                    source = fetched[(q * len(groups) + g) * lanes + j]
                    for n, i in enumerate(group):
                        for c in range(cap):
                            side = side_ref[(line_ref[i] * lanes + (lane ^ j)) * cap + c]
                            part = source.at[n, c]
                            if source.shape[2] > size:
                                part = source.at[n, c, pl.ds(base + first, size)]

                            @pl.when(side >= 0)
                            def _():
                                act(
                                    pltpu.make_async_copy(
                                        part,
                                        stage_ref.at[side, pl.ds(first, size), :],
                                        in_sem.at[number],
                                    )
                                )

                            number += 1

    slots(lambda copy: copy.start())
    slots(lambda copy: copy.wait())
    copies = []
    for j in range(parts):
        copies.append(
            pltpu.make_async_copy(
                stage_ref.at[pl.ds(2 * (column ^ j), 2)], outs[j], out_sem.at[j]
            )
        )
        copies[-1].start()
    for copy in copies:
        copy.wait()


def normed(values):
    mean = jnp.mean(values, axis=-1, keepdims=True)
    centred = values - mean
    var = jnp.mean(centred * centred, axis=-1, keepdims=True)
    return centred * lax.rsqrt(var + EPS)


def decode_kernel(parts, cuts, me_ref, gains_ref, whead_ref, wkv, wq, wo, *refs):
    pieces, out_ref = refs[: parts * len(cuts)], refs[parts * len(cuts)]
    scratch = refs[parts * len(cuts) + 1 :]
    emb_ref, qin_ref, min_ref, q_ref, kv_ref, ctx_ref, sem = scratch
    tokv, width = emb_ref.shape[1:]
    rows = tokv // parts
    column = me_ref[1]
    copies = []
    for q, (first, size) in enumerate(cuts):
        for j in range(parts):
            i = q * parts + j
            start = pl.multiple_of((column ^ j) * rows + first, size)
            copies.append(
                pltpu.make_async_copy(pieces[i], emb_ref.at[:, pl.ds(start, size), :], sem.at[i])
            )
            copies[-1].start()
    for copy in copies:
        copy.wait()

    def normalise(side):
        xhat = normed(emb_ref[side].astype(jnp.float32))
        qin_ref[side] = (xhat * gains_ref[side, 0:1, :]).astype(jnp.bfloat16)
        min_ref[1 - side] = (xhat * gains_ref[1 - side, 1:2, :]).astype(jnp.bfloat16)

    def project_query(side, start, size):
        q_ref[side, :, start : start + size] = jnp.dot(
            qin_ref[side], wq[side, :, start : start + size], preferred_element_type=jnp.float32
        ).astype(jnp.bfloat16)

    def project_keyval(side, start, size):
        kv_ref[side, :, start : start + size] = jnp.dot(
            min_ref[side], wkv[side, :, start : start + size], preferred_element_type=jnp.float32
        ).astype(jnp.bfloat16)

    head_size = width // HEADS
    lanes = 2 * head_size
    low = lax.broadcasted_iota(jnp.int32, (tokv, lanes), 1) < head_size

    def split(values):
        zero = jnp.zeros_like(values)
        return jnp.concatenate([jnp.where(low, values, zero), jnp.where(low, zero, values)], axis=0)

    def soft(scores):
        top = jnp.max(scores, axis=-1, keepdims=True)
        e = jnp.exp2((scores - top) * (LOG2_E / head_size**0.5))
        return (e * (1.0 / jnp.sum(e, axis=-1, keepdims=True))).astype(jnp.bfloat16)

    def two_heads_scores(side, i):
        start = i * lanes
        query = q_ref[side, :, start : start + lanes]
        keys = split(kv_ref[side, :, start : start + lanes])
        return lax.dot_general(
            query, keys, (((1,), (1,)), ((), ())), preferred_element_type=jnp.float32
        )

    def two_heads(side, i, scores):
        start = i * lanes
        values = split(kv_ref[side, :, width + start : width + start + lanes])
        probs = jnp.concatenate([soft(scores[:, :tokv]), soft(scores[:, tokv:])], axis=1)
        ctx_ref[side, :, start : start + lanes] = jnp.dot(
            probs, values, preferred_element_type=jnp.float32
        ).astype(jnp.bfloat16)

    def finish(side, product):
        updated = emb_ref[side].astype(jnp.float32) + product
        final = (normed(updated) * gains_ref[side, 2:3, :]).astype(jnp.bfloat16)
        head = lax.dot_general(
            whead_ref[side], final, (((1,), (1,)), ((), ())), preferred_element_type=jnp.float32
        )
        conf = 1.0 + jnp.exp(head[3:4, :])
        out_ref[side, 0:3, :] = head[0:3, :] * conf
        out_ref[side, 3:4, :] = conf

    def project_out(side):
        return jnp.dot(ctx_ref[side], wo[side], preferred_element_type=jnp.float32)

    steps = HEADS // 2
    block = 2 * width // steps
    normalise(1)
    project_keyval(0, 0, 2 * width)
    normalise(0)
    project_query(0, 0, width)
    scores = two_heads_scores(0, 0)
    for i in range(2 * steps):
        side, at = i // steps, i % steps
        now = scores
        if side == 0:
            project_keyval(1, at * block, block)
            if at % 2:
                project_query(1, at // 2 * block, block)
        if i + 1 < 2 * steps:
            scores = two_heads_scores((i + 1) // steps, (i + 1) % steps)
        two_heads(side, at, now)
        if i == steps:
            finish(0, project_out(0))
    finish(1, project_out(1))


def load(*weights):
    return pl.pallas_call(
        load_kernel,
        out_shape=[jax.ShapeDtypeStruct(w.shape, w.dtype) for w in weights],
        in_specs=[HBM] * len(weights),
        out_specs=[VMEM] * len(weights),
        scratch_shapes=[pltpu.SemaphoreType.DMA((len(weights),))],
        compiler_params=pltpu.CompilerParams(vmem_limit_bytes=50 * 1024 * 1024),
        name="load",
    )(*weights)


def embed(parts, cuts, me, w_embed, pieces):
    views, rows, _ = pieces[0].shape
    full, width = w_embed.shape
    return pl.pallas_call(
        functools.partial(embed_kernel, parts, cuts),
        out_shape=[
            jax.ShapeDtypeStruct((views, size, width), jnp.bfloat16)
            for size in [size for _, size in cuts] + [rows]
        ],
        in_specs=[SMEM, VMEM] + [HBM] * parts,
        out_specs=[HBM] * (len(cuts) + 1),
        scratch_shapes=[
            pltpu.VMEM((views, rows, full), jnp.bfloat16),
            pltpu.VMEM((views, rows, width), jnp.bfloat16),
            pltpu.SemaphoreType.DMA((parts,)),
            pltpu.SemaphoreType.DMA((len(cuts) + 1,)),
        ],
        compiler_params=pltpu.CompilerParams(vmem_limit_bytes=16 * 1024 * 1024),
        cost_estimate=pl.CostEstimate(
            flops=2 * views * rows * full * width,
            bytes_accessed=2 * (full * width + 2 * views * rows * full),
            transcendentals=0,
        ),
        name="embed",
    )(me, w_embed, *pieces)


def pick(lanes, slots, cap, me, line, wants, own, below, above):
    views, size, width = own.shape
    reach = len(below)
    return pl.pallas_call(
        functools.partial(pick_kernel, lanes, reach, slots, cap),
        out_shape=[jax.ShapeDtypeStruct((len(slots), cap, size, width), jnp.bfloat16)] * lanes,
        in_specs=[SMEM, SMEM, SMEM] + [HBM] * (1 + 2 * reach),
        out_specs=[HBM] * lanes,
        scratch_shapes=[
            pltpu.VMEM((len(slots), views, size, width), jnp.bfloat16),
            pltpu.SemaphoreType.DMA((len(slots),)),
            pltpu.SemaphoreType.DMA((lanes * len(slots) * cap,)),
        ],
        compiler_params=pltpu.CompilerParams(vmem_limit_bytes=16 * 1024 * 1024),
        cost_estimate=pl.CostEstimate(
            flops=0,
            bytes_accessed=4 * lanes * len(slots) * cap * size * width,
            transcendentals=0,
        ),
        name="pick",
    )(me, line, wants, own, *below, *above)


def route(lanes, parts, cap, cuts, groups, me, line, sides, fetched):
    width = fetched[0].shape[-1]
    size = sum(size for _, size in cuts)
    base = cuts[0][0]
    cuts = tuple((first - base, each) for first, each in cuts)
    copies = len(cuts) * sum(len(group) for group in groups) * lanes * cap
    return pl.pallas_call(
        functools.partial(route_kernel, lanes, parts, cap, base, cuts, groups),
        out_shape=[jax.ShapeDtypeStruct((2, size, width), jnp.bfloat16)] * parts,
        in_specs=[SMEM, SMEM, SMEM] + [HBM] * len(fetched),
        out_specs=[HBM] * parts,
        scratch_shapes=[
            pltpu.VMEM((2 * parts, size, width), jnp.bfloat16),
            pltpu.SemaphoreType.DMA((copies,)),
            pltpu.SemaphoreType.DMA((parts,)),
        ],
        compiler_params=pltpu.CompilerParams(vmem_limit_bytes=16 * 1024 * 1024),
        cost_estimate=pl.CostEstimate(
            flops=0, bytes_accessed=8 * parts * size * width, transcendentals=0
        ),
        name="route",
    )(me, line, sides, *fetched)


def decode(parts, cuts, me, gains, w_head, w_query, w_keyval, w_out, pieces):
    width = pieces[0].shape[2]
    tokv = parts * sum(size for _, size in cuts)
    flops = 2 * 2 * tokv * width * (5 * width + 2 * tokv)
    return pl.pallas_call(
        functools.partial(decode_kernel, parts, cuts),
        out_shape=jax.ShapeDtypeStruct((2, 4, tokv), jnp.float32),
        in_specs=[SMEM, VMEM, VMEM, VMEM, VMEM, VMEM] + [HBM] * (parts * len(cuts)),
        out_specs=VMEM,
        scratch_shapes=[
            pltpu.VMEM((2, tokv, width), jnp.bfloat16),
            pltpu.VMEM((2, tokv, width), jnp.bfloat16),
            pltpu.VMEM((2, tokv, width), jnp.bfloat16),
            pltpu.VMEM((2, tokv, width), jnp.bfloat16),
            pltpu.VMEM((2, tokv, 2 * width), jnp.bfloat16),
            pltpu.VMEM((2, tokv, width), jnp.bfloat16),
            pltpu.SemaphoreType.DMA((parts * len(cuts),)),
        ],
        compiler_params=pltpu.CompilerParams(vmem_limit_bytes=40 * 1024 * 1024),
        cost_estimate=pl.CostEstimate(
            flops=flops, bytes_accessed=20 * width * width, transcendentals=2 * HEADS * tokv * tokv
        ),
        name="decode",
    )(me, gains, w_head, w_keyval, w_query, w_out, *pieces)


def on_device(tokens, pairs, w_embed, w_query, w_keyval, w_out, w_head, gains):
    count = lax.axis_size("view")
    parts = lax.axis_size("mp")
    row = lax.axis_index("view")
    column = lax.axis_index("mp")
    me = jnp.stack([row, column]).astype(jnp.int32)
    view_dev, tokv, _ = tokens.shape
    rows = tokv // parts
    block_pairs = pairs.shape[0]
    pair_dev = block_pairs // parts
    side_count = 2 * block_pairs
    cap = max(2, (side_count + count - 1) // count)
    slot_total = count * cap
    lanes = 1 << ((count.bit_length() - 1) // 2)
    length = count // lanes
    cuts = ((0, rows // 2), (rows // 2, rows // 2)) if rows % 32 == 0 else ((0, rows),)

    pieces = []
    for j in range(parts):
        piece = lax.dynamic_slice_in_dim(tokens, (column ^ j) * rows, rows, axis=1)
        pieces.append(lax.ppermute(piece, "mp", xor_pairs(parts, j)) if j else piece)

    pairs, pieces[1] = lax.optimization_barrier((pairs, pieces[1]))
    side_views = pairs.reshape(side_count)
    owners = side_views // view_dev
    local_ids = side_views % view_dev
    positions = jnp.arange(side_count, dtype=jnp.int32)
    same_owner = owners[:, None] == owners[None, :]
    slot_rank = jnp.sum(
        jnp.logical_and(same_owner, positions[None, :] < positions[:, None]), axis=1
    )
    slot_index = owners * cap + slot_rank
    slot_match = jnp.arange(slot_total, dtype=jnp.int32)[:, None] == slot_index[None, :]
    wanted = jnp.sum(jnp.where(slot_match, local_ids[None, :], 0), axis=1)
    used = jnp.any(slot_match, axis=1)
    slot_side = jnp.where(used, jnp.sum(jnp.where(slot_match, positions[None, :], 0), axis=1), -1)
    slot_side = slot_side.astype(jnp.int32)
    wanted = jnp.where(used, wanted, -1).astype(jnp.int32)
    wants = jnp.concatenate(
        [lax.ppermute(wanted, "view", xor_pairs(count, j)) if j else wanted for j in range(lanes)]
    )
    nearest = [sorted(range(length), key=lambda at: (abs(at - z), at)) for z in range(length)]
    line = jnp.asarray(nearest, jnp.int32)[row // lanes]

    weights = load(w_embed, w_query, w_keyval, w_out)
    pieces, weights = lax.optimization_barrier((pieces, weights))
    w_embed, w_query, w_keyval, w_out = weights
    *embedded, whole = embed(parts, cuts, me, w_embed, pieces)
    embedded, wants = lax.optimization_barrier((embedded, wants))
    groups = ((0,), tuple(range(1, length - 1)), (length - 1,))

    def swap(picked):
        return [
            lax.ppermute(picked[j], "view", xor_pairs(count, j)) if j else picked[j]
            for j in range(lanes)
        ]

    shared = pick(lanes, groups[0], cap, me, line, wants, whole, [], [])
    below, above = [[] for _ in cuts], [[] for _ in cuts]
    for p in range(1, length):
        up = [
            (z * lanes + y, (z + 1) * lanes + y) for z in range(p - 1, length - 1) for y in range(lanes)
        ]
        down = [
            (z * lanes + y, (z - 1) * lanes + y) for z in range(1, length - p + 1) for y in range(lanes)
        ]
        for q in range(len(cuts)):
            below[q].append(lax.ppermute((below[q] or [embedded[q]])[-1], "view", up))
            above[q].append(lax.ppermute((above[q] or [embedded[q]])[-1], "view", down))
        if p == 1:
            below[0], above[0], shared = lax.optimization_barrier((below[0], above[0], shared))
            shared = swap(shared)
        if p == 2:
            below[0], above[0], shared = lax.optimization_barrier((below[0], above[0], shared))
    fetched = []
    for q in range(len(cuts)):
        picked = []
        for group in groups[1:]:
            near = below[q][: group[-1]], above[q][: group[-1]]
            picked.append(pick(lanes, group, cap, me, line, wants, embedded[q], *near))
        fetched.append(list(shared))
        for group in picked:
            fetched[-1] += swap(group)
    slot_pair = slot_side // 2
    results, arrived = [], None
    for c in range(pair_dev):
        mine = jnp.logical_and(slot_side >= 0, slot_pair % pair_dev == c)
        place = jnp.where(mine, 2 * (slot_pair // pair_dev) + slot_side % 2, -1).astype(jnp.int32)
        steps = [(cut,) for cut in cuts] if c == 0 else [cuts]
        parcels = []
        for q, step in enumerate(steps):
            wave = fetched[q : q + 1] if c == 0 else fetched
            parcels += route(
                lanes, parts, cap, step, groups, me, line, place, [each for g in wave for each in g]
            )
        if c:
            parcels, arrived = lax.optimization_barrier((parcels, arrived))
        arrived = [
            lax.ppermute(parcel, "mp", xor_pairs(parts, i % parts)) if i % parts else parcel
            for i, parcel in enumerate(parcels)
        ]
        results.append(
            decode(
                parts,
                cuts if c == 0 else ((0, rows),),
                me,
                gains,
                w_head,
                w_query,
                w_keyval,
                w_out,
                arrived,
            )
        )
    results = jnp.stack(results)

    every = lax.all_gather(results, "mp", axis=0, tiled=True).reshape(side_count, 4 * tokv)
    slotted = jnp.dot(slot_match.astype(jnp.float32), every, precision=lax.Precision.HIGHEST)
    tags = jnp.broadcast_to(wanted.astype(jnp.float32)[:, None], (slot_total, 128))
    slotted = jnp.concatenate([slotted, tags], axis=1).reshape(count, cap, 4 * tokv + 128)
    returned = lax.all_to_all(slotted, "view", split_axis=0, concat_axis=0, tiled=True)
    picker = returned[:, :, 4 * tokv :][:, :, :1] == jnp.arange(view_dev, dtype=jnp.float32)
    summed = jnp.einsum(
        "rcv,rcx->vx",
        picker.astype(jnp.float32),
        returned[:, :, : 4 * tokv],
        precision=lax.Precision.HIGHEST,
    )
    return summed.reshape(view_dev, 4, tokv)


def solution(mesh):
    return jax.shard_map(
        on_device,
        mesh=mesh,
        in_specs=(P("view", None, "mp"), P("view", None), P(), P(), P(), P(), P(), P()),
        out_specs=P("view", None, None),
        check_vma=False,
    )
```

```python
import functools

import jax
import jax.numpy as jnp
from jax import lax
from jax.experimental import pallas as pl
from jax.experimental.pallas import tpu as pltpu
from jax.sharding import PartitionSpec as P

HEADS = 12
EPS = 1e-06
LOG2_E = 1.4426950408889634
HBM = pl.BlockSpec(memory_space=pltpu.HBM)
SMEM = pl.BlockSpec(memory_space=pltpu.SMEM)
VMEM = pl.BlockSpec(memory_space=pltpu.VMEM)


def xor_pairs(count, step):
    return [(i, i ^ step) for i in range(count)]


def load_kernel(*refs):
    count = len(refs) // 2
    copies = [pltpu.make_async_copy(refs[i], refs[count + i], refs[-1].at[i]) for i in range(count)]
    for copy in copies:
        copy.start()
    for copy in copies:
        copy.wait()


def embed_kernel(parts, cuts, me_ref, w_vmem, *refs):
    pieces, outs, whole = refs[:parts], refs[parts : parts + len(cuts)], refs[parts + len(cuts)]
    x_ref, emb_ref, in_sem, out_sem = refs[parts + len(cuts) + 1 :]
    views, _, feat = pieces[0].shape
    width = w_vmem.shape[1]
    column = me_ref[1]
    copies = []
    for j in range(parts):
        start = pl.multiple_of((column ^ j) * feat, feat)
        copies.append(
            pltpu.make_async_copy(pieces[j], x_ref.at[:, :, pl.ds(start, feat)], in_sem.at[j])
        )
        copies[-1].start()
    for copy in copies:
        copy.wait()
    copies = []
    for q, (first, size) in enumerate(cuts):
        emb = jnp.dot(
            x_ref[:, first : first + size, :].reshape(views * size, parts * feat),
            w_vmem[...],
            preferred_element_type=jnp.float32,
        )
        emb_ref[:, first : first + size, :] = emb.astype(jnp.bfloat16).reshape(views, size, width)
        copies.append(
            pltpu.make_async_copy(
                emb_ref.at[:, pl.ds(first, size), :], outs[q], out_sem.at[q]
            )
        )
        copies[-1].start()
    copies.append(pltpu.make_async_copy(emb_ref, whole, out_sem.at[len(cuts)]))
    copies[-1].start()
    for copy in copies:
        copy.wait()


def pick_kernel(lanes, slots, cap, me_ref, line_ref, want_ref, *refs):
    count = len(slots)
    sources, outs = refs[:count], refs[count : count + lanes]
    stage_ref, in_sem, out_sem = refs[count + lanes :]
    lane = me_ref[0] % lanes
    rows = line_ref.shape[0] * lanes
    copies = [
        pltpu.make_async_copy(sources[n], stage_ref.at[n], in_sem.at[n]) for n in range(count)
    ]
    for copy in copies:
        copy.start()
    for copy in copies:
        copy.wait()
    copies = []
    for j in range(lanes):
        for n, i in enumerate(slots):
            for c in range(cap):
                view = want_ref[(j * rows + line_ref[i] * lanes + lane) * cap + c]
                copies.append(
                    pltpu.make_async_copy(
                        stage_ref.at[n, jnp.maximum(view, 0)], outs[j].at[n, c], out_sem.at[len(copies)]
                    )
                )
                copies[-1].start()
    for copy in copies:
        copy.wait()


def route_kernel(lanes, parts, cap, base, cuts, groups, me_ref, line_ref, side_ref, *refs):
    count = len(cuts) * len(groups) * lanes
    fetched, outs = refs[:count], refs[count : count + parts]
    stage_ref, in_sem, out_sem = refs[count + parts :]
    lane, column = me_ref[0] % lanes, me_ref[1]

    def slots(act):
        number = 0
        for q, (first, size) in enumerate(cuts):
            for g, group in enumerate(groups):
                for j in range(lanes):
                    source = fetched[(q * len(groups) + g) * lanes + j]
                    for n, i in enumerate(group):
                        for c in range(cap):
                            side = side_ref[(line_ref[i] * lanes + (lane ^ j)) * cap + c]
                            part = source.at[n, c]
                            if source.shape[2] > size:
                                part = source.at[n, c, pl.ds(base + first, size)]

                            @pl.when(side >= 0)
                            def _():
                                act(
                                    pltpu.make_async_copy(
                                        part,
                                        stage_ref.at[side, pl.ds(first, size), :],
                                        in_sem.at[number],
                                    )
                                )

                            number += 1

    slots(lambda copy: copy.start())
    slots(lambda copy: copy.wait())
    copies = []
    for j in range(parts):
        copies.append(
            pltpu.make_async_copy(
                stage_ref.at[pl.ds(2 * (column ^ j), 2)], outs[j], out_sem.at[j]
            )
        )
        copies[-1].start()
    for copy in copies:
        copy.wait()


def normed(values):
    mean = jnp.mean(values, axis=-1, keepdims=True)
    centred = values - mean
    var = jnp.mean(centred * centred, axis=-1, keepdims=True)
    return centred * lax.rsqrt(var + EPS)


def decode_kernel(parts, cuts, me_ref, gains_ref, whead_ref, wkv, wq, wo, *refs):
    pieces, out_ref = refs[: parts * len(cuts)], refs[parts * len(cuts)]
    scratch = refs[parts * len(cuts) + 1 :]
    emb_ref, qin_ref, min_ref, q_ref, kv_ref, ctx_ref, sem = scratch
    tokv, width = emb_ref.shape[1:]
    rows = tokv // parts
    column = me_ref[1]
    copies = []
    for q, (first, size) in enumerate(cuts):
        for j in range(parts):
            i = q * parts + j
            start = pl.multiple_of((column ^ j) * rows + first, size)
            copies.append(
                pltpu.make_async_copy(pieces[i], emb_ref.at[:, pl.ds(start, size), :], sem.at[i])
            )
            copies[-1].start()
    for copy in copies:
        copy.wait()

    def normalise(side):
        xhat = normed(emb_ref[side].astype(jnp.float32))
        qin_ref[side] = (xhat * gains_ref[side, 0:1, :]).astype(jnp.bfloat16)
        min_ref[1 - side] = (xhat * gains_ref[1 - side, 1:2, :]).astype(jnp.bfloat16)

    def project_query(side, start, size):
        q_ref[side, :, start : start + size] = jnp.dot(
            qin_ref[side], wq[side, :, start : start + size], preferred_element_type=jnp.float32
        ).astype(jnp.bfloat16)

    def project_keyval(side, start, size):
        kv_ref[side, :, start : start + size] = jnp.dot(
            min_ref[side], wkv[side, :, start : start + size], preferred_element_type=jnp.float32
        ).astype(jnp.bfloat16)

    head_size = width // HEADS
    lanes = 2 * head_size
    low = lax.broadcasted_iota(jnp.int32, (tokv, lanes), 1) < head_size

    def split(values):
        zero = jnp.zeros_like(values)
        return jnp.concatenate([jnp.where(low, values, zero), jnp.where(low, zero, values)], axis=0)

    def soft(scores):
        top = jnp.max(scores, axis=-1, keepdims=True)
        e = jnp.exp2((scores - top) * (LOG2_E / head_size**0.5))
        return (e * (1.0 / jnp.sum(e, axis=-1, keepdims=True))).astype(jnp.bfloat16)

    def two_heads_scores(side, i):
        start = i * lanes
        query = q_ref[side, :, start : start + lanes]
        keys = split(kv_ref[side, :, start : start + lanes])
        return lax.dot_general(
            query, keys, (((1,), (1,)), ((), ())), preferred_element_type=jnp.float32
        )

    def two_heads(side, i, scores):
        start = i * lanes
        values = split(kv_ref[side, :, width + start : width + start + lanes])
        probs = jnp.concatenate([soft(scores[:, :tokv]), soft(scores[:, tokv:])], axis=1)
        ctx_ref[side, :, start : start + lanes] = jnp.dot(
            probs, values, preferred_element_type=jnp.float32
        ).astype(jnp.bfloat16)

    def finish(side, product):
        updated = emb_ref[side].astype(jnp.float32) + product
        final = (normed(updated) * gains_ref[side, 2:3, :]).astype(jnp.bfloat16)
        head = lax.dot_general(
            whead_ref[side], final, (((1,), (1,)), ((), ())), preferred_element_type=jnp.float32
        )
        conf = 1.0 + jnp.exp(head[3:4, :])
        out_ref[side, 0:3, :] = head[0:3, :] * conf
        out_ref[side, 3:4, :] = conf

    def project_out(side):
        return jnp.dot(ctx_ref[side], wo[side], preferred_element_type=jnp.float32)

    steps = HEADS // 2
    block = 2 * width // steps
    normalise(1)
    project_keyval(0, 0, 2 * width)
    normalise(0)
    project_query(0, 0, width)
    scores = two_heads_scores(0, 0)
    for i in range(2 * steps):
        side, at = i // steps, i % steps
        now = scores
        if side == 0:
            project_keyval(1, at * block, block)
            if at % 2:
                project_query(1, at // 2 * block, block)
        if i + 1 < 2 * steps:
            scores = two_heads_scores((i + 1) // steps, (i + 1) % steps)
        two_heads(side, at, now)
        if i == steps:
            finish(0, project_out(0))
    finish(1, project_out(1))


def load(*weights):
    return pl.pallas_call(
        load_kernel,
        out_shape=[jax.ShapeDtypeStruct(w.shape, w.dtype) for w in weights],
        in_specs=[HBM] * len(weights),
        out_specs=[VMEM] * len(weights),
        scratch_shapes=[pltpu.SemaphoreType.DMA((len(weights),))],
        compiler_params=pltpu.CompilerParams(vmem_limit_bytes=50 * 1024 * 1024),
        name="load",
    )(*weights)


def embed(parts, cuts, me, w_embed, pieces):
    views, rows, _ = pieces[0].shape
    full, width = w_embed.shape
    return pl.pallas_call(
        functools.partial(embed_kernel, parts, cuts),
        out_shape=[
            jax.ShapeDtypeStruct((views, size, width), jnp.bfloat16)
            for size in [size for _, size in cuts] + [rows]
        ],
        in_specs=[SMEM, VMEM] + [HBM] * parts,
        out_specs=[HBM] * (len(cuts) + 1),
        scratch_shapes=[
            pltpu.VMEM((views, rows, full), jnp.bfloat16),
            pltpu.VMEM((views, rows, width), jnp.bfloat16),
            pltpu.SemaphoreType.DMA((parts,)),
            pltpu.SemaphoreType.DMA((len(cuts) + 1,)),
        ],
        compiler_params=pltpu.CompilerParams(vmem_limit_bytes=16 * 1024 * 1024),
        cost_estimate=pl.CostEstimate(
            flops=2 * views * rows * full * width,
            bytes_accessed=2 * (full * width + 2 * views * rows * full),
            transcendentals=0,
        ),
        name="embed",
    )(me, w_embed, *pieces)


def pick(lanes, slots, cap, me, line, wants, sources):
    views, size, width = sources[0].shape
    return pl.pallas_call(
        functools.partial(pick_kernel, lanes, slots, cap),
        out_shape=[jax.ShapeDtypeStruct((len(slots), cap, size, width), jnp.bfloat16)] * lanes,
        in_specs=[SMEM, SMEM, SMEM] + [HBM] * len(sources),
        out_specs=[HBM] * lanes,
        scratch_shapes=[
            pltpu.VMEM((len(slots), views, size, width), jnp.bfloat16),
            pltpu.SemaphoreType.DMA((len(slots),)),
            pltpu.SemaphoreType.DMA((lanes * len(slots) * cap,)),
        ],
        compiler_params=pltpu.CompilerParams(vmem_limit_bytes=16 * 1024 * 1024),
        cost_estimate=pl.CostEstimate(
            flops=0,
            bytes_accessed=4 * lanes * len(slots) * cap * size * width,
            transcendentals=0,
        ),
        name="pick",
    )(me, line, wants, *sources)


def route(lanes, parts, cap, cuts, groups, me, line, sides, fetched):
    width = fetched[0].shape[-1]
    size = sum(size for _, size in cuts)
    base = cuts[0][0]
    cuts = tuple((first - base, each) for first, each in cuts)
    copies = len(cuts) * sum(len(group) for group in groups) * lanes * cap
    return pl.pallas_call(
        functools.partial(route_kernel, lanes, parts, cap, base, cuts, groups),
        out_shape=[jax.ShapeDtypeStruct((2, size, width), jnp.bfloat16)] * parts,
        in_specs=[SMEM, SMEM, SMEM] + [HBM] * len(fetched),
        out_specs=[HBM] * parts,
        scratch_shapes=[
            pltpu.VMEM((2 * parts, size, width), jnp.bfloat16),
            pltpu.SemaphoreType.DMA((copies,)),
            pltpu.SemaphoreType.DMA((parts,)),
        ],
        compiler_params=pltpu.CompilerParams(vmem_limit_bytes=16 * 1024 * 1024),
        cost_estimate=pl.CostEstimate(
            flops=0, bytes_accessed=8 * parts * size * width, transcendentals=0
        ),
        name="route",
    )(me, line, sides, *fetched)


def decode(parts, cuts, me, gains, w_head, w_query, w_keyval, w_out, pieces):
    width = pieces[0].shape[2]
    tokv = parts * sum(size for _, size in cuts)
    flops = 2 * 2 * tokv * width * (5 * width + 2 * tokv)
    return pl.pallas_call(
        functools.partial(decode_kernel, parts, cuts),
        out_shape=jax.ShapeDtypeStruct((2, 4, tokv), jnp.float32),
        in_specs=[SMEM, VMEM, VMEM, VMEM, VMEM, VMEM] + [HBM] * (parts * len(cuts)),
        out_specs=VMEM,
        scratch_shapes=[
            pltpu.VMEM((2, tokv, width), jnp.bfloat16),
            pltpu.VMEM((2, tokv, width), jnp.bfloat16),
            pltpu.VMEM((2, tokv, width), jnp.bfloat16),
            pltpu.VMEM((2, tokv, width), jnp.bfloat16),
            pltpu.VMEM((2, tokv, 2 * width), jnp.bfloat16),
            pltpu.VMEM((2, tokv, width), jnp.bfloat16),
            pltpu.SemaphoreType.DMA((parts * len(cuts),)),
        ],
        compiler_params=pltpu.CompilerParams(vmem_limit_bytes=40 * 1024 * 1024),
        cost_estimate=pl.CostEstimate(
            flops=flops, bytes_accessed=20 * width * width, transcendentals=2 * HEADS * tokv * tokv
        ),
        name="decode",
    )(me, gains, w_head, w_keyval, w_query, w_out, *pieces)


def on_device(tokens, pairs, w_embed, w_query, w_keyval, w_out, w_head, gains):
    count = lax.axis_size("view")
    parts = lax.axis_size("mp")
    row = lax.axis_index("view")
    column = lax.axis_index("mp")
    me = jnp.stack([row, column]).astype(jnp.int32)
    view_dev, tokv, _ = tokens.shape
    rows = tokv // parts
    block_pairs = pairs.shape[0]
    pair_dev = block_pairs // parts
    side_count = 2 * block_pairs
    cap = max(2, (side_count + count - 1) // count)
    slot_total = count * cap
    lanes = 1 << ((count.bit_length() - 1) // 2)
    length = count // lanes
    cuts = ((0, rows // 2), (rows // 2, rows // 2)) if rows % 32 == 0 else ((0, rows),)

    pieces = []
    for j in range(parts):
        piece = lax.dynamic_slice_in_dim(tokens, (column ^ j) * rows, rows, axis=1)
        pieces.append(lax.ppermute(piece, "mp", xor_pairs(parts, j)) if j else piece)

    pairs, pieces[1] = lax.optimization_barrier((pairs, pieces[1]))
    side_views = pairs.reshape(side_count)
    owners = side_views // view_dev
    local_ids = side_views % view_dev
    positions = jnp.arange(side_count, dtype=jnp.int32)
    same_owner = owners[:, None] == owners[None, :]
    slot_rank = jnp.sum(
        jnp.logical_and(same_owner, positions[None, :] < positions[:, None]), axis=1
    )
    slot_index = owners * cap + slot_rank
    slot_match = jnp.arange(slot_total, dtype=jnp.int32)[:, None] == slot_index[None, :]
    wanted = jnp.sum(jnp.where(slot_match, local_ids[None, :], 0), axis=1)
    used = jnp.any(slot_match, axis=1)
    slot_side = jnp.where(used, jnp.sum(jnp.where(slot_match, positions[None, :], 0), axis=1), -1)
    slot_side = slot_side.astype(jnp.int32)
    wanted = jnp.where(used, wanted, -1).astype(jnp.int32)
    wants = jnp.concatenate(
        [lax.ppermute(wanted, "view", xor_pairs(count, j)) if j else wanted for j in range(lanes)]
    )
    ring = [0] + list(range(1, length, 2)) + list(range(2, length, 2))[::-1]
    nearest = [[ring[(ring.index(z) - i) % length] for i in range(length)] for z in range(length)]
    hop = [
        (ring[k] * lanes + y, ring[(k + 1) % length] * lanes + y)
        for k in range(length)
        for y in range(lanes)
    ]
    line = jnp.asarray(nearest, jnp.int32)[row // lanes]

    weights = load(w_embed, w_query, w_keyval, w_out)
    pieces, weights = lax.optimization_barrier((pieces, weights))
    w_embed, w_query, w_keyval, w_out = weights
    *embedded, whole = embed(parts, cuts, me, w_embed, pieces)
    embedded, wants = lax.optimization_barrier((embedded, wants))
    groups = ((0,), tuple(range(1, length - 1)), (length - 1,))

    def swap(picked):
        return [
            lax.ppermute(picked[j], "view", xor_pairs(count, j)) if j else picked[j]
            for j in range(lanes)
        ]

    shared = pick(lanes, groups[0], cap, me, line, wants, [whole])
    passed = [[part] for part in embedded]
    for p in range(1, length):
        for q in range(len(cuts)):
            passed[q].append(lax.ppermute(passed[q][-1], "view", hop))
        if p == 1:
            passed[0][1], shared = lax.optimization_barrier((passed[0][1], shared))
            shared = swap(shared)
        if p == 2:
            passed[0][2], shared = lax.optimization_barrier((passed[0][2], shared))
    fetched = []
    for q in range(len(cuts)):
        picked = []
        for group in groups[1:]:
            near = [passed[q][i] for i in group]
            picked.append(pick(lanes, group, cap, me, line, wants, near))
        fetched.append(list(shared))
        for group in picked:
            fetched[-1] += swap(group)
    slot_pair = slot_side // 2
    results = []
    for c in range(pair_dev):
        mine = jnp.logical_and(slot_side >= 0, slot_pair % pair_dev == c)
        place = jnp.where(mine, 2 * (slot_pair // pair_dev) + slot_side % 2, -1).astype(jnp.int32)
        steps = [(cut,) for cut in cuts] if c == 0 else [cuts]
        parcels = []
        for q, step in enumerate(steps):
            wave = fetched[q : q + 1] if c == 0 else fetched
            parcels += route(
                lanes, parts, cap, step, groups, me, line, place, [each for g in wave for each in g]
            )
        arrived = []
        for i, parcel in enumerate(parcels):
            arrived.append(
                lax.ppermute(parcel, "mp", xor_pairs(parts, i % parts)) if i % parts else parcel
            )
        results.append(
            decode(
                parts,
                cuts if c == 0 else ((0, rows),),
                me,
                gains,
                w_head,
                w_query,
                w_keyval,
                w_out,
                arrived,
            )
        )
    results = jnp.stack(results)

    every = lax.all_gather(results, "mp", axis=0, tiled=True).reshape(side_count, 4 * tokv)
    slotted = jnp.dot(slot_match.astype(jnp.float32), every, precision=lax.Precision.HIGHEST)
    tags = jnp.broadcast_to(wanted.astype(jnp.float32)[:, None], (slot_total, 128))
    slotted = jnp.concatenate([slotted, tags], axis=1).reshape(count, cap, 4 * tokv + 128)
    returned = lax.all_to_all(slotted, "view", split_axis=0, concat_axis=0, tiled=True)
    picker = returned[:, :, 4 * tokv :][:, :, :1] == jnp.arange(view_dev, dtype=jnp.float32)
    summed = jnp.einsum(
        "rcv,rcx->vx",
        picker.astype(jnp.float32),
        returned[:, :, : 4 * tokv],
        precision=lax.Precision.HIGHEST,
    )
    return summed.reshape(view_dev, 4, tokv)


def solution(mesh):
    return jax.shard_map(
        on_device,
        mesh=mesh,
        in_specs=(P("view", None, "mp"), P("view", None), P(), P(), P(), P(), P(), P()),
        out_specs=P("view", None, None),
        check_vma=False,
    )
```

```python
import functools

import jax
import jax.numpy as jnp
from jax import lax
from jax.experimental import pallas as pl
from jax.experimental.pallas import tpu as pltpu
from jax.sharding import PartitionSpec as P

HEADS = 12
EPS = 1e-06
LOG2_E = 1.4426950408889634
HBM = pl.BlockSpec(memory_space=pltpu.HBM)
SMEM = pl.BlockSpec(memory_space=pltpu.SMEM)
VMEM = pl.BlockSpec(memory_space=pltpu.VMEM)


def xor_pairs(count, step):
    return [(i, i ^ step) for i in range(count)]


def load_kernel(*refs):
    count = len(refs) // 2
    copies = [pltpu.make_async_copy(refs[i], refs[count + i], refs[-1].at[i]) for i in range(count)]
    for copy in copies:
        copy.start()
    for copy in copies:
        copy.wait()


def embed_kernel(parts, cuts, me_ref, w_vmem, *refs):
    pieces, outs, whole = refs[:parts], refs[parts : parts + len(cuts)], refs[parts + len(cuts)]
    x_ref, emb_ref, in_sem, out_sem = refs[parts + len(cuts) + 1 :]
    views, _, feat = pieces[0].shape
    width = w_vmem.shape[1]
    column = me_ref[1]
    copies = []
    for j in range(parts):
        start = pl.multiple_of((column ^ j) * feat, feat)
        copies.append(
            pltpu.make_async_copy(pieces[j], x_ref.at[:, :, pl.ds(start, feat)], in_sem.at[j])
        )
        copies[-1].start()
    for copy in copies:
        copy.wait()
    copies = []
    for q, (first, size) in enumerate(cuts):
        emb = jnp.dot(
            x_ref[:, first : first + size, :].reshape(views * size, parts * feat),
            w_vmem[...],
            preferred_element_type=jnp.float32,
        )
        emb_ref[:, first : first + size, :] = emb.astype(jnp.bfloat16).reshape(views, size, width)
        copies.append(
            pltpu.make_async_copy(
                emb_ref.at[:, pl.ds(first, size), :], outs[q], out_sem.at[q]
            )
        )
        copies[-1].start()
    copies.append(pltpu.make_async_copy(emb_ref, whole, out_sem.at[len(cuts)]))
    copies[-1].start()
    for copy in copies:
        copy.wait()


def pick_kernel(lanes, slots, cap, me_ref, line_ref, want_ref, *refs):
    count = len(slots)
    sources, outs = refs[:count], refs[count : count + lanes]
    stage_ref, in_sem, out_sem = refs[count + lanes :]
    lane = me_ref[0] % lanes
    rows = line_ref.shape[0] * lanes
    copies = [
        pltpu.make_async_copy(sources[n], stage_ref.at[n], in_sem.at[n]) for n in range(count)
    ]
    for copy in copies:
        copy.start()
    for copy in copies:
        copy.wait()
    copies = []
    for j in range(lanes):
        for n, i in enumerate(slots):
            for c in range(cap):
                view = want_ref[(j * rows + line_ref[i] * lanes + lane) * cap + c]
                copies.append(
                    pltpu.make_async_copy(
                        stage_ref.at[n, jnp.maximum(view, 0)], outs[j].at[n, c], out_sem.at[len(copies)]
                    )
                )
                copies[-1].start()
    for copy in copies:
        copy.wait()


def route_kernel(lanes, parts, cap, base, cuts, groups, me_ref, line_ref, side_ref, *refs):
    count = len(cuts) * len(groups) * lanes
    fetched, outs = refs[:count], refs[count : count + parts]
    stage_ref, in_sem, out_sem = refs[count + parts :]
    lane, column = me_ref[0] % lanes, me_ref[1]

    def slots(act):
        number = 0
        for q, (first, size) in enumerate(cuts):
            for g, group in enumerate(groups):
                for j in range(lanes):
                    source = fetched[(q * len(groups) + g) * lanes + j]
                    for n, i in enumerate(group):
                        for c in range(cap):
                            side = side_ref[(line_ref[i] * lanes + (lane ^ j)) * cap + c]
                            part = source.at[n, c]
                            if source.shape[2] > size:
                                part = source.at[n, c, pl.ds(base + first, size)]

                            @pl.when(side >= 0)
                            def _():
                                act(
                                    pltpu.make_async_copy(
                                        part,
                                        stage_ref.at[side, pl.ds(first, size), :],
                                        in_sem.at[number],
                                    )
                                )

                            number += 1

    slots(lambda copy: copy.start())
    slots(lambda copy: copy.wait())
    copies = []
    for j in range(parts):
        copies.append(
            pltpu.make_async_copy(
                stage_ref.at[pl.ds(2 * (column ^ j), 2)], outs[j], out_sem.at[j]
            )
        )
        copies[-1].start()
    for copy in copies:
        copy.wait()


def normed(values):
    mean = jnp.mean(values, axis=-1, keepdims=True)
    centred = values - mean
    var = jnp.mean(centred * centred, axis=-1, keepdims=True)
    return centred * lax.rsqrt(var + EPS)


def decode_kernel(parts, cuts, me_ref, gains_ref, whead_ref, wkv, wq, wo, *refs):
    pieces, out_ref = refs[: parts * len(cuts)], refs[parts * len(cuts)]
    scratch = refs[parts * len(cuts) + 1 :]
    emb_ref, qin_ref, min_ref, q_ref, kv_ref, ctx_ref, sem = scratch
    tokv, width = emb_ref.shape[1:]
    rows = tokv // parts
    column = me_ref[1]
    copies = []
    for q, (first, size) in enumerate(cuts):
        for j in range(parts):
            i = q * parts + j
            start = pl.multiple_of((column ^ j) * rows + first, size)
            copies.append(
                pltpu.make_async_copy(pieces[i], emb_ref.at[:, pl.ds(start, size), :], sem.at[i])
            )
            copies[-1].start()
    for copy in copies:
        copy.wait()

    def normalise(side):
        xhat = normed(emb_ref[side].astype(jnp.float32))
        qin_ref[side] = (xhat * gains_ref[side, 0:1, :]).astype(jnp.bfloat16)
        min_ref[1 - side] = (xhat * gains_ref[1 - side, 1:2, :]).astype(jnp.bfloat16)

    def project_query(side, start, size):
        q_ref[side, :, start : start + size] = jnp.dot(
            qin_ref[side], wq[side, :, start : start + size], preferred_element_type=jnp.float32
        ).astype(jnp.bfloat16)

    def project_keyval(side, start, size):
        kv_ref[side, :, start : start + size] = jnp.dot(
            min_ref[side], wkv[side, :, start : start + size], preferred_element_type=jnp.float32
        ).astype(jnp.bfloat16)

    head_size = width // HEADS
    lanes = 2 * head_size
    low = lax.broadcasted_iota(jnp.int32, (tokv, lanes), 1) < head_size

    def split(values):
        zero = jnp.zeros_like(values)
        return jnp.concatenate([jnp.where(low, values, zero), jnp.where(low, zero, values)], axis=0)

    def soft(scores):
        top = jnp.max(scores, axis=-1, keepdims=True)
        e = jnp.exp2((scores - top) * (LOG2_E / head_size**0.5))
        return (e * (1.0 / jnp.sum(e, axis=-1, keepdims=True))).astype(jnp.bfloat16)

    def two_heads_scores(side, i):
        start = i * lanes
        query = q_ref[side, :, start : start + lanes]
        keys = split(kv_ref[side, :, start : start + lanes])
        return lax.dot_general(
            query, keys, (((1,), (1,)), ((), ())), preferred_element_type=jnp.float32
        )

    def two_heads(side, i, scores):
        start = i * lanes
        values = split(kv_ref[side, :, width + start : width + start + lanes])
        probs = jnp.concatenate([soft(scores[:, :tokv]), soft(scores[:, tokv:])], axis=1)
        ctx_ref[side, :, start : start + lanes] = jnp.dot(
            probs, values, preferred_element_type=jnp.float32
        ).astype(jnp.bfloat16)

    def finish(side, product):
        updated = emb_ref[side].astype(jnp.float32) + product
        final = (normed(updated) * gains_ref[side, 2:3, :]).astype(jnp.bfloat16)
        head = lax.dot_general(
            whead_ref[side], final, (((1,), (1,)), ((), ())), preferred_element_type=jnp.float32
        )
        conf = 1.0 + jnp.exp(head[3:4, :])
        out_ref[side, 0:3, :] = head[0:3, :] * conf
        out_ref[side, 3:4, :] = conf

    def project_out(side):
        return jnp.dot(ctx_ref[side], wo[side], preferred_element_type=jnp.float32)

    steps = HEADS // 2
    block = 2 * width // steps
    normalise(1)
    project_keyval(0, 0, 2 * width)
    normalise(0)
    project_query(0, 0, width)
    scores = two_heads_scores(0, 0)
    for i in range(2 * steps):
        side, at = i // steps, i % steps
        now = scores
        if side == 0:
            project_keyval(1, at * block, block)
            if at % 2:
                project_query(1, at // 2 * block, block)
        if i + 1 < 2 * steps:
            scores = two_heads_scores((i + 1) // steps, (i + 1) % steps)
        two_heads(side, at, now)
        if i == steps:
            finish(0, project_out(0))
    finish(1, project_out(1))


def load(*weights):
    return pl.pallas_call(
        load_kernel,
        out_shape=[jax.ShapeDtypeStruct(w.shape, w.dtype) for w in weights],
        in_specs=[HBM] * len(weights),
        out_specs=[VMEM] * len(weights),
        scratch_shapes=[pltpu.SemaphoreType.DMA((len(weights),))],
        compiler_params=pltpu.CompilerParams(vmem_limit_bytes=50 * 1024 * 1024),
        name="load",
    )(*weights)


def embed(parts, cuts, me, w_embed, pieces):
    views, rows, _ = pieces[0].shape
    full, width = w_embed.shape
    return pl.pallas_call(
        functools.partial(embed_kernel, parts, cuts),
        out_shape=[
            jax.ShapeDtypeStruct((views, size, width), jnp.bfloat16)
            for size in [size for _, size in cuts] + [rows]
        ],
        in_specs=[SMEM, VMEM] + [HBM] * parts,
        out_specs=[HBM] * (len(cuts) + 1),
        scratch_shapes=[
            pltpu.VMEM((views, rows, full), jnp.bfloat16),
            pltpu.VMEM((views, rows, width), jnp.bfloat16),
            pltpu.SemaphoreType.DMA((parts,)),
            pltpu.SemaphoreType.DMA((len(cuts) + 1,)),
        ],
        compiler_params=pltpu.CompilerParams(vmem_limit_bytes=16 * 1024 * 1024),
        cost_estimate=pl.CostEstimate(
            flops=2 * views * rows * full * width,
            bytes_accessed=2 * (full * width + 2 * views * rows * full),
            transcendentals=0,
        ),
        name="embed",
    )(me, w_embed, *pieces)


def pick(lanes, slots, cap, me, line, wants, sources):
    views, size, width = sources[0].shape
    return pl.pallas_call(
        functools.partial(pick_kernel, lanes, slots, cap),
        out_shape=[jax.ShapeDtypeStruct((len(slots), cap, size, width), jnp.bfloat16)] * lanes,
        in_specs=[SMEM, SMEM, SMEM] + [HBM] * len(sources),
        out_specs=[HBM] * lanes,
        scratch_shapes=[
            pltpu.VMEM((len(slots), views, size, width), jnp.bfloat16),
            pltpu.SemaphoreType.DMA((len(slots),)),
            pltpu.SemaphoreType.DMA((lanes * len(slots) * cap,)),
        ],
        compiler_params=pltpu.CompilerParams(vmem_limit_bytes=16 * 1024 * 1024),
        cost_estimate=pl.CostEstimate(
            flops=0,
            bytes_accessed=4 * lanes * len(slots) * cap * size * width,
            transcendentals=0,
        ),
        name="pick",
    )(me, line, wants, *sources)


def route(lanes, parts, cap, cuts, groups, me, line, sides, fetched):
    width = fetched[0].shape[-1]
    size = sum(size for _, size in cuts)
    base = cuts[0][0]
    cuts = tuple((first - base, each) for first, each in cuts)
    copies = len(cuts) * sum(len(group) for group in groups) * lanes * cap
    return pl.pallas_call(
        functools.partial(route_kernel, lanes, parts, cap, base, cuts, groups),
        out_shape=[jax.ShapeDtypeStruct((2, size, width), jnp.bfloat16)] * parts,
        in_specs=[SMEM, SMEM, SMEM] + [HBM] * len(fetched),
        out_specs=[HBM] * parts,
        scratch_shapes=[
            pltpu.VMEM((2 * parts, size, width), jnp.bfloat16),
            pltpu.SemaphoreType.DMA((copies,)),
            pltpu.SemaphoreType.DMA((parts,)),
        ],
        compiler_params=pltpu.CompilerParams(vmem_limit_bytes=16 * 1024 * 1024),
        cost_estimate=pl.CostEstimate(
            flops=0, bytes_accessed=8 * parts * size * width, transcendentals=0
        ),
        name="route",
    )(me, line, sides, *fetched)


def decode(parts, cuts, me, gains, w_head, w_query, w_keyval, w_out, pieces):
    width = pieces[0].shape[2]
    tokv = parts * sum(size for _, size in cuts)
    flops = 2 * 2 * tokv * width * (5 * width + 2 * tokv)
    return pl.pallas_call(
        functools.partial(decode_kernel, parts, cuts),
        out_shape=jax.ShapeDtypeStruct((2, 4, tokv), jnp.float32),
        in_specs=[SMEM, VMEM, VMEM, VMEM, VMEM, VMEM] + [HBM] * (parts * len(cuts)),
        out_specs=VMEM,
        scratch_shapes=[
            pltpu.VMEM((2, tokv, width), jnp.bfloat16),
            pltpu.VMEM((2, tokv, width), jnp.bfloat16),
            pltpu.VMEM((2, tokv, width), jnp.bfloat16),
            pltpu.VMEM((2, tokv, width), jnp.bfloat16),
            pltpu.VMEM((2, tokv, 2 * width), jnp.bfloat16),
            pltpu.VMEM((2, tokv, width), jnp.bfloat16),
            pltpu.SemaphoreType.DMA((parts * len(cuts),)),
        ],
        compiler_params=pltpu.CompilerParams(vmem_limit_bytes=40 * 1024 * 1024),
        cost_estimate=pl.CostEstimate(
            flops=flops, bytes_accessed=20 * width * width, transcendentals=2 * HEADS * tokv * tokv
        ),
        name="decode",
    )(me, gains, w_head, w_keyval, w_query, w_out, *pieces)


def on_device(tokens, pairs, w_embed, w_query, w_keyval, w_out, w_head, gains):
    count = lax.axis_size("view")
    parts = lax.axis_size("mp")
    row = lax.axis_index("view")
    column = lax.axis_index("mp")
    me = jnp.stack([row, column]).astype(jnp.int32)
    view_dev, tokv, _ = tokens.shape
    rows = tokv // parts
    block_pairs = pairs.shape[0]
    pair_dev = block_pairs // parts
    side_count = 2 * block_pairs
    cap = max(2, (side_count + count - 1) // count)
    slot_total = count * cap
    lanes = 1 << ((count.bit_length() - 1) // 2)
    length = count // lanes
    cuts = ((0, rows // 2), (rows // 2, rows // 2)) if rows % 32 == 0 else ((0, rows),)

    pieces = []
    for j in range(parts):
        piece = lax.dynamic_slice_in_dim(tokens, (column ^ j) * rows, rows, axis=1)
        pieces.append(lax.ppermute(piece, "mp", xor_pairs(parts, j)) if j else piece)

    pairs, pieces[1] = lax.optimization_barrier((pairs, pieces[1]))
    side_views = pairs.reshape(side_count)
    owners = side_views // view_dev
    local_ids = side_views % view_dev
    positions = jnp.arange(side_count, dtype=jnp.int32)
    same_owner = owners[:, None] == owners[None, :]
    slot_rank = jnp.sum(
        jnp.logical_and(same_owner, positions[None, :] < positions[:, None]), axis=1
    )
    slot_index = owners * cap + slot_rank
    slot_match = jnp.arange(slot_total, dtype=jnp.int32)[:, None] == slot_index[None, :]
    wanted = jnp.sum(jnp.where(slot_match, local_ids[None, :], 0), axis=1)
    used = jnp.any(slot_match, axis=1)
    slot_side = jnp.where(used, jnp.sum(jnp.where(slot_match, positions[None, :], 0), axis=1), -1)
    slot_side = slot_side.astype(jnp.int32)
    wanted = jnp.where(used, wanted, -1).astype(jnp.int32)
    wants = jnp.concatenate(
        [lax.ppermute(wanted, "view", xor_pairs(count, j)) if j else wanted for j in range(lanes)]
    )
    ring = [0] + list(range(1, length, 2)) + list(range(2, length, 2))[::-1]
    nearest = [[ring[(ring.index(z) - i) % length] for i in range(length)] for z in range(length)]
    hop = [
        (ring[k] * lanes + y, ring[(k + 1) % length] * lanes + y)
        for k in range(length)
        for y in range(lanes)
    ]
    line = jnp.asarray(nearest, jnp.int32)[row // lanes]

    weights = load(w_embed, w_query, w_keyval)
    pieces, weights = lax.optimization_barrier((pieces, weights))
    w_embed, w_query, w_keyval = weights
    *embedded, whole = embed(parts, cuts, me, w_embed, pieces)
    embedded, wants = lax.optimization_barrier((embedded, wants))
    groups = ((0,), tuple(range(1, length - 1)), (length - 1,))

    def swap(picked):
        return [
            lax.ppermute(picked[j], "view", xor_pairs(count, j)) if j else picked[j]
            for j in range(lanes)
        ]

    shared = pick(lanes, groups[0], cap, me, line, wants, [whole])
    passed = [[part] for part in embedded]
    for p in range(1, length):
        for q in range(len(cuts)):
            passed[q].append(lax.ppermute(passed[q][-1], "view", hop))
        if p == 1:
            passed[0][1], shared = lax.optimization_barrier((passed[0][1], shared))
            shared = swap(shared)
        if p == 2:
            passed[0][2], shared = lax.optimization_barrier((passed[0][2], shared))
    fetched = []
    for q in range(len(cuts)):
        picked = []
        for group in groups[1:]:
            near = [passed[q][i] for i in group]
            picked.append(pick(lanes, group, cap, me, line, wants, near))
        fetched.append(list(shared))
        for group in picked:
            fetched[-1] += swap(group)
    slot_pair = slot_side // 2
    results = []
    (w_out,) = load(w_out)
    for c in range(pair_dev):
        mine = jnp.logical_and(slot_side >= 0, slot_pair % pair_dev == c)
        place = jnp.where(mine, 2 * (slot_pair // pair_dev) + slot_side % 2, -1).astype(jnp.int32)
        steps = [(cut,) for cut in cuts] if c == 0 else [cuts]
        parcels = []
        for q, step in enumerate(steps):
            wave = fetched[q : q + 1] if c == 0 else fetched
            sources = [each for group in wave for each in group]
            parcels += route(lanes, parts, cap, step, groups, me, line, place, sources)
        arrived = []
        for i, parcel in enumerate(parcels):
            arrived.append(
                lax.ppermute(parcel, "mp", xor_pairs(parts, i % parts)) if i % parts else parcel
            )
        results.append(
            decode(
                parts,
                cuts if c == 0 else ((0, rows),),
                me,
                gains,
                w_head,
                w_query,
                w_keyval,
                w_out,
                arrived,
            )
        )
    results = jnp.stack(results)

    every = lax.all_gather(results, "mp", axis=0, tiled=True).reshape(side_count, 4 * tokv)
    slotted = jnp.dot(slot_match.astype(jnp.float32), every, precision=lax.Precision.HIGHEST)
    tags = jnp.broadcast_to(wanted.astype(jnp.float32)[:, None], (slot_total, 128))
    slotted = jnp.concatenate([slotted, tags], axis=1).reshape(count, cap, 4 * tokv + 128)
    returned = lax.all_to_all(slotted, "view", split_axis=0, concat_axis=0, tiled=True)
    picker = returned[:, :, 4 * tokv :][:, :, :1] == jnp.arange(view_dev, dtype=jnp.float32)
    summed = jnp.einsum(
        "rcv,rcx->vx",
        picker.astype(jnp.float32),
        returned[:, :, : 4 * tokv],
        precision=lax.Precision.HIGHEST,
    )
    return summed.reshape(view_dev, 4, tokv)


def solution(mesh):
    return jax.shard_map(
        on_device,
        mesh=mesh,
        in_specs=(P("view", None, "mp"), P("view", None), P(), P(), P(), P(), P(), P()),
        out_specs=P("view", None, None),
        check_vma=False,
    )
```

```python
import functools

import jax
import jax.numpy as jnp
from jax import lax
from jax.experimental import pallas as pl
from jax.experimental.pallas import tpu as pltpu
from jax.sharding import PartitionSpec as P

HEADS = 12
EPS = 1e-06
LOG2_E = 1.4426950408889634
HBM = pl.BlockSpec(memory_space=pltpu.HBM)
SMEM = pl.BlockSpec(memory_space=pltpu.SMEM)
VMEM = pl.BlockSpec(memory_space=pltpu.VMEM)


def xor_pairs(count, step):
    return [(i, i ^ step) for i in range(count)]


def load_kernel(*refs):
    count = len(refs) // 2
    copies = [pltpu.make_async_copy(refs[i], refs[count + i], refs[-1].at[i]) for i in range(count)]
    for copy in copies:
        copy.start()
    for copy in copies:
        copy.wait()


def embed_kernel(parts, cuts, me_ref, w_vmem, *refs):
    pieces, outs, whole = refs[:parts], refs[parts : parts + len(cuts)], refs[parts + len(cuts)]
    x_ref, emb_ref, in_sem, out_sem = refs[parts + len(cuts) + 1 :]
    views, _, feat = pieces[0].shape
    width = w_vmem.shape[1]
    column = me_ref[1]
    copies = []
    for j in range(parts):
        start = pl.multiple_of((column ^ j) * feat, feat)
        copies.append(
            pltpu.make_async_copy(pieces[j], x_ref.at[:, :, pl.ds(start, feat)], in_sem.at[j])
        )
        copies[-1].start()
    for copy in copies:
        copy.wait()
    copies = []
    for q, (first, size) in enumerate(cuts):
        emb = jnp.dot(
            x_ref[:, first : first + size, :].reshape(views * size, parts * feat),
            w_vmem[...],
            preferred_element_type=jnp.float32,
        )
        emb_ref[:, first : first + size, :] = emb.astype(jnp.bfloat16).reshape(views, size, width)
        copies.append(
            pltpu.make_async_copy(
                emb_ref.at[:, pl.ds(first, size), :], outs[q], out_sem.at[q]
            )
        )
        copies[-1].start()
    copies.append(pltpu.make_async_copy(emb_ref, whole, out_sem.at[len(cuts)]))
    copies[-1].start()
    for copy in copies:
        copy.wait()


def pick_kernel(lanes, slots, cap, me_ref, line_ref, want_ref, *refs):
    count = len(slots)
    sources, outs = refs[:count], refs[count : count + lanes]
    stage_ref, in_sem, out_sem = refs[count + lanes :]
    lane = me_ref[0] % lanes
    rows = line_ref.shape[0] * lanes
    copies = [
        pltpu.make_async_copy(sources[n], stage_ref.at[n], in_sem.at[n]) for n in range(count)
    ]
    for copy in copies:
        copy.start()
    for copy in copies:
        copy.wait()
    copies = []
    for j in range(lanes):
        for n, i in enumerate(slots):
            for c in range(cap):
                view = want_ref[(j * rows + line_ref[i] * lanes + lane) * cap + c]
                copies.append(
                    pltpu.make_async_copy(
                        stage_ref.at[n, jnp.maximum(view, 0)], outs[j].at[n, c], out_sem.at[len(copies)]
                    )
                )
                copies[-1].start()
    for copy in copies:
        copy.wait()


def route_kernel(lanes, parts, cap, base, cuts, groups, me_ref, line_ref, side_ref, *refs):
    count = len(cuts) * len(groups) * lanes
    fetched, outs = refs[:count], refs[count : count + parts]
    stage_ref, in_sem, out_sem = refs[count + parts :]
    lane, column = me_ref[0] % lanes, me_ref[1]

    def slots(act):
        number = 0
        for q, (first, size) in enumerate(cuts):
            for g, group in enumerate(groups):
                for j in range(lanes):
                    source = fetched[(q * len(groups) + g) * lanes + j]
                    for n, i in enumerate(group):
                        for c in range(cap):
                            side = side_ref[(line_ref[i] * lanes + (lane ^ j)) * cap + c]
                            part = source.at[n, c]
                            if source.shape[2] > size:
                                part = source.at[n, c, pl.ds(base + first, size)]

                            @pl.when(side >= 0)
                            def _():
                                act(
                                    pltpu.make_async_copy(
                                        part,
                                        stage_ref.at[side, pl.ds(first, size), :],
                                        in_sem.at[number],
                                    )
                                )

                            number += 1

    slots(lambda copy: copy.start())
    slots(lambda copy: copy.wait())
    copies = []
    for j in range(parts):
        copies.append(
            pltpu.make_async_copy(
                stage_ref.at[pl.ds(2 * (column ^ j), 2)], outs[j], out_sem.at[j]
            )
        )
        copies[-1].start()
    for copy in copies:
        copy.wait()


def normed(values):
    mean = jnp.mean(values, axis=-1, keepdims=True)
    centred = values - mean
    var = jnp.mean(centred * centred, axis=-1, keepdims=True)
    return centred * lax.rsqrt(var + EPS)


def decode_kernel(parts, cuts, me_ref, gains_ref, whead_ref, wkv, wq, wo, *refs):
    pieces, out_ref = refs[: parts * len(cuts)], refs[parts * len(cuts)]
    scratch = refs[parts * len(cuts) + 1 :]
    emb_ref, qin_ref, min_ref, q_ref, kv_ref, ctx_ref, sem = scratch
    tokv, width = emb_ref.shape[1:]
    rows = tokv // parts
    column = me_ref[1]
    copies = []
    for q, (first, size) in enumerate(cuts):
        for j in range(parts):
            i = q * parts + j
            start = pl.multiple_of((column ^ j) * rows + first, size)
            copies.append(
                pltpu.make_async_copy(pieces[i], emb_ref.at[:, pl.ds(start, size), :], sem.at[i])
            )
            copies[-1].start()
    for copy in copies:
        copy.wait()

    def normalise(side):
        xhat = normed(emb_ref[side].astype(jnp.float32))
        qin_ref[side] = (xhat * gains_ref[side, 0:1, :]).astype(jnp.bfloat16)
        min_ref[1 - side] = (xhat * gains_ref[1 - side, 1:2, :]).astype(jnp.bfloat16)

    def project_query(side, start, size):
        q_ref[side, :, start : start + size] = jnp.dot(
            qin_ref[side], wq[side, :, start : start + size], preferred_element_type=jnp.float32
        ).astype(jnp.bfloat16)

    def project_keyval(side, start, size):
        kv_ref[side, :, start : start + size] = jnp.dot(
            min_ref[side], wkv[side, :, start : start + size], preferred_element_type=jnp.float32
        ).astype(jnp.bfloat16)

    head_size = width // HEADS
    lanes = 2 * head_size
    low = lax.broadcasted_iota(jnp.int32, (tokv, lanes), 1) < head_size

    def split(values):
        zero = jnp.zeros_like(values)
        return jnp.concatenate([jnp.where(low, values, zero), jnp.where(low, zero, values)], axis=0)

    def soft(scores):
        top = jnp.max(scores, axis=-1, keepdims=True)
        e = jnp.exp2((scores - top) * (LOG2_E / head_size**0.5))
        return (e * (1.0 / jnp.sum(e, axis=-1, keepdims=True))).astype(jnp.bfloat16)

    def two_heads_scores(side, i):
        start = i * lanes
        query = q_ref[side, :, start : start + lanes]
        keys = split(kv_ref[side, :, start : start + lanes])
        return lax.dot_general(
            query, keys, (((1,), (1,)), ((), ())), preferred_element_type=jnp.float32
        )

    def two_heads(side, i, scores):
        start = i * lanes
        values = split(kv_ref[side, :, width + start : width + start + lanes])
        probs = jnp.concatenate([soft(scores[:, :tokv]), soft(scores[:, tokv:])], axis=1)
        ctx_ref[side, :, start : start + lanes] = jnp.dot(
            probs, values, preferred_element_type=jnp.float32
        ).astype(jnp.bfloat16)

    def finish(side, product):
        updated = emb_ref[side].astype(jnp.float32) + product
        final = (normed(updated) * gains_ref[side, 2:3, :]).astype(jnp.bfloat16)
        head = lax.dot_general(
            whead_ref[side], final, (((1,), (1,)), ((), ())), preferred_element_type=jnp.float32
        )
        conf = 1.0 + jnp.exp(head[3:4, :])
        out_ref[side, 0:3, :] = head[0:3, :] * conf
        out_ref[side, 3:4, :] = conf

    def project_out(side):
        return jnp.dot(ctx_ref[side], wo[side], preferred_element_type=jnp.float32)

    steps = HEADS // 2
    block = 2 * width // steps
    normalise(1)
    project_keyval(0, 0, 2 * width)
    normalise(0)
    project_query(0, 0, width)
    scores = two_heads_scores(0, 0)
    for i in range(2 * steps):
        side, at = i // steps, i % steps
        now = scores
        if side == 0:
            project_keyval(1, at * block, block)
            if at % 2:
                project_query(1, at // 2 * block, block)
        if i + 1 < 2 * steps:
            scores = two_heads_scores((i + 1) // steps, (i + 1) % steps)
        two_heads(side, at, now)
        if i == steps:
            finish(0, project_out(0))
    finish(1, project_out(1))


def load(*weights):
    return pl.pallas_call(
        load_kernel,
        out_shape=[jax.ShapeDtypeStruct(w.shape, w.dtype) for w in weights],
        in_specs=[HBM] * len(weights),
        out_specs=[VMEM] * len(weights),
        scratch_shapes=[pltpu.SemaphoreType.DMA((len(weights),))],
        compiler_params=pltpu.CompilerParams(vmem_limit_bytes=50 * 1024 * 1024),
        name="load",
    )(*weights)


def embed(parts, cuts, me, w_embed, pieces):
    views, rows, _ = pieces[0].shape
    full, width = w_embed.shape
    return pl.pallas_call(
        functools.partial(embed_kernel, parts, cuts),
        out_shape=[
            jax.ShapeDtypeStruct((views, size, width), jnp.bfloat16)
            for size in [size for _, size in cuts] + [rows]
        ],
        in_specs=[SMEM, VMEM] + [HBM] * parts,
        out_specs=[HBM] * (len(cuts) + 1),
        scratch_shapes=[
            pltpu.VMEM((views, rows, full), jnp.bfloat16),
            pltpu.VMEM((views, rows, width), jnp.bfloat16),
            pltpu.SemaphoreType.DMA((parts,)),
            pltpu.SemaphoreType.DMA((len(cuts) + 1,)),
        ],
        compiler_params=pltpu.CompilerParams(vmem_limit_bytes=16 * 1024 * 1024),
        cost_estimate=pl.CostEstimate(
            flops=2 * views * rows * full * width,
            bytes_accessed=2 * (full * width + 2 * views * rows * full),
            transcendentals=0,
        ),
        name="embed",
    )(me, w_embed, *pieces)


def pick(lanes, slots, cap, me, line, wants, sources):
    views, size, width = sources[0].shape
    return pl.pallas_call(
        functools.partial(pick_kernel, lanes, slots, cap),
        out_shape=[jax.ShapeDtypeStruct((len(slots), cap, size, width), jnp.bfloat16)] * lanes,
        in_specs=[SMEM, SMEM, SMEM] + [HBM] * len(sources),
        out_specs=[HBM] * lanes,
        scratch_shapes=[
            pltpu.VMEM((len(slots), views, size, width), jnp.bfloat16),
            pltpu.SemaphoreType.DMA((len(slots),)),
            pltpu.SemaphoreType.DMA((lanes * len(slots) * cap,)),
        ],
        compiler_params=pltpu.CompilerParams(vmem_limit_bytes=16 * 1024 * 1024),
        cost_estimate=pl.CostEstimate(
            flops=0,
            bytes_accessed=4 * lanes * len(slots) * cap * size * width,
            transcendentals=0,
        ),
        name="pick",
    )(me, line, wants, *sources)


def route(lanes, parts, cap, cuts, groups, me, line, sides, fetched):
    width = fetched[0].shape[-1]
    size = sum(size for _, size in cuts)
    base = cuts[0][0]
    cuts = tuple((first - base, each) for first, each in cuts)
    copies = len(cuts) * sum(len(group) for group in groups) * lanes * cap
    return pl.pallas_call(
        functools.partial(route_kernel, lanes, parts, cap, base, cuts, groups),
        out_shape=[jax.ShapeDtypeStruct((2, size, width), jnp.bfloat16)] * parts,
        in_specs=[SMEM, SMEM, SMEM] + [HBM] * len(fetched),
        out_specs=[HBM] * parts,
        scratch_shapes=[
            pltpu.VMEM((2 * parts, size, width), jnp.bfloat16),
            pltpu.SemaphoreType.DMA((copies,)),
            pltpu.SemaphoreType.DMA((parts,)),
        ],
        compiler_params=pltpu.CompilerParams(vmem_limit_bytes=16 * 1024 * 1024),
        cost_estimate=pl.CostEstimate(
            flops=0, bytes_accessed=8 * parts * size * width, transcendentals=0
        ),
        name="route",
    )(me, line, sides, *fetched)


def decode(parts, cuts, me, gains, w_head, w_query, w_keyval, w_out, pieces):
    width = pieces[0].shape[2]
    tokv = parts * sum(size for _, size in cuts)
    flops = 2 * 2 * tokv * width * (5 * width + 2 * tokv)
    return pl.pallas_call(
        functools.partial(decode_kernel, parts, cuts),
        out_shape=jax.ShapeDtypeStruct((2, 4, tokv), jnp.float32),
        in_specs=[SMEM, VMEM, VMEM, VMEM, VMEM, VMEM] + [HBM] * (parts * len(cuts)),
        out_specs=VMEM,
        scratch_shapes=[
            pltpu.VMEM((2, tokv, width), jnp.bfloat16),
            pltpu.VMEM((2, tokv, width), jnp.bfloat16),
            pltpu.VMEM((2, tokv, width), jnp.bfloat16),
            pltpu.VMEM((2, tokv, width), jnp.bfloat16),
            pltpu.VMEM((2, tokv, 2 * width), jnp.bfloat16),
            pltpu.VMEM((2, tokv, width), jnp.bfloat16),
            pltpu.SemaphoreType.DMA((parts * len(cuts),)),
        ],
        compiler_params=pltpu.CompilerParams(vmem_limit_bytes=40 * 1024 * 1024),
        cost_estimate=pl.CostEstimate(
            flops=flops, bytes_accessed=20 * width * width, transcendentals=2 * HEADS * tokv * tokv
        ),
        name="decode",
    )(me, gains, w_head, w_keyval, w_query, w_out, *pieces)


def on_device(tokens, pairs, w_embed, w_query, w_keyval, w_out, w_head, gains):
    count = lax.axis_size("view")
    parts = lax.axis_size("mp")
    row = lax.axis_index("view")
    column = lax.axis_index("mp")
    me = jnp.stack([row, column]).astype(jnp.int32)
    view_dev, tokv, _ = tokens.shape
    rows = tokv // parts
    block_pairs = pairs.shape[0]
    pair_dev = block_pairs // parts
    side_count = 2 * block_pairs
    cap = max(2, (side_count + count - 1) // count)
    slot_total = count * cap
    lanes = 1 << ((count.bit_length() - 1) // 2)
    length = count // lanes
    cuts = ((0, rows // 2), (rows // 2, rows // 2)) if rows % 32 == 0 else ((0, rows),)

    pieces = []
    for j in range(parts):
        piece = lax.dynamic_slice_in_dim(tokens, (column ^ j) * rows, rows, axis=1)
        pieces.append(lax.ppermute(piece, "mp", xor_pairs(parts, j)) if j else piece)

    pairs, pieces[1] = lax.optimization_barrier((pairs, pieces[1]))
    side_views = pairs.reshape(side_count)
    owners = side_views // view_dev
    local_ids = side_views % view_dev
    positions = jnp.arange(side_count, dtype=jnp.int32)
    same_owner = owners[:, None] == owners[None, :]
    slot_rank = jnp.sum(
        jnp.logical_and(same_owner, positions[None, :] < positions[:, None]), axis=1
    )
    slot_index = owners * cap + slot_rank
    slot_match = jnp.arange(slot_total, dtype=jnp.int32)[:, None] == slot_index[None, :]
    wanted = jnp.sum(jnp.where(slot_match, local_ids[None, :], 0), axis=1)
    used = jnp.any(slot_match, axis=1)
    slot_side = jnp.where(used, jnp.sum(jnp.where(slot_match, positions[None, :], 0), axis=1), -1)
    slot_side = slot_side.astype(jnp.int32)
    wanted = jnp.where(used, wanted, -1).astype(jnp.int32)
    wants = jnp.concatenate(
        [lax.ppermute(wanted, "view", xor_pairs(count, j)) if j else wanted for j in range(lanes)]
    )
    ring = [0] + list(range(1, length, 2)) + list(range(2, length, 2))[::-1]
    nearest = [[ring[(ring.index(z) - i) % length] for i in range(length)] for z in range(length)]
    hop = [
        (ring[k] * lanes + y, ring[(k + 1) % length] * lanes + y)
        for k in range(length)
        for y in range(lanes)
    ]
    line = jnp.asarray(nearest, jnp.int32)[row // lanes]

    (w_embed,) = load(w_embed)
    pieces, w_embed, wants, line = lax.optimization_barrier((pieces, w_embed, wants, line))
    *embedded, whole = embed(parts, cuts, me, w_embed, pieces)
    groups = ((0,), tuple(range(1, length - 1)), (length - 1,))

    def swap(picked):
        return [
            lax.ppermute(picked[j], "view", xor_pairs(count, j)) if j else picked[j]
            for j in range(lanes)
        ]

    shared = pick(lanes, groups[0], cap, me, line, wants, [whole])
    passed = [[part] for part in embedded]
    for p in range(1, length):
        for q in range(len(cuts)):
            passed[q].append(lax.ppermute(passed[q][-1], "view", hop))
        if p == 1:
            passed[0][1], shared = lax.optimization_barrier((passed[0][1], shared))
            shared = swap(shared)
        if p == 2:
            passed[0][2], shared = lax.optimization_barrier((passed[0][2], shared))
    fetched = []
    for q in range(len(cuts)):
        picked = []
        for group in groups[1:]:
            near = [passed[q][i] for i in group]
            picked.append(pick(lanes, group, cap, me, line, wants, near))
        fetched.append(list(shared))
        for group in picked:
            fetched[-1] += swap(group)
    slot_pair = slot_side // 2
    results = []
    (w_out,) = load(w_out)
    for c in range(pair_dev):
        mine = jnp.logical_and(slot_side >= 0, slot_pair % pair_dev == c)
        place = jnp.where(mine, 2 * (slot_pair // pair_dev) + slot_side % 2, -1).astype(jnp.int32)
        steps = [(cut,) for cut in cuts] if c == 0 else [cuts]
        parcels = []
        for q, step in enumerate(steps):
            wave = fetched[q : q + 1] if c == 0 else fetched
            sources = [each for group in wave for each in group]
            parcels += route(lanes, parts, cap, step, groups, me, line, place, sources)
        arrived = []
        for i, parcel in enumerate(parcels):
            arrived.append(
                lax.ppermute(parcel, "mp", xor_pairs(parts, i % parts)) if i % parts else parcel
            )
        results.append(
            decode(
                parts,
                cuts if c == 0 else ((0, rows),),
                me,
                gains,
                w_head,
                w_query,
                w_keyval,
                w_out,
                arrived,
            )
        )
    results = jnp.stack(results)

    every = lax.all_gather(results, "mp", axis=0, tiled=True).reshape(side_count, 4 * tokv)
    slotted = jnp.dot(slot_match.astype(jnp.float32), every, precision=lax.Precision.HIGHEST)
    tags = jnp.broadcast_to(wanted.astype(jnp.float32)[:, None], (slot_total, 128))
    slotted = jnp.concatenate([slotted, tags], axis=1).reshape(count, cap, 4 * tokv + 128)
    returned = lax.all_to_all(slotted, "view", split_axis=0, concat_axis=0, tiled=True)
    picker = returned[:, :, 4 * tokv :][:, :, :1] == jnp.arange(view_dev, dtype=jnp.float32)
    summed = jnp.einsum(
        "rcv,rcx->vx",
        picker.astype(jnp.float32),
        returned[:, :, : 4 * tokv],
        precision=lax.Precision.HIGHEST,
    )
    return summed.reshape(view_dev, 4, tokv)


def solution(mesh):
    return jax.shard_map(
        on_device,
        mesh=mesh,
        in_specs=(P("view", None, "mp"), P("view", None), P(), P(), P(), P(), P(), P()),
        out_specs=P("view", None, None),
        check_vma=False,
    )
```

```python
import functools

import jax
import jax.numpy as jnp
from jax import lax
from jax.experimental import pallas as pl
from jax.experimental.pallas import tpu as pltpu
from jax.sharding import PartitionSpec as P

HEADS = 12
EPS = 1e-06
LOG2_E = 1.4426950408889634
HBM = pl.BlockSpec(memory_space=pltpu.HBM)
SMEM = pl.BlockSpec(memory_space=pltpu.SMEM)
VMEM = pl.BlockSpec(memory_space=pltpu.VMEM)


def xor_pairs(count, step):
    return [(i, i ^ step) for i in range(count)]


def load_kernel(*refs):
    count = len(refs) // 2
    copies = [pltpu.make_async_copy(refs[i], refs[count + i], refs[-1].at[i]) for i in range(count)]
    for copy in copies:
        copy.start()
    for copy in copies:
        copy.wait()


def embed_kernel(parts, cuts, keep, me_ref, w_vmem, *refs):
    pieces, outs = refs[:parts], refs[parts : parts + len(cuts) + keep]
    x_ref, emb_ref, in_sem, out_sem = refs[parts + len(cuts) + keep :]
    views, _, feat = pieces[0].shape
    width = w_vmem.shape[1]
    column = me_ref[1]
    copies = []
    for j in range(parts):
        start = pl.multiple_of((column ^ j) * feat, feat)
        copies.append(
            pltpu.make_async_copy(pieces[j], x_ref.at[:, :, pl.ds(start, feat)], in_sem.at[j])
        )
        copies[-1].start()
    for copy in copies:
        copy.wait()
    copies = []
    for q, (first, size) in enumerate(cuts):
        emb = jnp.dot(
            x_ref[:, first : first + size, :].reshape(views * size, parts * feat),
            w_vmem[...],
            preferred_element_type=jnp.float32,
        )
        emb_ref[:, first : first + size, :] = emb.astype(jnp.bfloat16).reshape(views, size, width)
        copies.append(
            pltpu.make_async_copy(
                emb_ref.at[:, pl.ds(first, size), :], outs[q], out_sem.at[q]
            )
        )
        copies[-1].start()
    if keep:
        copies.append(pltpu.make_async_copy(emb_ref, outs[-1], out_sem.at[len(cuts)]))
        copies[-1].start()
    for copy in copies:
        copy.wait()


def pick_kernel(lanes, slots, cap, me_ref, line_ref, want_ref, *refs):
    count = len(slots)
    sources, outs = refs[:count], refs[count : count + lanes]
    stage_ref, in_sem, out_sem = refs[count + lanes :]
    lane = me_ref[0] % lanes
    rows = line_ref.shape[0] * lanes
    copies = [
        pltpu.make_async_copy(sources[n], stage_ref.at[n], in_sem.at[n]) for n in range(count)
    ]
    for copy in copies:
        copy.start()
    for copy in copies:
        copy.wait()
    copies = []
    for j in range(lanes):
        for n, i in enumerate(slots):
            for c in range(cap):
                view = want_ref[(j * rows + line_ref[i] * lanes + lane) * cap + c]
                copies.append(
                    pltpu.make_async_copy(
                        stage_ref.at[n, jnp.maximum(view, 0)], outs[j].at[n, c], out_sem.at[len(copies)]
                    )
                )
                copies[-1].start()
    for copy in copies:
        copy.wait()


def route_kernel(lanes, parts, cap, base, cuts, groups, me_ref, line_ref, side_ref, *refs):
    count = len(cuts) * len(groups) * lanes
    fetched, outs = refs[:count], refs[count : count + parts]
    stage_ref, in_sem, out_sem = refs[count + parts :]
    lane, column = me_ref[0] % lanes, me_ref[1]

    def slots(act):
        number = 0
        for q, (first, size) in enumerate(cuts):
            for g, group in enumerate(groups):
                for j in range(lanes):
                    source = fetched[(q * len(groups) + g) * lanes + j]
                    for n, i in enumerate(group):
                        for c in range(cap):
                            side = side_ref[(line_ref[i] * lanes + (lane ^ j)) * cap + c]
                            part = source.at[n, c]
                            if source.shape[2] > size:
                                part = source.at[n, c, pl.ds(base + first, size)]

                            @pl.when(side >= 0)
                            def _():
                                act(
                                    pltpu.make_async_copy(
                                        part,
                                        stage_ref.at[side, pl.ds(first, size), :],
                                        in_sem.at[number],
                                    )
                                )

                            number += 1

    slots(lambda copy: copy.start())
    slots(lambda copy: copy.wait())
    copies = []
    for j in range(parts):
        copies.append(
            pltpu.make_async_copy(
                stage_ref.at[pl.ds(2 * (column ^ j), 2)], outs[j], out_sem.at[j]
            )
        )
        copies[-1].start()
    for copy in copies:
        copy.wait()


def normed(values):
    mean = jnp.mean(values, axis=-1, keepdims=True)
    centred = values - mean
    var = jnp.mean(centred * centred, axis=-1, keepdims=True)
    return centred * lax.rsqrt(var + EPS)


def decode_kernel(parts, cuts, me_ref, gains_ref, whead_ref, wkv, wq, wo, *refs):
    pieces, out_ref = refs[: parts * len(cuts)], refs[parts * len(cuts)]
    scratch = refs[parts * len(cuts) + 1 :]
    emb_ref, qin_ref, min_ref, q_ref, kv_ref, ctx_ref, sem = scratch
    tokv, width = emb_ref.shape[1:]
    rows = tokv // parts
    column = me_ref[1]
    copies = []
    for q, (first, size) in enumerate(cuts):
        for j in range(parts):
            i = q * parts + j
            start = pl.multiple_of((column ^ j) * rows + first, size)
            copies.append(
                pltpu.make_async_copy(pieces[i], emb_ref.at[:, pl.ds(start, size), :], sem.at[i])
            )
            copies[-1].start()
    for copy in copies:
        copy.wait()

    def normalise(side):
        xhat = normed(emb_ref[side].astype(jnp.float32))
        qin_ref[side] = (xhat * gains_ref[side, 0:1, :]).astype(jnp.bfloat16)
        min_ref[1 - side] = (xhat * gains_ref[1 - side, 1:2, :]).astype(jnp.bfloat16)

    def project_query(side, start, size):
        q_ref[side, :, start : start + size] = jnp.dot(
            qin_ref[side], wq[side, :, start : start + size], preferred_element_type=jnp.float32
        ).astype(jnp.bfloat16)

    def project_keyval(side, start, size):
        kv_ref[side, :, start : start + size] = jnp.dot(
            min_ref[side], wkv[side, :, start : start + size], preferred_element_type=jnp.float32
        ).astype(jnp.bfloat16)

    head_size = width // HEADS
    lanes = 2 * head_size
    low = lax.broadcasted_iota(jnp.int32, (tokv, lanes), 1) < head_size

    def split(values):
        zero = jnp.zeros_like(values)
        return jnp.concatenate([jnp.where(low, values, zero), jnp.where(low, zero, values)], axis=0)

    def soft(scores):
        top = jnp.max(scores, axis=-1, keepdims=True)
        e = jnp.exp2((scores - top) * (LOG2_E / head_size**0.5))
        return (e * (1.0 / jnp.sum(e, axis=-1, keepdims=True))).astype(jnp.bfloat16)

    def two_heads_scores(side, i):
        start = i * lanes
        query = q_ref[side, :, start : start + lanes]
        keys = split(kv_ref[side, :, start : start + lanes])
        return lax.dot_general(
            query, keys, (((1,), (1,)), ((), ())), preferred_element_type=jnp.float32
        )

    def two_heads(side, i, scores):
        start = i * lanes
        values = split(kv_ref[side, :, width + start : width + start + lanes])
        probs = jnp.concatenate([soft(scores[:, :tokv]), soft(scores[:, tokv:])], axis=1)
        ctx_ref[side, :, start : start + lanes] = jnp.dot(
            probs, values, preferred_element_type=jnp.float32
        ).astype(jnp.bfloat16)

    def finish(side, product):
        updated = emb_ref[side].astype(jnp.float32) + product
        final = (normed(updated) * gains_ref[side, 2:3, :]).astype(jnp.bfloat16)
        head = lax.dot_general(
            whead_ref[side], final, (((1,), (1,)), ((), ())), preferred_element_type=jnp.float32
        )
        conf = 1.0 + jnp.exp(head[3:4, :])
        out_ref[side, 0:3, :] = head[0:3, :] * conf
        out_ref[side, 3:4, :] = conf

    def project_out(side):
        return jnp.dot(ctx_ref[side], wo[side], preferred_element_type=jnp.float32)

    steps = HEADS // 2
    block = 2 * width // steps
    normalise(1)
    project_keyval(0, 0, 2 * width)
    normalise(0)
    project_query(0, 0, width)
    scores = two_heads_scores(0, 0)
    for i in range(2 * steps):
        side, at = i // steps, i % steps
        now = scores
        if side == 0:
            project_keyval(1, at * block, block)
            if at % 2:
                project_query(1, at // 2 * block, block)
        if i + 1 < 2 * steps:
            scores = two_heads_scores((i + 1) // steps, (i + 1) % steps)
        two_heads(side, at, now)
        if i == steps:
            finish(0, project_out(0))
    finish(1, project_out(1))


def load(*weights):
    return pl.pallas_call(
        load_kernel,
        out_shape=[jax.ShapeDtypeStruct(w.shape, w.dtype) for w in weights],
        in_specs=[HBM] * len(weights),
        out_specs=[VMEM] * len(weights),
        scratch_shapes=[pltpu.SemaphoreType.DMA((len(weights),))],
        compiler_params=pltpu.CompilerParams(vmem_limit_bytes=50 * 1024 * 1024),
        name="load",
    )(*weights)


def embed(parts, cuts, keep, me, w_embed, pieces):
    views, rows, _ = pieces[0].shape
    full, width = w_embed.shape
    return pl.pallas_call(
        functools.partial(embed_kernel, parts, cuts, keep),
        out_shape=[
            jax.ShapeDtypeStruct((views, size, width), jnp.bfloat16)
            for size in [size for _, size in cuts] + [rows] * keep
        ],
        in_specs=[SMEM, VMEM] + [HBM] * parts,
        out_specs=[HBM] * (len(cuts) + keep),
        scratch_shapes=[
            pltpu.VMEM((views, rows, full), jnp.bfloat16),
            pltpu.VMEM((views, rows, width), jnp.bfloat16),
            pltpu.SemaphoreType.DMA((parts,)),
            pltpu.SemaphoreType.DMA((len(cuts) + 1,)),
        ],
        compiler_params=pltpu.CompilerParams(vmem_limit_bytes=16 * 1024 * 1024),
        cost_estimate=pl.CostEstimate(
            flops=2 * views * rows * full * width,
            bytes_accessed=2 * (full * width + 2 * views * rows * full),
            transcendentals=0,
        ),
        name="embed",
    )(me, w_embed, *pieces)


def pick(lanes, slots, cap, me, line, wants, sources):
    views, size, width = sources[0].shape
    return pl.pallas_call(
        functools.partial(pick_kernel, lanes, slots, cap),
        out_shape=[jax.ShapeDtypeStruct((len(slots), cap, size, width), jnp.bfloat16)] * lanes,
        in_specs=[SMEM, SMEM, SMEM] + [HBM] * len(sources),
        out_specs=[HBM] * lanes,
        scratch_shapes=[
            pltpu.VMEM((len(slots), views, size, width), jnp.bfloat16),
            pltpu.SemaphoreType.DMA((len(slots),)),
            pltpu.SemaphoreType.DMA((lanes * len(slots) * cap,)),
        ],
        compiler_params=pltpu.CompilerParams(vmem_limit_bytes=16 * 1024 * 1024),
        cost_estimate=pl.CostEstimate(
            flops=0,
            bytes_accessed=4 * lanes * len(slots) * cap * size * width,
            transcendentals=0,
        ),
        name="pick",
    )(me, line, wants, *sources)


def route(lanes, parts, cap, cuts, groups, me, line, sides, fetched):
    width = fetched[0].shape[-1]
    size = sum(size for _, size in cuts)
    base = cuts[0][0]
    cuts = tuple((first - base, each) for first, each in cuts)
    copies = len(cuts) * sum(len(group) for group in groups) * lanes * cap
    return pl.pallas_call(
        functools.partial(route_kernel, lanes, parts, cap, base, cuts, groups),
        out_shape=[jax.ShapeDtypeStruct((2, size, width), jnp.bfloat16)] * parts,
        in_specs=[SMEM, SMEM, SMEM] + [HBM] * len(fetched),
        out_specs=[HBM] * parts,
        scratch_shapes=[
            pltpu.VMEM((2 * parts, size, width), jnp.bfloat16),
            pltpu.SemaphoreType.DMA((copies,)),
            pltpu.SemaphoreType.DMA((parts,)),
        ],
        compiler_params=pltpu.CompilerParams(vmem_limit_bytes=16 * 1024 * 1024),
        cost_estimate=pl.CostEstimate(
            flops=0, bytes_accessed=8 * parts * size * width, transcendentals=0
        ),
        name="route",
    )(me, line, sides, *fetched)


def decode(parts, cuts, me, gains, w_head, w_query, w_keyval, w_out, pieces):
    width = pieces[0].shape[2]
    tokv = parts * sum(size for _, size in cuts)
    flops = 2 * 2 * tokv * width * (5 * width + 2 * tokv)
    return pl.pallas_call(
        functools.partial(decode_kernel, parts, cuts),
        out_shape=jax.ShapeDtypeStruct((2, 4, tokv), jnp.float32),
        in_specs=[SMEM, VMEM, VMEM, VMEM, VMEM, VMEM] + [HBM] * (parts * len(cuts)),
        out_specs=VMEM,
        scratch_shapes=[
            pltpu.VMEM((2, tokv, width), jnp.bfloat16),
            pltpu.VMEM((2, tokv, width), jnp.bfloat16),
            pltpu.VMEM((2, tokv, width), jnp.bfloat16),
            pltpu.VMEM((2, tokv, width), jnp.bfloat16),
            pltpu.VMEM((2, tokv, 2 * width), jnp.bfloat16),
            pltpu.VMEM((2, tokv, width), jnp.bfloat16),
            pltpu.SemaphoreType.DMA((parts * len(cuts),)),
        ],
        compiler_params=pltpu.CompilerParams(vmem_limit_bytes=40 * 1024 * 1024),
        cost_estimate=pl.CostEstimate(
            flops=flops, bytes_accessed=20 * width * width, transcendentals=2 * HEADS * tokv * tokv
        ),
        name="decode",
    )(me, gains, w_head, w_keyval, w_query, w_out, *pieces)


def on_device(tokens, pairs, w_embed, w_query, w_keyval, w_out, w_head, gains):
    count = lax.axis_size("view")
    parts = lax.axis_size("mp")
    row = lax.axis_index("view")
    column = lax.axis_index("mp")
    me = jnp.stack([row, column]).astype(jnp.int32)
    view_dev, tokv, _ = tokens.shape
    rows = tokv // parts
    block_pairs = pairs.shape[0]
    pair_dev = block_pairs // parts
    side_count = 2 * block_pairs
    cap = max(2, (side_count + count - 1) // count)
    slot_total = count * cap
    lanes = 1 << ((count.bit_length() - 1) // 2)
    length = count // lanes
    cuts = ((0, rows // 2), (rows // 2, rows // 2)) if rows % 32 == 0 else ((0, rows),)

    pieces = []
    for j in range(parts):
        piece = lax.dynamic_slice_in_dim(tokens, (column ^ j) * rows, rows, axis=1)
        pieces.append(lax.ppermute(piece, "mp", xor_pairs(parts, j)) if j else piece)

    pairs, pieces[1] = lax.optimization_barrier((pairs, pieces[1]))
    side_views = pairs.reshape(side_count)
    owners = side_views // view_dev
    local_ids = side_views % view_dev
    positions = jnp.arange(side_count, dtype=jnp.int32)
    same_owner = owners[:, None] == owners[None, :]
    slot_rank = jnp.sum(
        jnp.logical_and(same_owner, positions[None, :] < positions[:, None]), axis=1
    )
    slot_index = owners * cap + slot_rank
    slot_match = jnp.arange(slot_total, dtype=jnp.int32)[:, None] == slot_index[None, :]
    wanted = jnp.sum(jnp.where(slot_match, local_ids[None, :], 0), axis=1)
    used = jnp.any(slot_match, axis=1)
    slot_side = jnp.where(used, jnp.sum(jnp.where(slot_match, positions[None, :], 0), axis=1), -1)
    slot_side = slot_side.astype(jnp.int32)
    wanted = jnp.where(used, wanted, -1).astype(jnp.int32)
    wants = jnp.concatenate(
        [lax.ppermute(wanted, "view", xor_pairs(count, j)) if j else wanted for j in range(lanes)]
    )
    ring = [0] + list(range(1, length, 2)) + list(range(2, length, 2))[::-1]
    nearest = [[ring[(ring.index(z) - i) % length] for i in range(length)] for z in range(length)]
    hop = [
        (ring[k] * lanes + y, ring[(k + 1) % length] * lanes + y)
        for k in range(length)
        for y in range(lanes)
    ]
    line = jnp.asarray(nearest, jnp.int32)[row // lanes]

    (w_embed,) = load(w_embed)
    pieces, w_embed, wants, line = lax.optimization_barrier((pieces, w_embed, wants, line))
    (first_cut,) = embed(parts, cuts[:1], 0, me, w_embed, pieces)
    *embedded, whole = embed(parts, cuts, 1, me, w_embed, pieces)
    embedded[0] = first_cut
    groups = ((0,), tuple(range(1, length - 1)), (length - 1,))

    def swap(picked):
        return [
            lax.ppermute(picked[j], "view", xor_pairs(count, j)) if j else picked[j]
            for j in range(lanes)
        ]

    shared = pick(lanes, groups[0], cap, me, line, wants, [whole])
    passed = [[part] for part in embedded]
    for p in range(1, length):
        for q in range(len(cuts)):
            passed[q].append(lax.ppermute(passed[q][-1], "view", hop))
        if p == 1:
            passed[0][1], shared = lax.optimization_barrier((passed[0][1], shared))
            shared = swap(shared)
        if p == 2:
            passed[0][2], shared = lax.optimization_barrier((passed[0][2], shared))
    fetched = []
    for q in range(len(cuts)):
        picked = []
        for group in groups[1:]:
            near = [passed[q][i] for i in group]
            picked.append(pick(lanes, group, cap, me, line, wants, near))
        fetched.append(list(shared))
        for group in picked:
            fetched[-1] += swap(group)
    slot_pair = slot_side // 2
    results = []
    (w_out,) = load(w_out)
    for c in range(pair_dev):
        mine = jnp.logical_and(slot_side >= 0, slot_pair % pair_dev == c)
        place = jnp.where(mine, 2 * (slot_pair // pair_dev) + slot_side % 2, -1).astype(jnp.int32)
        steps = [(cut,) for cut in cuts] if c == 0 else [cuts]
        parcels = []
        for q, step in enumerate(steps):
            wave = fetched[q : q + 1] if c == 0 else fetched
            sources = [each for group in wave for each in group]
            parcels += route(lanes, parts, cap, step, groups, me, line, place, sources)
        arrived = []
        for i, parcel in enumerate(parcels):
            arrived.append(
                lax.ppermute(parcel, "mp", xor_pairs(parts, i % parts)) if i % parts else parcel
            )
        results.append(
            decode(
                parts,
                cuts if c == 0 else ((0, rows),),
                me,
                gains,
                w_head,
                w_query,
                w_keyval,
                w_out,
                arrived,
            )
        )
    results = jnp.stack(results)

    every = lax.all_gather(results, "mp", axis=0, tiled=True).reshape(side_count, 4 * tokv)
    slotted = jnp.dot(slot_match.astype(jnp.float32), every, precision=lax.Precision.HIGHEST)
    tags = jnp.broadcast_to(wanted.astype(jnp.float32)[:, None], (slot_total, 128))
    slotted = jnp.concatenate([slotted, tags], axis=1).reshape(count, cap, 4 * tokv + 128)
    returned = lax.all_to_all(slotted, "view", split_axis=0, concat_axis=0, tiled=True)
    picker = returned[:, :, 4 * tokv :][:, :, :1] == jnp.arange(view_dev, dtype=jnp.float32)
    summed = jnp.einsum(
        "rcv,rcx->vx",
        picker.astype(jnp.float32),
        returned[:, :, : 4 * tokv],
        precision=lax.Precision.HIGHEST,
    )
    return summed.reshape(view_dev, 4, tokv)


def solution(mesh):
    return jax.shard_map(
        on_device,
        mesh=mesh,
        in_specs=(P("view", None, "mp"), P("view", None), P(), P(), P(), P(), P(), P()),
        out_specs=P("view", None, None),
        check_vma=False,
    )
```

```python
import functools

import jax
import jax.numpy as jnp
from jax import lax
from jax.experimental import pallas as pl
from jax.experimental.pallas import tpu as pltpu
from jax.sharding import PartitionSpec as P

HEADS = 12
EPS = 1e-06
LOG2_E = 1.4426950408889634
HBM = pl.BlockSpec(memory_space=pltpu.HBM)
SMEM = pl.BlockSpec(memory_space=pltpu.SMEM)
VMEM = pl.BlockSpec(memory_space=pltpu.VMEM)


def xor_pairs(count, step):
    return [(i, i ^ step) for i in range(count)]


def load_kernel(*refs):
    count = len(refs) // 2
    copies = [pltpu.make_async_copy(refs[i], refs[count + i], refs[-1].at[i]) for i in range(count)]
    for copy in copies:
        copy.start()
    for copy in copies:
        copy.wait()


def embed_kernel(parts, cuts, keep, me_ref, w_vmem, *refs):
    pieces, outs = refs[:parts], refs[parts : parts + len(cuts) + keep]
    x_ref, emb_ref, in_sem, out_sem = refs[parts + len(cuts) + keep :]
    views, _, feat = pieces[0].shape
    width = w_vmem.shape[1]
    column = me_ref[1]
    copies = []
    for j in range(parts):
        start = pl.multiple_of((column ^ j) * feat, feat)
        copies.append(
            pltpu.make_async_copy(pieces[j], x_ref.at[:, :, pl.ds(start, feat)], in_sem.at[j])
        )
        copies[-1].start()
    for copy in copies:
        copy.wait()
    copies = []
    for q, (first, size) in enumerate(cuts):
        emb = jnp.dot(
            x_ref[:, first : first + size, :].reshape(views * size, parts * feat),
            w_vmem[...],
            preferred_element_type=jnp.float32,
        )
        emb_ref[:, first : first + size, :] = emb.astype(jnp.bfloat16).reshape(views, size, width)
        copies.append(
            pltpu.make_async_copy(
                emb_ref.at[:, pl.ds(first, size), :], outs[q], out_sem.at[q]
            )
        )
        copies[-1].start()
    if keep:
        copies.append(pltpu.make_async_copy(emb_ref, outs[-1], out_sem.at[len(cuts)]))
        copies[-1].start()
    for copy in copies:
        copy.wait()


def pick_kernel(lanes, slots, cap, me_ref, line_ref, want_ref, *refs):
    count = len(slots)
    sources, outs = refs[:count], refs[count : count + lanes]
    out_sem = refs[count + lanes]
    lane = me_ref[0] % lanes
    rows = line_ref.shape[0] * lanes
    copies = []
    for j in range(lanes):
        for n, i in enumerate(slots):
            for c in range(cap):
                view = want_ref[(j * rows + line_ref[i] * lanes + lane) * cap + c]
                copies.append(
                    pltpu.make_async_copy(
                        sources[n].at[jnp.maximum(view, 0)], outs[j].at[n, c], out_sem.at[len(copies)]
                    )
                )
                copies[-1].start()
    for copy in copies:
        copy.wait()


def route_kernel(lanes, parts, cap, base, cuts, groups, me_ref, line_ref, side_ref, *refs):
    count = len(cuts) * len(groups) * lanes
    fetched, outs = refs[:count], refs[count : count + parts]
    stage_ref, in_sem, out_sem = refs[count + parts :]
    lane, column = me_ref[0] % lanes, me_ref[1]

    def slots(act):
        number = 0
        for q, (first, size) in enumerate(cuts):
            for g, group in enumerate(groups):
                for j in range(lanes):
                    source = fetched[(q * len(groups) + g) * lanes + j]
                    for n, i in enumerate(group):
                        for c in range(cap):
                            side = side_ref[(line_ref[i] * lanes + (lane ^ j)) * cap + c]
                            part = source.at[n, c]
                            if source.shape[2] > size:
                                part = source.at[n, c, pl.ds(base + first, size)]

                            @pl.when(side >= 0)
                            def _():
                                act(
                                    pltpu.make_async_copy(
                                        part,
                                        stage_ref.at[side, pl.ds(first, size), :],
                                        in_sem.at[number],
                                    )
                                )

                            number += 1

    slots(lambda copy: copy.start())
    slots(lambda copy: copy.wait())
    copies = []
    for j in range(parts):
        copies.append(
            pltpu.make_async_copy(
                stage_ref.at[pl.ds(2 * (column ^ j), 2)], outs[j], out_sem.at[j]
            )
        )
        copies[-1].start()
    for copy in copies:
        copy.wait()


def normed(values):
    mean = jnp.mean(values, axis=-1, keepdims=True)
    centred = values - mean
    var = jnp.mean(centred * centred, axis=-1, keepdims=True)
    return centred * lax.rsqrt(var + EPS)


def decode_kernel(parts, cuts, me_ref, gains_ref, whead_ref, wkv, wq, wo, *refs):
    pieces, out_ref = refs[: parts * len(cuts)], refs[parts * len(cuts)]
    scratch = refs[parts * len(cuts) + 1 :]
    emb_ref, qin_ref, min_ref, q_ref, kv_ref, ctx_ref, sem = scratch
    tokv, width = emb_ref.shape[1:]
    rows = tokv // parts
    column = me_ref[1]
    copies = []
    for q, (first, size) in enumerate(cuts):
        for j in range(parts):
            i = q * parts + j
            start = pl.multiple_of((column ^ j) * rows + first, size)
            copies.append(
                pltpu.make_async_copy(pieces[i], emb_ref.at[:, pl.ds(start, size), :], sem.at[i])
            )
            copies[-1].start()
    for copy in copies:
        copy.wait()

    def normalise(side):
        xhat = normed(emb_ref[side].astype(jnp.float32))
        qin_ref[side] = (xhat * gains_ref[side, 0:1, :]).astype(jnp.bfloat16)
        min_ref[1 - side] = (xhat * gains_ref[1 - side, 1:2, :]).astype(jnp.bfloat16)

    def project_query(side, start, size):
        q_ref[side, :, start : start + size] = jnp.dot(
            qin_ref[side], wq[side, :, start : start + size], preferred_element_type=jnp.float32
        ).astype(jnp.bfloat16)

    def project_keyval(side, start, size):
        kv_ref[side, :, start : start + size] = jnp.dot(
            min_ref[side], wkv[side, :, start : start + size], preferred_element_type=jnp.float32
        ).astype(jnp.bfloat16)

    head_size = width // HEADS
    lanes = 2 * head_size
    low = lax.broadcasted_iota(jnp.int32, (tokv, lanes), 1) < head_size

    def split(values):
        zero = jnp.zeros_like(values)
        return jnp.concatenate([jnp.where(low, values, zero), jnp.where(low, zero, values)], axis=0)

    def soft(scores):
        top = jnp.max(scores, axis=-1, keepdims=True)
        e = jnp.exp2((scores - top) * (LOG2_E / head_size**0.5))
        return (e * (1.0 / jnp.sum(e, axis=-1, keepdims=True))).astype(jnp.bfloat16)

    def two_heads_scores(side, i):
        start = i * lanes
        query = q_ref[side, :, start : start + lanes]
        keys = split(kv_ref[side, :, start : start + lanes])
        return lax.dot_general(
            query, keys, (((1,), (1,)), ((), ())), preferred_element_type=jnp.float32
        )

    def two_heads(side, i, scores):
        start = i * lanes
        values = split(kv_ref[side, :, width + start : width + start + lanes])
        probs = jnp.concatenate([soft(scores[:, :tokv]), soft(scores[:, tokv:])], axis=1)
        ctx_ref[side, :, start : start + lanes] = jnp.dot(
            probs, values, preferred_element_type=jnp.float32
        ).astype(jnp.bfloat16)

    def finish(side, product):
        updated = emb_ref[side].astype(jnp.float32) + product
        final = (normed(updated) * gains_ref[side, 2:3, :]).astype(jnp.bfloat16)
        head = lax.dot_general(
            whead_ref[side], final, (((1,), (1,)), ((), ())), preferred_element_type=jnp.float32
        )
        conf = 1.0 + jnp.exp(head[3:4, :])
        out_ref[side, 0:3, :] = head[0:3, :] * conf
        out_ref[side, 3:4, :] = conf

    def project_out(side):
        return jnp.dot(ctx_ref[side], wo[side], preferred_element_type=jnp.float32)

    steps = HEADS // 2
    block = 2 * width // steps
    normalise(1)
    project_keyval(0, 0, 2 * width)
    normalise(0)
    project_query(0, 0, width)
    scores = two_heads_scores(0, 0)
    for i in range(2 * steps):
        side, at = i // steps, i % steps
        now = scores
        if side == 0:
            project_keyval(1, at * block, block)
            if at % 2:
                project_query(1, at // 2 * block, block)
        if i + 1 < 2 * steps:
            scores = two_heads_scores((i + 1) // steps, (i + 1) % steps)
        two_heads(side, at, now)
        if i == steps:
            finish(0, project_out(0))
    finish(1, project_out(1))


def load(*weights):
    return pl.pallas_call(
        load_kernel,
        out_shape=[jax.ShapeDtypeStruct(w.shape, w.dtype) for w in weights],
        in_specs=[HBM] * len(weights),
        out_specs=[VMEM] * len(weights),
        scratch_shapes=[pltpu.SemaphoreType.DMA((len(weights),))],
        compiler_params=pltpu.CompilerParams(vmem_limit_bytes=50 * 1024 * 1024),
        name="load",
    )(*weights)


def embed(parts, cuts, keep, me, w_embed, pieces):
    views, rows, _ = pieces[0].shape
    full, width = w_embed.shape
    return pl.pallas_call(
        functools.partial(embed_kernel, parts, cuts, keep),
        out_shape=[
            jax.ShapeDtypeStruct((views, size, width), jnp.bfloat16)
            for size in [size for _, size in cuts] + [rows] * keep
        ],
        in_specs=[SMEM, VMEM] + [HBM] * parts,
        out_specs=[HBM] * (len(cuts) + keep),
        scratch_shapes=[
            pltpu.VMEM((views, rows, full), jnp.bfloat16),
            pltpu.VMEM((views, rows, width), jnp.bfloat16),
            pltpu.SemaphoreType.DMA((parts,)),
            pltpu.SemaphoreType.DMA((len(cuts) + 1,)),
        ],
        compiler_params=pltpu.CompilerParams(vmem_limit_bytes=16 * 1024 * 1024),
        cost_estimate=pl.CostEstimate(
            flops=2 * views * rows * full * width,
            bytes_accessed=2 * (full * width + 2 * views * rows * full),
            transcendentals=0,
        ),
        name="embed",
    )(me, w_embed, *pieces)


def pick(lanes, slots, cap, me, line, wants, sources):
    _, size, width = sources[0].shape
    return pl.pallas_call(
        functools.partial(pick_kernel, lanes, slots, cap),
        out_shape=[jax.ShapeDtypeStruct((len(slots), cap, size, width), jnp.bfloat16)] * lanes,
        in_specs=[SMEM, SMEM, SMEM] + [HBM] * len(sources),
        out_specs=[HBM] * lanes,
        scratch_shapes=[
            pltpu.SemaphoreType.DMA((lanes * len(slots) * cap,)),
        ],
        compiler_params=pltpu.CompilerParams(vmem_limit_bytes=16 * 1024 * 1024),
        cost_estimate=pl.CostEstimate(
            flops=0,
            bytes_accessed=4 * lanes * len(slots) * cap * size * width,
            transcendentals=0,
        ),
        name="pick",
    )(me, line, wants, *sources)


def route(lanes, parts, cap, cuts, groups, me, line, sides, fetched):
    width = fetched[0].shape[-1]
    size = sum(size for _, size in cuts)
    base = cuts[0][0]
    cuts = tuple((first - base, each) for first, each in cuts)
    copies = len(cuts) * sum(len(group) for group in groups) * lanes * cap
    return pl.pallas_call(
        functools.partial(route_kernel, lanes, parts, cap, base, cuts, groups),
        out_shape=[jax.ShapeDtypeStruct((2, size, width), jnp.bfloat16)] * parts,
        in_specs=[SMEM, SMEM, SMEM] + [HBM] * len(fetched),
        out_specs=[HBM] * parts,
        scratch_shapes=[
            pltpu.VMEM((2 * parts, size, width), jnp.bfloat16),
            pltpu.SemaphoreType.DMA((copies,)),
            pltpu.SemaphoreType.DMA((parts,)),
        ],
        compiler_params=pltpu.CompilerParams(vmem_limit_bytes=16 * 1024 * 1024),
        cost_estimate=pl.CostEstimate(
            flops=0, bytes_accessed=8 * parts * size * width, transcendentals=0
        ),
        name="route",
    )(me, line, sides, *fetched)


def decode(parts, cuts, me, gains, w_head, w_query, w_keyval, w_out, pieces):
    width = pieces[0].shape[2]
    tokv = parts * sum(size for _, size in cuts)
    flops = 2 * 2 * tokv * width * (5 * width + 2 * tokv)
    return pl.pallas_call(
        functools.partial(decode_kernel, parts, cuts),
        out_shape=jax.ShapeDtypeStruct((2, 4, tokv), jnp.float32),
        in_specs=[SMEM, VMEM, VMEM, VMEM, VMEM, VMEM] + [HBM] * (parts * len(cuts)),
        out_specs=VMEM,
        scratch_shapes=[
            pltpu.VMEM((2, tokv, width), jnp.bfloat16),
            pltpu.VMEM((2, tokv, width), jnp.bfloat16),
            pltpu.VMEM((2, tokv, width), jnp.bfloat16),
            pltpu.VMEM((2, tokv, width), jnp.bfloat16),
            pltpu.VMEM((2, tokv, 2 * width), jnp.bfloat16),
            pltpu.VMEM((2, tokv, width), jnp.bfloat16),
            pltpu.SemaphoreType.DMA((parts * len(cuts),)),
        ],
        compiler_params=pltpu.CompilerParams(vmem_limit_bytes=40 * 1024 * 1024),
        cost_estimate=pl.CostEstimate(
            flops=flops, bytes_accessed=20 * width * width, transcendentals=2 * HEADS * tokv * tokv
        ),
        name="decode",
    )(me, gains, w_head, w_keyval, w_query, w_out, *pieces)


def on_device(tokens, pairs, w_embed, w_query, w_keyval, w_out, w_head, gains):
    count = lax.axis_size("view")
    parts = lax.axis_size("mp")
    row = lax.axis_index("view")
    column = lax.axis_index("mp")
    me = jnp.stack([row, column]).astype(jnp.int32)
    view_dev, tokv, _ = tokens.shape
    rows = tokv // parts
    block_pairs = pairs.shape[0]
    pair_dev = block_pairs // parts
    side_count = 2 * block_pairs
    cap = max(2, (side_count + count - 1) // count)
    slot_total = count * cap
    lanes = 1 << ((count.bit_length() - 1) // 2)
    length = count // lanes
    cuts = ((0, rows // 2), (rows // 2, rows // 2)) if rows % 32 == 0 else ((0, rows),)

    pieces = []
    for j in range(parts):
        piece = lax.dynamic_slice_in_dim(tokens, (column ^ j) * rows, rows, axis=1)
        pieces.append(lax.ppermute(piece, "mp", xor_pairs(parts, j)) if j else piece)

    pairs, pieces[1] = lax.optimization_barrier((pairs, pieces[1]))
    side_views = pairs.reshape(side_count)
    owners = side_views // view_dev
    local_ids = side_views % view_dev
    positions = jnp.arange(side_count, dtype=jnp.int32)
    same_owner = owners[:, None] == owners[None, :]
    slot_rank = jnp.sum(
        jnp.logical_and(same_owner, positions[None, :] < positions[:, None]), axis=1
    )
    slot_index = owners * cap + slot_rank
    slot_match = jnp.arange(slot_total, dtype=jnp.int32)[:, None] == slot_index[None, :]
    wanted = jnp.sum(jnp.where(slot_match, local_ids[None, :], 0), axis=1)
    used = jnp.any(slot_match, axis=1)
    slot_side = jnp.where(used, jnp.sum(jnp.where(slot_match, positions[None, :], 0), axis=1), -1)
    slot_side = slot_side.astype(jnp.int32)
    wanted = jnp.where(used, wanted, -1).astype(jnp.int32)
    wants = jnp.concatenate(
        [lax.ppermute(wanted, "view", xor_pairs(count, j)) if j else wanted for j in range(lanes)]
    )
    ring = [0] + list(range(1, length, 2)) + list(range(2, length, 2))[::-1]
    nearest = [[ring[(ring.index(z) - i) % length] for i in range(length)] for z in range(length)]
    hop = [
        (ring[k] * lanes + y, ring[(k + 1) % length] * lanes + y)
        for k in range(length)
        for y in range(lanes)
    ]
    line = jnp.asarray(nearest, jnp.int32)[row // lanes]

    (w_embed,) = load(w_embed)
    pieces, w_embed, wants, line = lax.optimization_barrier((pieces, w_embed, wants, line))
    (first_cut,) = embed(parts, cuts[:1], 0, me, w_embed, pieces)
    *embedded, whole = embed(parts, cuts, 1, me, w_embed, pieces)
    embedded[0] = first_cut
    groups = ((0,), tuple(range(1, length - 1)), (length - 1,))

    def swap(picked):
        return [
            lax.ppermute(picked[j], "view", xor_pairs(count, j)) if j else picked[j]
            for j in range(lanes)
        ]

    shared = pick(lanes, groups[0], cap, me, line, wants, [whole])
    passed = [[part] for part in embedded]
    for p in range(1, length):
        for q in range(len(cuts)):
            passed[q].append(lax.ppermute(passed[q][-1], "view", hop))
        if p == 1:
            passed[0][1], shared = lax.optimization_barrier((passed[0][1], shared))
            shared = swap(shared)
        if p == 2:
            passed[0][2], shared = lax.optimization_barrier((passed[0][2], shared))
    fetched = []
    for q in range(len(cuts)):
        picked = []
        for group in groups[1:]:
            near = [passed[q][i] for i in group]
            picked.append(pick(lanes, group, cap, me, line, wants, near))
        fetched.append(list(shared))
        for group in picked:
            fetched[-1] += swap(group)
    slot_pair = slot_side // 2
    results = []
    (w_out,) = load(w_out)
    for c in range(pair_dev):
        mine = jnp.logical_and(slot_side >= 0, slot_pair % pair_dev == c)
        place = jnp.where(mine, 2 * (slot_pair // pair_dev) + slot_side % 2, -1).astype(jnp.int32)
        steps = [(cut,) for cut in cuts] if c == 0 else [cuts]
        parcels = []
        for q, step in enumerate(steps):
            wave = fetched[q : q + 1] if c == 0 else fetched
            sources = [each for group in wave for each in group]
            parcels += route(lanes, parts, cap, step, groups, me, line, place, sources)
        arrived = []
        for i, parcel in enumerate(parcels):
            arrived.append(
                lax.ppermute(parcel, "mp", xor_pairs(parts, i % parts)) if i % parts else parcel
            )
        results.append(
            decode(
                parts,
                cuts if c == 0 else ((0, rows),),
                me,
                gains,
                w_head,
                w_query,
                w_keyval,
                w_out,
                arrived,
            )
        )
    results = jnp.stack(results)

    every = lax.all_gather(results, "mp", axis=0, tiled=True).reshape(side_count, 4 * tokv)
    slotted = jnp.dot(slot_match.astype(jnp.float32), every, precision=lax.Precision.HIGHEST)
    tags = jnp.broadcast_to(wanted.astype(jnp.float32)[:, None], (slot_total, 128))
    slotted = jnp.concatenate([slotted, tags], axis=1).reshape(count, cap, 4 * tokv + 128)
    returned = lax.all_to_all(slotted, "view", split_axis=0, concat_axis=0, tiled=True)
    picker = returned[:, :, 4 * tokv :][:, :, :1] == jnp.arange(view_dev, dtype=jnp.float32)
    summed = jnp.einsum(
        "rcv,rcx->vx",
        picker.astype(jnp.float32),
        returned[:, :, : 4 * tokv],
        precision=lax.Precision.HIGHEST,
    )
    return summed.reshape(view_dev, 4, tokv)


def solution(mesh):
    return jax.shard_map(
        on_device,
        mesh=mesh,
        in_specs=(P("view", None, "mp"), P("view", None), P(), P(), P(), P(), P(), P()),
        out_specs=P("view", None, None),
        check_vma=False,
    )
```
